32 devices in a mesh: fsdp: 4 (over y, x), context: 2 (over core), tensor: 4 (over z).
Axes of the slice: x: 2, y: 2, z: 4, core: 2. Of those that a mesh axis runs over, the one named last changes fastest.
Arguments:
- x_in: bfloat16 [4, 2048, 2048], P('fsdp', 'context'), may hold values from -6 to 6
- teacher: bfloat16 [4, 2048, 2048], P('fsdp', 'context'), may hold values from -9 to 9
- segments: int32 [4, 2048], P('fsdp', 'context'), may hold values from 0 to 11, never falling along the last dimension, each value on 1 to 1024 neighbouring positions
- valid: int32 [4, 2048], P('fsdp', 'context'), may hold values from 0 to 1, as said below
- norm_gain: bfloat16 [2048], P('fsdp'), may hold values from 0.5 to 1.5
- w_in: bfloat16 [2048, 2, 4096], P('fsdp', None, 'tensor'), may hold values from -0.125 to 0.125
- conv_w: bfloat16 [4, 4096], P(None, ('tensor', 'fsdp')), may hold values from -3 to 3
- conv_b: bfloat16 [4096], P(('tensor', 'fsdp')), may hold values from -0.5 to 0.5
- x_proj: bfloat16 [160, 4096], P(None, ('tensor', 'fsdp')), may hold values from -0.09375 to 0.09375
- dt_w: bfloat16 [128, 4096], P(None, ('tensor', 'fsdp')), may hold values from -0.5 to 0.5
- dt_bias: bfloat16 [4096], P(('tensor', 'fsdp')), may hold values from -6.5 to -2.5
- a_log: bfloat16 [16, 4096], P(None, ('tensor', 'fsdp')), may hold values from 0 to 2.75
- d_skip: bfloat16 [4096], P(('tensor', 'fsdp')), may hold values from 0.5 to 1.5
- w_out: bfloat16 [4096, 2048], P('tensor', 'fsdp'), may hold values from -0.375 to 0.375
Outputs:
- mixed_out: float32 [4, 2048, 2048], P('fsdp', 'context', 'tensor')
- loss_value: float32 [], replicated
- grad_input: float32 [4, 2048, 2048], P('fsdp', 'context', 'tensor')
- grad_norm_gain: float32 [2048], P('fsdp')
- grad_w_in: float32 [2048, 2, 4096], P('fsdp', None, 'tensor')
- grad_conv_w: float32 [4, 4096], P(None, ('tensor', 'fsdp'))
- grad_conv_b: float32 [4096], P(('tensor', 'fsdp'))
- grad_x_proj: float32 [160, 4096], P(None, ('tensor', 'fsdp'))
- grad_dt_w: float32 [128, 4096], P(None, ('tensor', 'fsdp'))
- grad_dt_bias: float32 [4096], P(('tensor', 'fsdp'))
- grad_a_log: float32 [16, 4096], P(None, ('tensor', 'fsdp'))
- grad_d_skip: float32 [4096], P(('tensor', 'fsdp'))
- grad_w_out: float32 [4096, 2048], P('tensor', 'fsdp')
The draws below stay inside these ranges and needn't reach their ends.
Inputs may be any that keep to these rules, and one draw needn't show every extreme that they name: The last token of every sequence has valid = 1.
All inputs are finite; a program needn't handle non-finite values.
Results may differ from the reference program's by a relative error of at most 0.0074.
Values may be sent and summed in bfloat16 or wider, within the bound.
No kernel may reach another device: no remote copies, remote signals or barrier semaphores. Data moves between devices by JAX's collectives and lax.ppermute only.
A program may use at most 448 MiB of HBM per device.

```python
import math
import jax
import jax.numpy as jnp
import numpy as np
from jax import lax

D = 2048
DI = 4096
NST = 16
RANK = 128
KCONV = 4
LENGTH = 2048
STRIP = 8
DOCS = 12
LONGDOC = 1024
SEQS = 4
TOKENS = 8192


def draw_valid(key, part):
    positions = jnp.arange(LENGTH, dtype=jnp.int32)[None, :]
    row_index = jnp.arange(SEQS, dtype=jnp.int32)[:, None]
    limit = 250 + 600 * positions // LENGTH + 100 * row_index // SEQS
    rolled = jax.random.randint(key, (SEQS, LENGTH), 0, 1000, dtype=jnp.int32)
    chosen = (rolled < limit) | (positions == LENGTH - 1)
    return jnp.where(chosen, 1, 0).astype(jnp.int32)


def with_spikes(array, stream_key, source, target, parts, factor):
    def block_of(axis_at):
        return (jnp.arange(array.shape[axis_at]) // (array.shape[axis_at] // parts)).reshape((-1,) + (1,) * (array.ndim - 1 - axis_at))

    first = jax.random.permutation(stream_key, parts)[block_of(target)]
    far = (block_of(target) + parts // 2) % parts
    return jnp.where((block_of(source) == first) | (block_of(source) == far), factor * array, array)


def steps_of(own_key, extent, cuts, low, top_value):
    factor_of, own = 1.0, jax.random.fold_in(own_key, 6)
    for position, blocks in cuts:
        heights = jnp.exp(jax.random.uniform(jax.random.fold_in(own, position), (blocks,), jnp.float32, low / len(cuts), top_value / len(cuts)))
        factor_of = factor_of * jnp.repeat(heights, extent[position] // blocks).reshape([-1 if axis == position else 1 for axis in range(len(extent))])
    return factor_of


def split_up(number_of, total, reach, lean):
    weights = [(1 << 20) // math.isqrt(standing ** lean) + 1 for standing in range(2, number_of + 1)]
    rest, counts = total - reach - (number_of - 1), [1] * (number_of - 1)
    while rest > 0:
        free = [i for i in range(number_of - 1) if counts[i] < reach]
        pool, left = sum([weights[i] for i in free]), rest
        for i in free:
            addition = min(reach - counts[i], max(1, left * weights[i] // pool), rest)
            counts[i] = counts[i] + addition
            rest = rest - addition
    return np.array([reach] + counts)


def ragged_sizes(rng, amount, total, most, slope):
    if amount == 2:
        one = jax.random.randint(rng, (), max(1, total - most), min(most, total - 1) + 1)
        return jnp.stack([one, total - one])
    sizes = jnp.asarray(split_up(amount, total, most, slope), jnp.int32)
    twos = (amount - 1) // 2
    donor, sink = sizes[1:1 + 2 * twos:2], sizes[2:2 + 2 * twos:2]
    slack = jnp.minimum(donor - 1, most - sink)
    passed = jax.random.randint(jax.random.fold_in(rng, 1), (twos,), 0, 1 << 20) % (slack + 1)
    sizes = sizes.at[1:1 + 2 * twos:2].set(donor - passed).at[2:2 + 2 * twos:2].set(sink + passed)
    return sizes[jax.random.permutation(jax.random.fold_in(rng, 2), amount)]


def centred(key, dims, spread, most, cuts=(), kind=jnp.bfloat16):
    drawn = spread * jax.random.normal(key, dims, jnp.float32)
    if cuts:
        drawn = drawn * steps_of(key, dims, cuts, -0.22, 0.18)
    return jnp.clip(drawn, -most, most).astype(kind)


def bell_draw_with(stream_key, extent, deviation, most, shards, heavy, kind=jnp.bfloat16):
    drawn = deviation * jax.random.normal(stream_key, extent, jnp.float32)
    if shards:
        drawn = drawn * steps_of(stream_key, extent, shards, -0.22, 0.18)
    return jnp.clip(with_spikes(drawn, jax.random.fold_in(stream_key, 3), *heavy), -most, most).astype(kind)


def setup_inputs(seed: int = 0) -> dict:
    seeds = jax.random.split(jax.random.key(seed), 15)
    return {
        "x_in": centred(seeds[0], (SEQS, LENGTH, D), 1.0, 6.0, ((0, 4), (1, 2))),
        "teacher": bell_draw_with(seeds[1], (SEQS, LENGTH, D), 1.5, 9.0, ((0, 4), (1, 2)), (1, 2, 2, 2.0)),
        "segments": jax.vmap(lambda own: jnp.searchsorted(jnp.cumsum(ragged_sizes(own, DOCS, LENGTH, LONGDOC, 2)), jnp.arange(LENGTH), side="right"))(jax.random.split(seeds[2], SEQS)).reshape((SEQS, LENGTH)).astype(jnp.int32),
        "valid": draw_valid(jax.random.fold_in(seeds[14], 71), 0),
        "norm_gain": jnp.clip(1.0 + 0.1 * jax.random.normal(seeds[4], (D,), jnp.float32), 0.5, 1.5).astype(jnp.bfloat16),
        "w_in": centred(seeds[5], (D, 2, DI), D ** -0.5, 0.125, ((0, 4), (2, 4))),
        "conv_w": centred(seeds[6], (KCONV, DI), 0.5, 3.0, ((1, 16),)),
        "conv_b": jnp.clip(jax.random.uniform(seeds[7], (DI,), jnp.float32, -0.5, 0.5) * steps_of(seeds[7], (DI,), ((0, 16),), -0.4, 0.0), -0.5, 0.5).astype(jnp.bfloat16),
        "x_proj": centred(seeds[8], (RANK + 2 * NST, DI), DI ** -0.5, 0.09375, ((1, 16),)),
        "dt_w": centred(seeds[9], (RANK, DI), RANK ** -0.5, 0.5, ((1, 16),)),
        "dt_bias": jnp.clip(-6.5 + 4.0 * jax.random.uniform(seeds[10], (DI,), jnp.float32) ** steps_of(seeds[10], (DI,), ((0, 16),), -0.2, 0.2), -6.5, -2.5).astype(jnp.bfloat16),
        "a_log": jnp.clip(2.75 * jax.random.uniform(seeds[11], (NST, DI), jnp.float32) ** steps_of(seeds[11], (NST, DI), ((1, 16),), -0.2, 0.2), 0.0, 2.75).astype(jnp.bfloat16),
        "d_skip": jnp.clip(0.5 + 1.0 * jax.random.uniform(seeds[12], (DI,), jnp.float32) ** steps_of(seeds[12], (DI,), ((0, 16),), -0.2, 0.2), 0.5, 1.5).astype(jnp.bfloat16),
        "w_out": centred(seeds[13], (DI, D), (DI // 16) ** -0.5, 0.375, ((0, 4), (1, 4))),
    }


@jax.custom_vjp
def low(v):
    return lax.optimization_barrier(v.astype(jnp.bfloat16)).astype(jnp.float32)

@jax.custom_vjp
def low_back(v):
    return v

def low_keep(v):
    return (low(v), None)

def low_pass(kept, grad):
    return (grad,)

def back_keep(v):
    return (v, None)

def back_low(kept, grad):
    return (low(grad),)
low.defvjp(low_keep, low_pass)
low_back.defvjp(back_keep, back_low)
highest = lax.Precision.HIGHEST
eps = 1e-05

def strip_states(carry_in, deltas, driven, input_b, seg_ids, seg_before, rates):
    log_decay = jnp.cumsum(deltas[:, :, None, :] * rates[None, None], axis=1)
    span = deltas.shape[1]
    positions = jnp.arange(span)
    causal = positions[:, None] >= positions[None, :]
    same_doc = (seg_ids[:, :, None] == seg_ids[:, None, :]) & causal[None]
    open_pair = same_doc[:, :, :, None, None]
    log_gap = log_decay[:, :, None] - log_decay[:, None, :]
    weight = jnp.where(open_pair, jnp.exp(jnp.where(open_pair, log_gap, 0.0)), 0.0)
    source = input_b[:, :, :, None] * driven[:, :, None, :]
    inside = lax.optimization_barrier(jnp.sum(weight * source[:, None], axis=2))
    kept = (seg_ids == seg_before[:, None]).astype(jnp.float32)
    return inside + jnp.exp(log_decay) * kept[:, :, None, None] * carry_in[:, None]

def conv_mix(ext_x, ext_seg, conv_weight, conv_bias):
    conv_taps = conv_weight.shape[0]
    span = ext_x.shape[1] - conv_taps + 1
    seg_now = ext_seg[:, conv_taps - 1:]
    total = jnp.zeros_like(ext_x[:, conv_taps - 1:]) + conv_bias
    for shift_by in range(conv_taps):
        same_doc = (ext_seg[:, shift_by:shift_by + span] == seg_now).astype(jnp.float32)
        total = total + conv_weight[shift_by] * ext_x[:, shift_by:shift_by + span] * same_doc[..., None]
    return total

def sequence_scan(deltas, driven, input_b, output_c, seg_ids, rates):
    batch, length_all, channels = deltas.shape
    pieces = length_all // STRIP

    def fold(values):
        return jnp.moveaxis(values.reshape((batch, pieces, STRIP) + values.shape[2:]), 1, 0)
    before_all = jnp.concatenate([jnp.full((batch, 1), -1, jnp.int32), seg_ids[:, :-1].astype(jnp.int32)], axis=1)

    @jax.checkpoint
    def advance(carry_in, items):
        deltas_s, driven_s, b_s, c_s, seg_s, before_s = items
        states = strip_states(carry_in, deltas_s, driven_s, b_s, seg_s, before_s, rates)
        return (states[:, -1], lax.optimization_barrier(jnp.sum(states * c_s[..., None], axis=2)))
    start = jnp.zeros((batch, input_b.shape[2], channels), jnp.float32)
    items = (fold(deltas), fold(driven), fold(input_b), fold(output_c), fold(seg_ids), fold(before_all)[:, :, 0])
    final, outs = lax.scan(advance, start, items)
    return jnp.moveaxis(outs, 0, 1).reshape(batch, length_all, channels)

def layer(hidden, target, seg_ids, valid_rows, weights):
    norm_gain, w_in, conv_w, conv_b, x_proj, dt_w, dt_bias, a_log, d_skip, w_out = weights
    batch, length_all, model_width = hidden.shape
    channels = w_in.shape[2]
    scale = lax.rsqrt(lax.optimization_barrier(jnp.mean(hidden * hidden, axis=-1, keepdims=True)) + eps)
    normed = low(hidden * scale * norm_gain)
    mixed_in = low_back(jnp.einsum('td,dkc->tkc', normed.reshape(-1, model_width), w_in, precision=highest))
    branch_x = mixed_in[:, 0].reshape(batch, length_all, channels)
    branch_z = mixed_in[:, 1].reshape(batch, length_all, channels)
    conv_taps = conv_w.shape[0]
    ext_x = jnp.pad(branch_x, ((0, 0), (conv_taps - 1, 0), (0, 0)))
    ext_seg = jnp.pad(seg_ids, ((0, 0), (conv_taps - 1, 0)), constant_values=-1)
    xconv = conv_mix(ext_x, ext_seg, conv_w, conv_b)
    inner_u = low(jax.nn.silu(xconv))
    proj = low_back(jnp.dot(inner_u.reshape(-1, channels), x_proj.T, precision=highest))
    rank_low = low(proj[:, :RANK])
    input_b = proj[:, RANK:RANK + NST].reshape(batch, length_all, NST)
    output_c = proj[:, RANK + NST:].reshape(batch, length_all, NST)
    step_pre = low_back(jnp.dot(rank_low, dt_w, precision=highest)) + dt_bias
    deltas = jax.nn.softplus(step_pre).reshape(batch, length_all, channels)
    rates = -jnp.exp(a_log)
    scanned = sequence_scan(deltas, deltas * inner_u, input_b, output_c, seg_ids, rates)
    y_value = scanned + d_skip * inner_u
    gated = low(y_value * jax.nn.silu(branch_z))
    branch_out = low_back(jnp.dot(gated.reshape(-1, channels), w_out, precision=highest))
    block_out = hidden + branch_out.reshape(batch, length_all, model_width)
    errors = block_out - target
    part = jnp.sum(valid_rows[..., None] * errors * errors) / model_width
    return (block_out, part)

def reference(x_in, teacher, segments, valid, norm_gain, w_in, conv_w, conv_b, x_proj, dt_w, dt_bias, a_log, d_skip, w_out):
    hidden = x_in.astype(jnp.float32)
    target = teacher.astype(jnp.float32)
    valid_rows = valid.astype(jnp.float32)
    params = (norm_gain.astype(jnp.float32), w_in.astype(jnp.float32), conv_w.astype(jnp.float32), conv_b.astype(jnp.float32), x_proj.astype(jnp.float32), dt_w.astype(jnp.float32), dt_bias.astype(jnp.float32), a_log.astype(jnp.float32), d_skip.astype(jnp.float32), w_out.astype(jnp.float32))
    count = jnp.sum(valid_rows)
    batch_step = 2 if SEQS % 2 == 0 else 1
    steps_count = SEQS // batch_step

    def regroup(values):
        return values.reshape((steps_count, batch_step) + values.shape[1:])

    def forward(hidden_all, weights):

        @jax.checkpoint
        def group_pass(total, items):
            hidden_g, target_g, seg_g, valid_g = items
            out_g, part = layer(hidden_g, target_g, seg_g, valid_g, weights)
            return (total + part, out_g)
        total, outs = lax.scan(group_pass, jnp.zeros((), jnp.float32), (regroup(hidden_all), regroup(target), regroup(segments), regroup(valid_rows)))
        return (outs.reshape(hidden_all.shape), total / count)
    (block_out, loss_value), pull = jax.vjp(forward, hidden, params)
    loss_scale = TOKENS * D / 2
    grad_hidden, grad_weights = pull((jnp.zeros_like(block_out), jnp.ones_like(loss_value) * loss_scale))
    return (block_out, loss_value, grad_hidden, grad_weights[0], grad_weights[1], grad_weights[2], grad_weights[3], grad_weights[4], grad_weights[5], grad_weights[6], grad_weights[7], grad_weights[8], grad_weights[9])
```

```python
import jax
import jax.numpy as jnp
from jax import lax
from jax.experimental import pallas as pl
from jax.experimental.pallas import tpu as pltpu
from jax.sharding import PartitionSpec as P

f32 = jnp.float32
bf16 = jnp.bfloat16
eps = 1e-05
LOG2E = 1.4426950408889634
LN2 = 0.6931471805599453
FAR=1e30
SUB=8

def softplus(v):
    tail=jnp.exp(-jnp.abs(v))
    small=tail*(1.0-tail*(0.5-tail*(1.0/3.0)))
    return jnp.maximum(v,0.0)+jnp.where(tail<0.0078125,small,jnp.log(1.0+tail))

def sigmoid(v):
    return 1.0/(1.0+jnp.exp(-v))

def fold_rows(parts, row):
    half=1
    while len(parts)>1:
        low=(row & half)==0
        parts=[jnp.where(low,a,b)+pltpu.roll(jnp.where(low,b,a),half,0) for a,b in zip(parts[0::2],parts[1::2])]
        half*=2
    return parts[0]

def tiles_of(ref,base,w):
    return [ref[pl.ds(base,SUB),g*w:(g+1)*w] for g in range(ref.shape[1]//w)]

def row_of(tile,r):
    return jnp.broadcast_to(tile[r:r+1,:],tile.shape)

def scan_fwd_kernel(bct_ref, rank_ref, u_ref, z_ref, keep_ref, dtw_ref, dtb_ref, a2_ref, skip_ref,
                    gated_ref, y_ref, h_ref, state, dec_s, du_s):
    TB,C=u_ref.shape; N=a2_ref.shape[0]; w=min(128,C); NG=C//w; NI=N//SUB
    @pl.when(pl.program_id(0)==0)
    def _(): state[...]=jnp.zeros_like(state)
    pre=jnp.dot(rank_ref[...],dtw_ref[...],preferred_element_type=f32)+dtb_ref[...]
    delta=softplus(pre)
    u=u_ref[...].astype(f32)
    du_s[...]=delta*u
    dec_s[...]=jnp.where(keep_ref[...]>0.5,delta,FAR)
    row=lax.broadcasted_iota(jnp.int32,(SUB,w),0)
    bt=[bct_ref[SUB*i:SUB*(i+1),:] for i in range(NI)]
    ct=[bct_ref[N+SUB*i:N+SUB*(i+1),:] for i in range(NI)]
    a2=[[a2_ref[SUB*i:SUB*(i+1),g*w:(g+1)*w] for g in range(NG)] for i in range(NI)]
    def body(j,h):
        h=[list(r) for r in h]
        base=pl.multiple_of(j*SUB,SUB)
        acc=[[] for _ in range(NG)]
        dls=tiles_of(dec_s,base,w); dus=tiles_of(du_s,base,w)
        for r in range(SUB):
            t=base+r
            idx=jnp.full((SUB,TB),t,jnp.int32)
            bv=[jnp.take_along_axis(b,idx,axis=1)[:,:w] for b in bt]
            cv=[jnp.take_along_axis(c,idx,axis=1)[:,:w] for c in ct]
            for g in range(NG):
                dl=row_of(dls[g],r); du=row_of(dus[g],r)
                p=None
                for i in range(NI):
                    h[i][g]=jnp.exp2(dl*a2[i][g])*h[i][g]+bv[i]*du
                    h_ref[pl.ds(pl.multiple_of(t*N+SUB*i,SUB),SUB),g*w:(g+1)*w]=h[i][g].astype(h_ref.dtype)
                    q=cv[i]*h[i][g]
                    p=q if p is None else p+q
                acc[g].append(p)
        for g in range(NG):
            y_ref[pl.ds(base,SUB),g*w:(g+1)*w]=fold_rows(acc[g],row)
        return tuple(tuple(r) for r in h)
    h0=tuple(tuple(state[SUB*i:SUB*(i+1),g*w:(g+1)*w] for g in range(NG)) for i in range(NI))
    h1=lax.fori_loop(0,TB//SUB,body,h0)
    for i in range(NI):
        for g in range(NG):
            state[SUB*i:SUB*(i+1),g*w:(g+1)*w]=h1[i][g]
    y=y_ref[...]+skip_ref[...]*u_ref[...].astype(f32)
    y_ref[...]=y
    z=z_ref[...].astype(f32)
    gated_ref[...]=(y*z*sigmoid(z)).astype(bf16)

def scan_fwd(bct, rank_low, u, z, keep, dtw, dtb, a2, skip, TB=128, hdt=f32):
    TOK,C=u.shape; N=a2.shape[0]; K=rank_low.shape[1]
    blk=lambda s:pl.BlockSpec((TB,s),lambda i:(i,0))
    whole=lambda a:pl.BlockSpec(a.shape,lambda i:(0,0))
    return pl.pallas_call(scan_fwd_kernel,name="scan_fwd",grid=(TOK//TB,),
        in_specs=[pl.BlockSpec((2*N,TB),lambda i:(0,i)),blk(K),blk(C),blk(C),blk(1),whole(dtw),whole(dtb),whole(a2),whole(skip)],
        out_specs=[blk(C),blk(C),pl.BlockSpec((TB*N,C),lambda i:(i,0))],
        out_shape=[jax.ShapeDtypeStruct((TOK,C),bf16),jax.ShapeDtypeStruct((TOK,C),f32),jax.ShapeDtypeStruct((TOK*N,C),hdt)],
        scratch_shapes=[pltpu.VMEM((N,C),f32),pltpu.VMEM((TB,C),f32),pltpu.VMEM((TB,C),f32)],
        compiler_params=pltpu.CompilerParams(dimension_semantics=("arbitrary",)),
    )(bct,rank_low,u,z,keep,dtw,dtb,a2,skip)

def scan_bwd_kernel(bct_ref, rank_ref, u_ref, z_ref, keep_ref, y_ref, gg_ref, h_ref, hp_ref, dtw_ref, dtb_ref, a2_ref, skip_ref,
                    gz_ref, gpl_ref, gu_ref, grank_ref, gbc_ref, ga_ref, gdtw_ref, gvec_ref,
                    dlam_s, ga_s, dec_s, du_s, gy_s, s1_s, s2_s):
    TB,C=u_ref.shape; N=a2_ref.shape[0]; w=min(128,C); NG=C//w; NI=N//SUB
    step=pl.program_id(0)
    @pl.when(step==0)
    def _():
        dlam_s[...]=jnp.zeros_like(dlam_s); ga_s[...]=jnp.zeros_like(ga_s)
        gdtw_ref[...]=jnp.zeros_like(gdtw_ref); gvec_ref[...]=jnp.zeros_like(gvec_ref)
    pre=jnp.dot(rank_ref[...],dtw_ref[...],preferred_element_type=f32)+dtb_ref[...]
    delta=softplus(pre)
    u=u_ref[...].astype(f32)
    du_s[...]=delta*u
    dec_s[...]=jnp.where(keep_ref[...]>0.5,delta,FAR)
    z=z_ref[...].astype(f32); sg=sigmoid(z); gg=gg_ref[...]
    gy=gg*z*sg
    gy_s[...]=gy
    gz_ref[...]=(gg*y_ref[...]*sg*(1.0+z*(1.0-sg))).astype(bf16)
    row=lax.broadcasted_iota(jnp.int32,(SUB,w),0)
    lane=lax.broadcasted_iota(jnp.int32,(SUB,TB),1)
    bt=[bct_ref[SUB*i:SUB*(i+1),:] for i in range(NI)]
    ct=[bct_ref[N+SUB*i:N+SUB*(i+1),:] for i in range(NI)]
    a2=[[a2_ref[SUB*i:SUB*(i+1),g*w:(g+1)*w] for g in range(NG)] for i in range(NI)]
    at=lambda i,t:pl.ds(pl.multiple_of(t*N+SUB*i,SUB),SUB)
    gb0=tuple(jnp.zeros((SUB,TB),f32) for _ in range(2*NI))
    def token(r,t,dls,dus,gys,first,dlam,ga,gb,acc1,acc2):
        idx=jnp.full((SUB,TB),t,jnp.int32)
        bv=[jnp.take_along_axis(b,idx,axis=1)[:,:w] for b in bt]
        cv=[jnp.take_along_axis(c,idx,axis=1)[:,:w] for c in ct]
        sumb=[None]*NI; sumc=[None]*NI
        for g in range(NG):
            lo=slice(g*w,(g+1)*w)
            dl=row_of(dls[g],r); du=row_of(dus[g],r); gyr=row_of(gys[g],r)
            p1=None;p2=None
            for i in range(NI):
                h_now=h_ref[at(i,t),lo].astype(f32)
                if first: h_prev=hp_ref[SUB*i:SUB*(i+1),lo].astype(f32)
                else: h_prev=h_ref[at(i,t-1),lo].astype(f32)
                lam=cv[i]*gyr+dlam[i][g]
                dlm=jnp.exp2(dl*a2[i][g])*lam
                dlam[i][g]=dlm
                q=dlm*h_prev
                x1=a2[i][g]*q; x2=lam*bv[i]
                p1=x1 if p1 is None else p1+x1
                p2=x2 if p2 is None else p2+x2
                ga[i][g]=ga[i][g]+dl*q
                b=lam*du; c=gyr*h_now
                sumb[i]=b if sumb[i] is None else sumb[i]+b
                sumc[i]=c if sumc[i] is None else sumc[i]+c
            acc1[g].append(p1); acc2[g].append(p2)
        here=lane==t
        for i in range(NI):
            gb[i]=jnp.where(here,jnp.sum(sumb[i],axis=1,keepdims=True),gb[i])
            gb[NI+i]=jnp.where(here,jnp.sum(sumc[i],axis=1,keepdims=True),gb[NI+i])
    def group(base,head,carry):
        dlam,ga,gb=carry
        dlam=[list(r) for r in dlam]; ga=[list(r) for r in ga]; gb=list(gb)
        dls=tiles_of(dec_s,base,w); dus=tiles_of(du_s,base,w); gys=tiles_of(gy_s,base,w)
        acc1=[[] for _ in range(NG)]; acc2=[[] for _ in range(NG)]
        for r in reversed(range(SUB)):
            token(r,base+r,dls,dus,gys,head and r==0, dlam,ga,gb,acc1,acc2)
        for g in range(NG):
            s1_s[pl.ds(base,SUB),g*w:(g+1)*w]=fold_rows(acc1[g][::-1],row)
            s2_s[pl.ds(base,SUB),g*w:(g+1)*w]=fold_rows(acc2[g][::-1],row)
        return tuple(map(tuple,dlam)),tuple(map(tuple,ga)),tuple(gb)
    ld=lambda ref:tuple(tuple(ref[SUB*i:SUB*(i+1),g*w:(g+1)*w] for g in range(NG)) for i in range(NI))
    nj=TB//SUB
    carry=lax.fori_loop(0,nj-1,lambda j,c:group(pl.multiple_of((nj-1-j)*SUB,SUB),False,c),(ld(dlam_s),ld(ga_s),gb0))
    dlam,ga,gb=group(0,True,carry)
    for i in range(NI):
        gbc_ref[SUB*i:SUB*(i+1),:]=gb[i]; gbc_ref[N+SUB*i:N+SUB*(i+1),:]=gb[NI+i]
        for g in range(NG):
            dlam_s[SUB*i:SUB*(i+1),g*w:(g+1)*w]=dlam[i][g]
            ga_s[SUB*i:SUB*(i+1),g*w:(g+1)*w]=ga[i][g]
    ga_ref[...]=ga_s[...]
    u=u_ref[...].astype(f32); s2=s2_s[...]; gy=gy_s[...]
    gpre=(s1_s[...]*LN2+u*s2)*sigmoid(pre)
    low=gpre.astype(bf16)
    gpl_ref[...]=low
    gu_ref[...]=gy*skip_ref[...]+delta*s2
    grank_ref[...]=lax.dot_general(low,dtw_ref[...],(((1,),(1,)),((),())),preferred_element_type=f32)
    gdtw_ref[...]+=lax.dot_general(rank_ref[...],low,(((0,),(0,)),((),())),preferred_element_type=f32)
    gvec_ref[0:1,:]+=jnp.sum(gpre,axis=0,keepdims=True)
    gvec_ref[1:2,:]+=jnp.sum(gy*u,axis=0,keepdims=True)

def scan_bwd(bct, rank_low, u, z, keep, y, gg, h, dtw, dtb, a2, skip, TB=128):
    TOK,C=u.shape; N=a2.shape[0]; K=rank_low.shape[1]; nb=TOK//TB
    blk=lambda s:pl.BlockSpec((TB,s),lambda i:(nb-1-i,0))
    whole=lambda s:pl.BlockSpec(s,lambda i:(0,0))
    sd=jax.ShapeDtypeStruct
    return pl.pallas_call(scan_bwd_kernel,name="scan_bwd",grid=(nb,),
        in_specs=[pl.BlockSpec((2*N,TB),lambda i:(0,nb-1-i)),blk(K),blk(C),blk(C),blk(1),blk(C),blk(C),
                  pl.BlockSpec((TB*N,C),lambda i:(nb-1-i,0)),
                  pl.BlockSpec((N,C),lambda i:(jnp.maximum((nb-1-i)*TB-1,0),0)),
                  whole(dtw.shape),whole(dtb.shape),whole(a2.shape),whole(skip.shape)],
        out_specs=[blk(C),blk(C),blk(C),blk(K),pl.BlockSpec((2*N,TB),lambda i:(0,nb-1-i)),whole((N,C)),whole((K,C)),whole((8,C))],
        out_shape=[sd((TOK,C),bf16),sd((TOK,C),bf16),sd((TOK,C),f32),sd((TOK,K),f32),sd((2*N,TOK),f32),sd((N,C),f32),sd((K,C),f32),sd((8,C),f32)],
        scratch_shapes=[pltpu.VMEM((N,C),f32),pltpu.VMEM((N,C),f32)]+[pltpu.VMEM((TB,C),f32)]*5,
        compiler_params=pltpu.CompilerParams(dimension_semantics=("arbitrary",)),
    )(bct,rank_low,u,z,keep,y,gg,h,h,dtw,dtb,a2,skip)


def swap_cores(value):
    return lax.ppermute(value, "context", [(0, 1), (1, 0)])


def gather_context(value):
    if lax.axis_size("context") != 2:
        return lax.all_gather(value, "context")
    other = swap_cores(value)
    first = lax.axis_index("context") == 0
    return jnp.stack([jnp.where(first, value, other), jnp.where(first, other, value)])


def scatter_context(parts):
    if lax.axis_size("context") != 2:
        return lax.psum_scatter(parts, "context", scatter_dimension=0)
    place = lax.axis_index("context")
    other = swap_cores(lax.dynamic_index_in_dim(parts, 1 - place, 0, False))
    own = lax.dynamic_index_in_dim(parts, place, 0, False)
    return (own.astype(jnp.float32) + other.astype(jnp.float32)).astype(parts.dtype)


def shifted(values, steps):
    if steps == 0:
        return values
    blank = jnp.zeros((abs(steps),) + values.shape[1:], values.dtype)
    if steps > 0:
        return jnp.concatenate([blank, values[:-steps]], axis=0)
    return jnp.concatenate([values[-steps:], blank], axis=0)


def silu_slope(values):
    sigma = jax.nn.sigmoid(values)
    return sigma * (1.0 + values * (1.0 - sigma))


def on_device(
    x_in,
    teacher,
    segments,
    valid,
    norm_gain,
    w_in,
    conv_w,
    conv_b,
    x_proj,
    dt_w,
    dt_bias,
    a_log,
    d_skip,
    w_out,
):
    groups, blocklen, width = x_in.shape
    nf, ctx, tp = (lax.axis_size(name) for name in ("fsdp", "context", "tensor"))
    place = lax.axis_index("context")
    rows_here, _, chans_tensor = w_in.shape
    piece = conv_w.shape[1] // ctx
    chans = nf * piece
    taps, rank_dim, nstate = conv_w.shape[0], dt_w.shape[0], a_log.shape[0]
    proj_dim = x_proj.shape[0]
    share = width // tp
    cols_here = w_out.shape[1]
    full = blocklen * ctx
    tokens = groups * full

    small = jnp.concatenate(
        [conv_w, conv_b[None], x_proj, dt_w, dt_bias[None], a_log, d_skip[None]], axis=0
    )
    nsmall = small.shape[0]
    small = lax.dynamic_slice_in_dim(small, place * piece, piece, 1)
    small = jnp.concatenate([small, norm_gain.reshape(-1, piece)], axis=0)
    small = lax.all_gather(small, "fsdp")
    gain_all = small[:, nsmall:].reshape(width).astype(f32)
    small = jnp.swapaxes(small[:, :nsmall], 0, 1).reshape(nsmall, chans)
    marks = [0, taps, taps + 1]
    for size in (proj_dim, rank_dim, 1, nstate, 1):
        marks.append(marks[-1] + size)
    convw_v, convb_v, xproj_v, dtw_v, dtb_v, alog_v, skip_v = (
        small[a:b] for a, b in zip(marks[:-1], marks[1:])
    )
    convw_v, convb_v, skip_v, dtb_v = (v.astype(f32) for v in (convw_v, convb_v, skip_v, dtb_v))
    rates = -jnp.exp(alog_v.astype(f32))

    win_own = lax.dynamic_index_in_dim(
        w_in.reshape(rows_here, 2, nf, ctx, piece), place, 3, False
    ).reshape(rows_here, 2 * chans)
    win_v = lax.all_gather(win_own, "fsdp", axis=0, tiled=True)
    wout_own = lax.dynamic_index_in_dim(
        w_out.reshape(nf, ctx, piece, cols_here), place, 1, False
    ).reshape(chans, cols_here)
    wout_v = jnp.swapaxes(lax.all_gather(wout_own, "fsdp"), 0, 1).reshape(chans, tp, share)

    hidden = x_in.astype(f32)
    scale = lax.rsqrt(jnp.mean(hidden * hidden, axis=-1, keepdims=True) + eps)
    normed = (hidden * scale * gain_all).astype(bf16)
    normed = jnp.swapaxes(gather_context(normed), 0, 1).reshape(tokens, width)
    seg = jnp.swapaxes(gather_context(segments), 0, 1).reshape(groups, full)
    masks = []
    for back in range(taps):
        same = seg[:, back:] == seg[:, : full - back]
        same = jnp.pad(same, ((0, 0), (back, 0)), constant_values=False)
        masks.append(same.reshape(tokens, 1).astype(f32))

    mixed = jnp.dot(normed, win_v, preferred_element_type=f32)
    branch_x, branch_z = mixed[:, :chans], mixed[:, chans:]
    xconv = convb_v
    for tap in range(taps):
        back = taps - 1 - tap
        xconv = xconv + convw_v[tap][None] * (shifted(branch_x, back) * masks[back])
    u_low = jax.nn.silu(xconv).astype(bf16)
    proj = lax.psum(
        lax.dot_general(u_low, xproj_v, (((1,), (1,)), ((), ())), preferred_element_type=f32),
        ("tensor", "context"),
    )
    rank_low = proj[:, :rank_dim].astype(bf16)
    bct = proj[:, rank_dim:].T
    a2 = rates * LOG2E
    gated, y_value, states = scan_fwd(
        bct, rank_low, u_low, branch_z, masks[1], dtw_v, dtb_v, a2, skip_v
    )

    def to_shares(parts):
        parts = parts.reshape(tp, groups, ctx, blocklen, share)
        parts = scatter_context(jnp.moveaxis(parts, 2, 0))
        return lax.psum_scatter(parts, "tensor", scatter_dimension=0).astype(f32)

    out_part = jnp.einsum("tc,czj->ztj", gated, wout_v, preferred_element_type=f32).astype(bf16)
    first_col = lax.axis_index("tensor") * share
    hidden_share = lax.dynamic_slice_in_dim(x_in, first_col, share, 2).astype(f32)
    target_share = lax.dynamic_slice_in_dim(teacher, first_col, share, 2).astype(f32)
    out_share = hidden_share + to_shares(out_part)
    errors = out_share - target_share
    valid_rows = valid.astype(f32)[..., None]
    count = lax.psum(jnp.sum(valid_rows), ("fsdp", "context"))
    loss_part = jnp.sum(valid_rows * errors * errors) / width
    grad_out = (tokens * nf / count) * valid_rows * errors
    grad_branch = lax.all_gather(grad_out.astype(bf16), "tensor")
    grad_branch = jnp.moveaxis(gather_context(grad_branch), 0, 2).reshape(tp, tokens, share)
    grad_gated = jnp.einsum("ztj,czj->tc", grad_branch, wout_v, preferred_element_type=f32)
    grad_wout = jnp.einsum("tc,ztj->czj", gated, grad_branch, preferred_element_type=f32)
    grad_wout = jnp.swapaxes(grad_wout.reshape(chans, nf, cols_here), 0, 1).astype(bf16)
    grad_wout = lax.psum_scatter(grad_wout, "fsdp", scatter_dimension=0).astype(f32)

    grad_z, grad_pre, grad_u, grad_rank, grad_bc, grad_rates2, grad_dtw, grad_vec = scan_bwd(
        bct, rank_low, u_low, branch_z, masks[1], y_value, grad_gated, states, dtw_v, dtb_v, a2, skip_v
    )
    grad_proj = lax.psum(
        jnp.concatenate([grad_rank, grad_bc.T], axis=1), ("tensor", "context")
    ).astype(bf16)
    grad_xproj = lax.dot_general(
        grad_proj, u_low, (((0,), (0,)), ((), ())), preferred_element_type=f32
    )
    grad_inner = grad_u + jnp.dot(grad_proj, xproj_v, preferred_element_type=f32)
    grad_xconv = grad_inner * silu_slope(xconv)
    grad_x = 0.0
    grad_convw = []
    for tap in range(taps):
        back = taps - 1 - tap
        reached = grad_xconv * masks[back]
        grad_convw.append(jnp.sum(reached * shifted(branch_x, back), axis=0, keepdims=True))
        grad_x = grad_x + convw_v[tap][None] * shifted(reached, -back)
    grad_convb = jnp.sum(grad_xconv, axis=0, keepdims=True)
    grad_mixed = jnp.concatenate([grad_x.astype(bf16), grad_z], axis=1)
    along = jnp.sum(grad_mixed.astype(f32) * mixed, axis=1).reshape(groups, ctx, blocklen)
    along = lax.psum(along, ("tensor", "context"))
    along = lax.dynamic_index_in_dim(along, place, 1, False)[..., None] / width
    normed_part = lax.dot_general(
        grad_mixed, win_v.reshape(tp, share, 2 * chans), (((1,), (2,)), ((), ())),
        preferred_element_type=f32,
    )
    normed_part = jnp.swapaxes(normed_part, 0, 1).astype(bf16)
    grad_normed = to_shares(normed_part)
    grad_win = lax.dot_general(
        normed, grad_mixed, (((0,), (0,)), ((), ())), preferred_element_type=f32
    ).astype(bf16)
    grad_win = lax.psum_scatter(grad_win, "fsdp", scatter_dimension=0, tiled=True).astype(f32)

    hat_share = hidden_share * scale
    gain_share = lax.dynamic_slice_in_dim(gain_all, first_col, share, 0)
    grad_share = grad_out + scale * (grad_normed * gain_share - hat_share * along)
    gain_part = jnp.sum(grad_normed * hat_share, axis=(0, 1))
    sums = jnp.zeros((width + share,), f32)
    sums = lax.dynamic_update_slice_in_dim(sums, gain_part, first_col, 0)
    sums = lax.dynamic_update_slice_in_dim(sums, loss_part[None], width, 0)
    sums = lax.psum(sums, ("fsdp", "context", "tensor"))
    loss_value = sums[width] / count
    grad_gain = lax.dynamic_slice_in_dim(
        sums, lax.axis_index("fsdp") * norm_gain.shape[0], norm_gain.shape[0], 0
    )

    small_grads = jnp.concatenate(
        grad_convw
        + [grad_convb, grad_xproj, grad_dtw, grad_vec[0:1], grad_rates2 * rates, grad_vec[1:2]],
        axis=0,
    )
    small_grads = jnp.swapaxes(small_grads.reshape(nsmall, nf, piece), 0, 1)
    small_grads = lax.psum_scatter(small_grads, "fsdp", scatter_dimension=0)
    small_grads = jnp.swapaxes(gather_context(small_grads), 0, 1).reshape(nsmall, ctx * piece)
    convw_g, convb_g, xproj_g, dtw_g, dtb_g, alog_g, skip_g = (
        small_grads[a:b] for a, b in zip(marks[:-1], marks[1:])
    )
    win_g = jnp.moveaxis(
        gather_context(grad_win).reshape(ctx, rows_here, 2, nf, piece), 0, 3
    ).reshape(rows_here, 2, chans_tensor)
    wout_g = jnp.swapaxes(
        gather_context(grad_wout).reshape(ctx, nf, piece, cols_here), 0, 1
    ).reshape(chans_tensor, cols_here)
    return (
        out_share,
        loss_value,
        grad_share,
        grad_gain,
        win_g,
        convw_g,
        convb_g[0],
        xproj_g,
        dtw_g,
        dtb_g[0],
        alog_g,
        skip_g[0],
        wout_g,
    )


def solution(mesh):
    return jax.shard_map(
        on_device,
        mesh=mesh,
        in_specs=(
            P("fsdp", "context", None),
            P("fsdp", "context", None),
            P("fsdp", "context"),
            P("fsdp", "context"),
            P("fsdp"),
            P("fsdp", None, "tensor"),
            P(None, ("tensor", "fsdp")),
            P(("tensor", "fsdp")),
            P(None, ("tensor", "fsdp")),
            P(None, ("tensor", "fsdp")),
            P(("tensor", "fsdp")),
            P(None, ("tensor", "fsdp")),
            P(("tensor", "fsdp")),
            P("tensor", "fsdp"),
        ),
        out_specs=(
            P("fsdp", "context", "tensor"),
            P(),
            P("fsdp", "context", "tensor"),
            P("fsdp"),
            P("fsdp", None, "tensor"),
            P(None, ("tensor", "fsdp")),
            P(("tensor", "fsdp")),
            P(None, ("tensor", "fsdp")),
            P(None, ("tensor", "fsdp")),
            P(("tensor", "fsdp")),
            P(None, ("tensor", "fsdp")),
            P(("tensor", "fsdp")),
            P("tensor", "fsdp"),
        ),
        check_vma=False,
    )
```

```python
import functools

import jax
import jax.numpy as jnp
from jax import lax
from jax.experimental import pallas as pl
from jax.experimental.pallas import tpu as pltpu
from jax.sharding import PartitionSpec as P

f32 = jnp.float32
bf16 = jnp.bfloat16
eps = 1e-05
LOG2E = 1.4426950408889634
LN2 = 0.6931471805599453
FAR = 1e30
SUB = 8
CHUNKS = 2
SCAN_BLOCK = 128
CONV_BLOCK = 256


def pick_block(total, most):
    size = min(total, most)
    while total % size:
        size //= 2
    return size


def whole(shape):
    return pl.BlockSpec(shape, lambda *_: (0,) * len(shape))


def params(*semantics):
    return pltpu.CompilerParams(dimension_semantics=semantics or None)


def cost(flops, arrays, exps=0):
    moved = sum(a.size * a.dtype.itemsize for a in arrays)
    return pl.CostEstimate(flops=int(flops), bytes_accessed=int(moved), transcendentals=int(exps))


def softplus(v):
    tail = jnp.exp(-jnp.abs(v))
    small = tail * (1.0 - tail * (0.5 - tail * (1.0 / 3.0)))
    return jnp.maximum(v, 0.0) + jnp.where(tail < 0.0078125, small, jnp.log(1.0 + tail))


def sigmoid(v):
    return 0.5 * jnp.tanh(0.5 * v) + 0.5


def fold_rows(parts, row):
    half = 1
    while len(parts) > 1:
        low = (row & half) == 0
        parts = [
            jnp.where(low, a, b) + pltpu.roll(jnp.where(low, b, a), half, 0)
            for a, b in zip(parts[0::2], parts[1::2])
        ]
        half *= 2
    return parts[0]


def tiles_of(ref, base, w):
    return [ref[pl.ds(base, SUB), g * w : (g + 1) * w] for g in range(ref.shape[1] // w)]


def row_of(tile, r):
    return jnp.broadcast_to(tile[r : r + 1, :], tile.shape)


UNROLL = 8


def put_columns(ref, values, wide_s, rows_s):
    TB, count = values.shape
    w = ref.shape[1]
    high = values.astype(bf16).astype(f32)
    wide_s[:, 0:count] = high
    wide_s[:, count : 2 * count] = values - high
    wide_s[:, 2 * count :] = jnp.zeros((TB, 128 - 2 * count), f32)
    row = lax.broadcasted_iota(jnp.int32, (SUB, 128), 0)
    lane = lax.broadcasted_iota(jnp.int32, (SUB, 128), 1)
    tiles = count // SUB
    picks = [(lane == row + SUB * i) | (lane == row + SUB * i + count) for i in range(tiles)]
    for t in range(0, TB, 2):
        pair = [jnp.broadcast_to(wide_s[t + d : t + d + 1, :], (SUB, 128)) for d in range(2)]
        for i in range(tiles):
            both = jnp.concatenate([jnp.where(picks[i], v, 0.0) for v in pair], axis=0)
            rows_s[(i * TB + t) * SUB : (i * TB + t + 2) * SUB, :] = both.astype(bf16)
    ones = jnp.ones((128, w), bf16)
    for i in range(tiles):
        block = slice(i * TB * SUB, (i + 1) * TB * SUB)
        ref[block, :] = jnp.dot(rows_s[block, :], ones, preferred_element_type=f32)


def row_sums(ref, TB, NG):
    columns = []
    for g in range(NG):
        parts = [ref[pl.ds(g * TB * SUB + s, TB, stride=SUB), :] for s in range(SUB)]
        while len(parts) > 1:
            parts = [a + b for a, b in zip(parts[0::2], parts[1::2])]
        columns.append(parts[0])
    return jnp.concatenate(columns, axis=1) if NG > 1 else columns[0]


def at_row(t, scale, offset=0):
    return pl.ds(pl.multiple_of(t * scale + offset, SUB), SUB)


def scan_fwd_kernel(
    bc_ref, rank_ref, u_ref, z_ref, keep_ref, dtw_ref, dtb_ref, a2_ref, skip_ref, start_ref,
    gated_ref, y_ref, delta_ref, h_ref, last_ref,
    dec_s, du_s, p_s, bc_s, wide_s, rows_s,
):
    TB, C = u_ref.shape
    N = a2_ref.shape[0]
    w = min(128, C)
    NG, NI = C // w, N // SUB

    @pl.when(pl.program_id(1) == 0)
    def _():
        last_ref[...] = start_ref[...]

    put_columns(bc_s, bc_ref[...], wide_s, rows_s)
    delta = softplus(
        jnp.dot(rank_ref[...], dtw_ref[...], preferred_element_type=f32) + dtb_ref[...]
    )
    delta_ref[...] = delta
    du_s[...] = delta * u_ref[...].astype(f32)
    dec_s[...] = jnp.where(keep_ref[...] > 0.5, delta, FAR)
    part = lambda ref: [
        [ref[SUB * i : SUB * (i + 1), g * w : (g + 1) * w] for g in range(NG)] for i in range(NI)
    ]
    a2 = part(a2_ref)

    def body(j, h):
        h = [list(r) for r in h]
        base = pl.multiple_of(j * UNROLL, SUB)
        dls, dus = tiles_of(dec_s, base, w), tiles_of(du_s, base, w)
        for r in range(UNROLL):
            t = base + r
            bv = [bc_s[at_row(t, SUB, i * TB * SUB), :] for i in range(NI)]
            cv = [bc_s[at_row(t, SUB, (NI + i) * TB * SUB), :] for i in range(NI)]
            for g in range(NG):
                dl, du = row_of(dls[g], r), row_of(dus[g], r)
                p = None
                for i in range(NI):
                    h_ref[at_row(t, N, SUB * i), g * w : (g + 1) * w] = h[i][g]
                    h[i][g] = jnp.exp2(dl * a2[i][g]) * h[i][g] + bv[i] * du
                    q = cv[i] * h[i][g]
                    p = q if p is None else p + q
                p_s[at_row(t, SUB, g * TB * SUB), :] = p
        return tuple(tuple(r) for r in h)

    h = lax.fori_loop(0, TB // UNROLL, body, tuple(tuple(r) for r in part(last_ref)))
    for i in range(NI):
        for g in range(NG):
            last_ref[SUB * i : SUB * (i + 1), g * w : (g + 1) * w] = h[i][g]
    y = row_sums(p_s, TB, NG) + skip_ref[...] * u_ref[...].astype(f32)
    y_ref[...] = y
    z = z_ref[...]
    gated_ref[...] = (y * z * sigmoid(z)).astype(bf16)


def scan_fwd(groups, bc, rank_low, u, z, keep, dtw, dtb, a2, skip, start):
    rows, C = u.shape
    N, R = a2.shape[0], rank_low.shape[1]
    w = min(128, C)
    TB = pick_block(rows // groups, SCAN_BLOCK)
    nb = rows // groups // TB
    blk = lambda s, n=TB: pl.BlockSpec((n, s), lambda g, b: (g * nb + b, 0))
    own = pl.BlockSpec((N, C), lambda g, b: (g, 0))
    sd = jax.ShapeDtypeStruct
    outs = [
        sd((rows, C), bf16), sd((rows, C), f32), sd((rows, C), f32), sd((rows * N, C), f32),
        sd((groups * N, C), f32),
    ]
    return pl.pallas_call(
        scan_fwd_kernel,
        name="scan_fwd",
        grid=(groups, nb),
        in_specs=[
            blk(2 * N), blk(R), blk(C), blk(C), blk(1),
            whole(dtw.shape), whole(dtb.shape), whole(a2.shape), whole(skip.shape),
            own,
        ],
        out_specs=[blk(C), blk(C), blk(C), blk(C, TB * N), own],
        out_shape=outs,
        scratch_shapes=[pltpu.VMEM((TB, C), f32)] * 2
        + [pltpu.VMEM((TB * (C // w) * SUB, w), f32), pltpu.VMEM((TB * 2 * N, w), f32)]
        + [pltpu.VMEM((TB, 128), f32), pltpu.VMEM((TB * 2 * N, 128), bf16)],
        compiler_params=params("arbitrary", "arbitrary"),
        cost_estimate=cost(rows * C * N * 8, outs, rows * C * N),
    )(bc, rank_low, u, z, keep, dtw, dtb, a2, skip, start)


def scan_bwd_kernel(
    bc_ref, rank_ref, u_ref, z_ref, keep_ref, y_ref, delta_ref, gg_ref, h_ref,
    dtw_ref, a2_ref, skip_ref, end_ref, late_ref,
    gz_ref, gpl_ref, gu_ref, grank_ref, gb_ref, gc_ref, first_ref, ga_ref, gdtw_ref, gvec_ref,
    dec_s, du_s, gy_s, r_s, s2_s, bc_s, mb_s, mc_s, next_s, wide_s, rows_s,
):
    TB, C = u_ref.shape
    N = a2_ref.shape[0]
    w = min(128, C)
    NG, NI = C // w, N // SUB
    b = pl.program_id(1)

    @pl.when((b == 0) & (pl.program_id(0) == 0))
    def _():
        ga_ref[...] = jnp.zeros_like(ga_ref)
        gdtw_ref[...] = jnp.zeros_like(gdtw_ref)
        gvec_ref[...] = jnp.zeros_like(gvec_ref)

    @pl.when(b == 0)
    def _():
        first_ref[...] = late_ref[...]
        next_s[...] = end_ref[...]

    put_columns(bc_s, bc_ref[...], wide_s, rows_s)
    delta = delta_ref[...]
    u = u_ref[...].astype(f32)
    du_s[...] = delta * u
    dec_s[...] = jnp.where(keep_ref[...] > 0.5, delta, FAR)
    z = z_ref[...]
    sg = sigmoid(z)
    gg = gg_ref[...]
    gy = gg * z * sg
    gy_s[...] = gy
    gz_ref[...] = (gg * y_ref[...] * sg * (1.0 + z * (1.0 - sg))).astype(bf16)
    gvec_ref[1:2, :] += jnp.sum(gy * u, axis=0, keepdims=True)
    part = lambda ref: [
        [ref[SUB * i : SUB * (i + 1), g * w : (g + 1) * w] for g in range(NG)] for i in range(NI)
    ]
    a2 = part(a2_ref)

    def body(j, carry):
        dlam, ga, h_now = ([list(r) for r in rows] for rows in carry)
        base = pl.multiple_of(TB - UNROLL - j * UNROLL, SUB)
        dls, dus, gys = tiles_of(dec_s, base, w), tiles_of(du_s, base, w), tiles_of(gy_s, base, w)
        for r in reversed(range(UNROLL)):
            t = base + r
            bv = [bc_s[at_row(t, SUB, i * TB * SUB), :] for i in range(NI)]
            cv = [bc_s[at_row(t, SUB, (NI + i) * TB * SUB), :] for i in range(NI)]
            mb, mc = [None] * NI, [None] * NI
            for g in range(NG):
                dl, du, gyr = row_of(dls[g], r), row_of(dus[g], r), row_of(gys[g], r)
                p, s2 = None, None
                for i in range(NI):
                    h_prev = h_ref[at_row(t, N, SUB * i), g * w : (g + 1) * w]
                    lam = cv[i] * gyr + dlam[i][g]
                    e = dl * a2[i][g]
                    dlam[i][g] = jnp.exp2(e) * lam
                    q = e * (dlam[i][g] * h_prev)
                    p = q if p is None else p + q
                    ga[i][g] = ga[i][g] + q
                    x = lam * bv[i]
                    s2 = x if s2 is None else s2 + x
                    x = lam * du
                    mb[i] = x if mb[i] is None else mb[i] + x
                    x = gyr * h_now[i][g]
                    mc[i] = x if mc[i] is None else mc[i] + x
                    h_now[i][g] = h_prev
                r_s[at_row(t, SUB, g * TB * SUB), :] = p
                s2_s[at_row(t, SUB, g * TB * SUB), :] = s2
            for i in range(NI):
                mb_s[at_row(t, N, SUB * i), :] = mb[i]
                mc_s[at_row(t, N, SUB * i), :] = mc[i]
        return tuple(tuple(tuple(r) for r in rows) for rows in (dlam, ga, h_now))

    carry = tuple(tuple(tuple(r) for r in part(ref)) for ref in (first_ref, ga_ref, next_s))
    for ref, rows in zip(
        (first_ref, ga_ref, next_s), lax.fori_loop(0, TB // UNROLL, body, carry)
    ):
        for i in range(NI):
            for g in range(NG):
                ref[SUB * i : SUB * (i + 1), g * w : (g + 1) * w] = rows[i][g]
    ones = jnp.ones((SUB, w), bf16)
    for s, ref in ((mb_s, gb_ref), (mc_s, gc_ref)):
        ref[...] = lax.dot_general(
            ones, s[...].astype(bf16), (((1,), (1,)), ((), ())), preferred_element_type=f32
        )
    s2 = row_sums(s2_s, TB, NG)
    ratio = jnp.where(
        delta < 0.0625,
        1.0 - delta * (0.5 - delta * (1.0 / 6.0 - delta * (1.0 / 24.0 - delta * (1.0 / 120.0)))),
        (1.0 - jnp.exp(-delta)) / jnp.maximum(delta, 0.0625),
    )
    gpre = ratio * (row_sums(r_s, TB, NG) * LN2 + du_s[...] * s2)
    low = gpre.astype(bf16)
    gpl_ref[...] = low
    gu_ref[...] = gy_s[...] * skip_ref[...] + delta * s2
    grank_ref[...] = lax.dot_general(
        low, dtw_ref[...], (((1,), (1,)), ((), ())), preferred_element_type=f32
    )
    gdtw_ref[...] += lax.dot_general(
        rank_ref[...], low, (((0,), (0,)), ((), ())), preferred_element_type=f32
    )
    gvec_ref[0:1, :] += jnp.sum(gpre, axis=0, keepdims=True)


def scan_bwd(groups, bc, rank_low, u, z, keep, y, delta, gg, h, dtw, a2, skip, end, late):
    rows, C = u.shape
    N, R = a2.shape[0], rank_low.shape[1]
    w = min(128, C)
    TB = pick_block(rows // groups, SCAN_BLOCK)
    nb = rows // groups // TB
    where = lambda g, b: g * nb + nb - 1 - b
    blk = lambda s, n=TB: pl.BlockSpec((n, s), lambda g, b: (where(g, b), 0))
    own = pl.BlockSpec((N, C), lambda g, b: (g, 0))
    across = pl.BlockSpec((SUB, TB * N), lambda g, b: (0, where(g, b)))
    sd = jax.ShapeDtypeStruct
    outs = [
        sd((rows, C), bf16), sd((rows, C), bf16), sd((rows, C), f32), sd((rows, R), f32),
        sd((SUB, rows * N), f32), sd((SUB, rows * N), f32), sd((groups * N, C), f32),
        sd((N, C), f32), sd((R, C), f32), sd((8, C), f32),
    ]
    fold = pltpu.VMEM((TB * (C // w) * SUB, w), f32)
    return pl.pallas_call(
        scan_bwd_kernel,
        name="scan_bwd",
        grid=(groups, nb),
        in_specs=[
            blk(2 * N), blk(R), blk(C), blk(C), blk(1), blk(C), blk(C), blk(C), blk(C, TB * N),
            whole(dtw.shape), whole(a2.shape), whole(skip.shape), own, own,
        ],
        out_specs=[
            blk(C), blk(C), blk(C), blk(R), across, across, own,
            whole((N, C)), whole((R, C)), whole((8, C)),
        ],
        out_shape=outs,
        scratch_shapes=[pltpu.VMEM((TB, C), f32)] * 3
        + [fold] * 2
        + [pltpu.VMEM((TB * 2 * N, w), f32)]
        + [pltpu.VMEM((TB * N, w), f32)] * 2
        + [pltpu.VMEM((N, C), f32)]
        + [pltpu.VMEM((TB, 128), f32), pltpu.VMEM((TB * 2 * N, 128), bf16)],
        compiler_params=params("arbitrary", "arbitrary"),
        cost_estimate=cost(rows * C * N * 20, outs + [h], rows * C * N),
    )(bc, rank_low, u, z, keep, y, delta, gg, h, dtw, a2, skip, end, late)


def pick_kernel(slot_ref, w_ref, x_ref, z_ref):
    x_ref[...] = w_ref[:, 0, :]
    z_ref[...] = w_ref[:, 1, :]


def pick(place, w_in, pieces, ctx):
    rows, _, total = w_in.shape
    piece = total // pieces // ctx
    if piece % 128:
        own = lax.dynamic_index_in_dim(
            w_in.reshape(rows, 2, pieces, ctx, piece), place, 3, False
        ).reshape(rows, 2, pieces * piece)
        return own[:, 0], own[:, 1]
    out = jax.ShapeDtypeStruct((rows, pieces * piece), w_in.dtype)
    spec = pl.BlockSpec((rows, piece), lambda f, s: (0, f))
    return pl.pallas_call(
        pick_kernel,
        name="pick",
        grid_spec=pltpu.PrefetchScalarGridSpec(
            num_scalar_prefetch=1,
            grid=(pieces,),
            in_specs=[pl.BlockSpec((rows, 2, piece), lambda f, s: (0, 0, f * ctx + s[0]))],
            out_specs=[spec, spec],
        ),
        out_shape=[out, out],
        compiler_params=params("arbitrary"),
        cost_estimate=cost(0, [out, out, out, out]),
    )(place.reshape(1).astype(jnp.int32), w_in)


def put_kernel(slot_ref, xa_ref, xb_ref, za_ref, zb_ref, o_ref):
    first = slot_ref[0] == 0
    piece = o_ref.shape[2] // 2
    for branch, (own, other) in enumerate(((xa_ref, xb_ref), (za_ref, zb_ref))):
        a, b = own[...], other[...]
        o_ref[:, branch, 0:piece] = jnp.where(first, a, b)
        o_ref[:, branch, piece:] = jnp.where(first, b, a)


def put(place, x_own, x_other, z_own, z_other, pieces):
    rows, C = x_own.shape
    piece = C // pieces
    TB = pick_block(rows, 256)
    spec = pl.BlockSpec((TB, piece), lambda b, f, s: (b, f))
    out = jax.ShapeDtypeStruct((rows, 2, 2 * C), x_own.dtype)
    return pl.pallas_call(
        put_kernel,
        name="put",
        grid_spec=pltpu.PrefetchScalarGridSpec(
            num_scalar_prefetch=1,
            grid=(rows // TB, pieces),
            in_specs=[spec] * 4,
            out_specs=pl.BlockSpec((TB, 2, 2 * piece), lambda b, f, s: (b, 0, f)),
        ),
        out_shape=out,
        compiler_params=params("arbitrary", "arbitrary"),
        cost_estimate=cost(0, [out, out]),
    )(place.reshape(1).astype(jnp.int32), x_own, x_other, z_own, z_other)


def conv_in_kernel(
    place_ref, own_ref, other_ref, gain_ref, mask_ref, cw_ref, cb_ref, xp_ref, halo_ref, *refs
):
    pieces, outs = refs[:-8], refs[-8:]
    norm_ref, scale_ref, bx_ref, xc_ref, u_ref, proj_ref, tail_ref, ext_s = outs
    TB, C = u_ref.shape
    taps = cw_ref.shape[0]

    @pl.when(pl.program_id(1) == 0)
    def _():
        ext_s[0:SUB, :] = halo_ref[...]

    x = jnp.where(place_ref[1] == 1, own_ref[...], other_ref[...]).astype(f32)
    scale = lax.rsqrt(jnp.mean(x * x, axis=1, keepdims=True) + eps)
    scale_ref[...] = scale
    norm_ref[...] = (x * scale * gain_ref[...]).astype(bf16)
    bx = 0.0
    for turn, w_ref in enumerate(pieces):
        deep = w_ref.shape[0]
        first = pl.multiple_of((place_ref[0] ^ turn) * deep, deep)
        bx += jnp.dot(norm_ref[:, pl.ds(first, deep)], w_ref[...], preferred_element_type=f32)
    bx_ref[...] = bx
    ext_s[SUB:, :] = bx
    total = cb_ref[...] + cw_ref[taps - 1 : taps, :] * bx
    for tap in range(taps - 1):
        back = taps - 1 - tap
        total += cw_ref[tap : tap + 1, :] * (
            ext_s[SUB - back : SUB - back + TB, :] * mask_ref[:, back : back + 1]
        )
    xc_ref[...] = total
    u = (total * sigmoid(total)).astype(bf16)
    u_ref[...] = u
    proj_ref[...] = lax.dot_general(
        u, xp_ref[...], (((1,), (1,)), ((), ())), preferred_element_type=f32
    )
    ext_s[0:SUB, :] = bx[TB - SUB :, :]
    tail_ref[...] = bx[TB - SUB :, :]


def conv_in(groups, me, use_own, own, other, gain, pieces, masks, cw, cb, xp, halo):
    rows, D = own.shape
    C = pieces[0].shape[1]
    TB = pick_block(rows // groups, CONV_BLOCK)
    nb = rows // groups // TB
    blk = lambda s: pl.BlockSpec((TB, s), lambda g, b, _: (g * nb + b, 0))
    mine = pl.BlockSpec((SUB, C), lambda g, b, _: (g, 0))
    sd = jax.ShapeDtypeStruct
    R = xp.shape[0]
    outs = [
        sd((rows, D), bf16), sd((rows, 1), f32), sd((rows, C), f32), sd((rows, C), f32),
        sd((rows, C), bf16), sd((rows, R), f32), sd((groups * SUB, C), f32),
    ]
    return pl.pallas_call(
        conv_in_kernel,
        name="conv_in",
        grid_spec=pltpu.PrefetchScalarGridSpec(
            num_scalar_prefetch=1,
            grid=(groups, nb),
            in_specs=[
                pl.BlockSpec((TB, D), lambda g, b, p: ((g * nb + b) * p[1], 0)),
                pl.BlockSpec((TB, D), lambda g, b, p: ((g * nb + b) * (1 - p[1]), 0)),
                whole(gain.shape), blk(masks.shape[1]), whole(cw.shape), whole(cb.shape),
                whole(xp.shape), mine,
            ]
            + [whole(p.shape) for p in pieces],
            out_specs=[blk(D), blk(1), blk(C), blk(C), blk(C), blk(R), mine],
            scratch_shapes=[pltpu.VMEM((TB + SUB, C), f32)],
        ),
        out_shape=outs,
        compiler_params=params("arbitrary", "arbitrary"),
        cost_estimate=cost(2 * rows * D * C, outs + [own], rows * C),
    )(jnp.stack([me, use_own]).astype(jnp.int32), own, other, gain, masks, cw, cb, xp, halo, *pieces)


def conv_out_kernel(
    gu_ref, gp_ref, xp_ref, xc_ref, bx_ref, z_ref, gz_ref, u_ref, mask_ref, cw_ref, late_ref,
    gm_ref, along_ref, early_ref, gconv_ref, gxp_ref,
    *ext_s,
):
    TB, C = u_ref.shape
    taps = cw_ref.shape[0]

    @pl.when((pl.program_id(1) == 0) & (pl.program_id(0) == 0))
    def _():
        gconv_ref[...] = jnp.zeros_like(gconv_ref)
        gxp_ref[...] = jnp.zeros_like(gxp_ref)

    @pl.when(pl.program_id(1) == 0)
    def _():
        for back in range(1, taps):
            ext_s[back - 1][TB:, :] = late_ref[(back - 1) * SUB : back * SUB, :]

    gp = gp_ref[...]
    xc = xc_ref[...]
    sg = sigmoid(xc)
    inner = gu_ref[...] + jnp.dot(gp, xp_ref[...], preferred_element_type=f32)
    gxc = inner * (sg * (1.0 + xc * (1.0 - sg)))
    bx = bx_ref[...]
    gx = cw_ref[taps - 1 : taps, :] * gxc
    gconv_ref[taps - 1 : taps, :] += jnp.sum(gxc * bx, axis=0, keepdims=True)
    gconv_ref[taps : taps + 1, :] += jnp.sum(gxc, axis=0, keepdims=True)
    for back in range(1, taps):
        tap = taps - 1 - back
        ext = ext_s[back - 1]
        reached = gxc * mask_ref[:, back : back + 1]
        ext[0:TB, :] = reached
        moved = ext[back : back + TB, :]
        gx += cw_ref[tap : tap + 1, :] * moved
        gconv_ref[tap : tap + 1, :] += jnp.sum(moved * bx, axis=0, keepdims=True)
        ext[TB:, :] = reached[0:SUB, :]
        early_ref[(back - 1) * SUB : back * SUB, :] = reached[0:SUB, :]
    gz = gz_ref[...]
    gx = gx.astype(bf16)
    gm_ref[:, 0:C] = gx
    gm_ref[:, C:] = gz
    terms = (gx.astype(f32) * bx + gz.astype(f32) * z_ref[...]).astype(bf16)
    along_ref[...] = lax.dot_general(
        jnp.ones((SUB, C), bf16), terms, (((1,), (1,)), ((), ())), preferred_element_type=f32
    )
    gxp_ref[...] += lax.dot_general(
        gp, u_ref[...], (((0,), (0,)), ((), ())), preferred_element_type=f32
    )


def conv_out(groups, gu, gp, xp, xc, bx, z, gz, u, masks, cw, late):
    rows, C = u.shape
    taps = cw.shape[0]
    R = xp.shape[0]
    TB = pick_block(rows // groups, CONV_BLOCK)
    nb = rows // groups // TB
    blk = lambda s: pl.BlockSpec((TB, s), lambda g, b: (g * nb + nb - 1 - b, 0))
    own = pl.BlockSpec(((taps - 1) * SUB, C), lambda g, b: (g, 0))
    sd = jax.ShapeDtypeStruct
    outs = [
        sd((rows, 2 * C), bf16), sd((SUB, rows), f32), sd((groups * (taps - 1) * SUB, C), f32),
        sd((8, C), f32), sd((R, C), f32),
    ]
    return pl.pallas_call(
        conv_out_kernel,
        name="conv_out",
        grid=(groups, nb),
        in_specs=[
            blk(C), blk(R), whole(xp.shape), blk(C), blk(C), blk(C), blk(C), blk(C),
            blk(masks.shape[1]), whole(cw.shape), own,
        ],
        out_specs=[
            blk(2 * C),
            pl.BlockSpec((SUB, TB), lambda g, b: (0, g * nb + nb - 1 - b)),
            own,
            whole((8, C)),
            whole((R, C)),
        ],
        out_shape=outs,
        scratch_shapes=[pltpu.VMEM((TB + SUB, C), f32)] * (taps - 1),
        compiler_params=params("arbitrary", "arbitrary"),
        cost_estimate=cost(4 * rows * R * C, outs + [gu, xc, bx, z], rows * C),
    )(gu, gp, xp, xc, bx, z, gz, u, masks, cw, late)


def spread_kernel(slot_ref, x_ref, w_ref, *refs):
    o_ref = refs[-1]
    for z in range(o_ref.shape[0]):
        total = jnp.dot(x_ref[0], w_ref[z], preferred_element_type=f32)
        if len(refs) > 1:
            total = total + refs[0][z].astype(f32)
        o_ref[z] = total.astype(bf16)


def spread(slot, x, w, *added):
    _, rows, K = x.shape
    shares, _, share = w.shape
    per = 2 if shares % 2 == 0 and rows * share <= 512 * 512 else 1
    out = jax.ShapeDtypeStruct((shares, rows, share), bf16)
    block = pl.BlockSpec((per, rows, share), lambda z, s: (z, 0, 0))
    return pl.pallas_call(
        spread_kernel,
        name="spread",
        grid_spec=pltpu.PrefetchScalarGridSpec(
            num_scalar_prefetch=1,
            grid=(shares // per,),
            in_specs=[
                pl.BlockSpec((1, rows, K), lambda z, s: (s[0], 0, 0)),
                pl.BlockSpec((per, K, share), lambda z, s: (z, 0, 0)),
            ]
            + [block] * len(added),
            out_specs=block,
        ),
        out_shape=out,
        compiler_params=params("arbitrary"),
        cost_estimate=cost(2 * rows * K * shares * share, [out, x, w]),
    )(slot, x, w, *added)


def collect_kernel(slot_ref, own_ref, other_ref, w_ref, o_ref):
    shares, _, share = own_ref.shape

    def product(ref):
        total = jnp.dot(ref[0], w_ref[0:share, :], preferred_element_type=f32)
        for z in range(1, shares):
            total += jnp.dot(
                ref[z], w_ref[z * share : (z + 1) * share, :], preferred_element_type=f32
            )
        o_ref[0] = total

    @pl.when(pl.program_id(0) == 0)
    def _():
        product(own_ref)

    @pl.when(pl.program_id(0) == 1)
    def _():
        product(other_ref)


def collect(slot, own, other, w):
    shares, rows, share = own.shape
    C = w.shape[1]
    out = jax.ShapeDtypeStruct((2, rows, C), f32)
    return pl.pallas_call(
        collect_kernel,
        name="collect",
        grid_spec=pltpu.PrefetchScalarGridSpec(
            num_scalar_prefetch=1,
            grid=(2,),
            in_specs=[
                pl.BlockSpec(own.shape, lambda s, p: (0, 0, 0)),
                pl.BlockSpec(own.shape, lambda s, p: (0, 0, 0)),
                pl.BlockSpec(w.shape, lambda s, p: (0, 0)),
            ],
            out_specs=pl.BlockSpec((1, rows, C), lambda s, p: (s + p[0] - 2 * s * p[0], 0, 0)),
        ),
        out_shape=out,
        compiler_params=params("arbitrary"),
        cost_estimate=cost(4 * rows * C * share * shares, [out, own, other, w]),
    )(slot, own, other, w)


def after(value, *others):
    return lax.optimization_barrier((value,) + others)[0]


def swap_cores(value):
    return lax.ppermute(value, "context", [(0, 1), (1, 0)])


def paired():
    return lax.axis_size("context") == 2


def in_order(own, other):
    first = lax.axis_index("context") == 0
    return jnp.where(first, own, other), jnp.where(first, other, own)


def gather_context(value):
    if not paired():
        return lax.all_gather(value, "context")
    return jnp.stack(in_order(value, swap_cores(value)))


def sum_over(value, *axes):
    for axis in axes:
        size, step = lax.axis_size(axis), 1
        if size & (size - 1):
            value = lax.psum(value, axis)
            continue
        while step < size:
            value = value + lax.ppermute(value, axis, [(i, i ^ step) for i in range(size)])
            step *= 2
    return value


ROW = [(0, 1), (1, 0), (2, 3), (3, 2)]
COLUMN = [(0, 2), (2, 0), (1, 3), (3, 1)]


def gather_fsdp(value, *hold):
    size = lax.axis_size("fsdp")
    if size != 4 or value.shape[0] % 2:
        pieces = lax.all_gather(value, "fsdp")
        return jnp.zeros((), jnp.int32), [pieces[i] for i in range(size)]
    half = value.shape[0] // 2
    row = lax.ppermute(value, "fsdp", ROW)
    column = lax.ppermute(value, "fsdp", COLUMN)
    if hold:
        row, column = lax.optimization_barrier((row, column) + hold)[:2]
    far = jnp.concatenate(
        [lax.ppermute(row[:half], "fsdp", COLUMN), lax.ppermute(column[half:], "fsdp", ROW)]
    )
    return lax.axis_index("fsdp"), [value, row, column, far]


def stacked(me, pieces):
    if len(pieces) != 4:
        return jnp.stack(pieces)
    a, b, c, d = pieces
    odd, high = me % 2 == 1, me // 2 == 1
    pick2 = lambda flag, x, y: jnp.where(flag, y, x)
    return jnp.stack(
        [
            pick2(high, pick2(odd, a, b), pick2(odd, c, d)),
            pick2(high, pick2(odd, b, a), pick2(odd, d, c)),
            pick2(high, pick2(odd, c, d), pick2(odd, a, b)),
            pick2(high, pick2(odd, d, c), pick2(odd, b, a)),
        ]
    )


def scatter_fsdp(parts, *hold):
    size = lax.axis_size("fsdp")
    if size & (size - 1):
        return lax.psum_scatter(parts, "fsdp", scatter_dimension=0).astype(f32)
    me = lax.axis_index("fsdp")
    take = lambda i: lax.dynamic_index_in_dim(parts, i, 0, False)
    got = [
        lax.ppermute(take(me ^ turn), "fsdp", [(i, i ^ turn) for i in range(size)])
        for turn in range(1, size)
    ]
    if hold:
        got = lax.optimization_barrier((*got, *hold))[: size - 1]
    return sum([g.astype(f32) for g in got], take(me).astype(f32))


def flip(value, step):
    size = lax.axis_size("tensor")
    return lax.ppermute(value, "tensor", [(i, i ^ step) for i in range(size)])


def start_sum(part, groups):
    rows, R = part.shape
    tp, ctx = lax.axis_size("tensor"), lax.axis_size("context")
    if not paired() or tp & (tp - 1):
        return lax.psum(part, ("tensor", "context")), []
    place = lax.axis_index("context")
    part = jnp.moveaxis(part.reshape(groups, ctx, rows // groups // ctx, R), 1, 0)
    other = swap_cores(lax.dynamic_index_in_dim(part, 1 - place, 0, False).astype(bf16))
    total = lax.dynamic_index_in_dim(part, place, 0, False) + other.astype(f32)
    sent = total.astype(bf16)
    return total, [flip(sent, step) for step in range(1, tp)]


def end_sum(begun, rows, out_type, *meanwhile):
    total, got = begun
    R = total.shape[-1]
    for piece in got:
        total = total + after(piece, *meanwhile).astype(f32)
    total = total.astype(out_type)
    if got:
        total = jnp.moveaxis(jnp.stack(in_order(total, swap_cores(total))), 0, 1)
    return total.reshape(rows, R)


def sum_parts(parts, groups, fillers):
    rows, R = parts[0].shape
    tp, ctx = lax.axis_size("tensor"), lax.axis_size("context")
    if not paired() or tp & (tp - 1):
        fillers(0, parts[0])
        return [lax.psum(part, ("tensor", "context")) for part in parts]
    place = lax.axis_index("context")
    part = jnp.stack(
        [jnp.moveaxis(p.reshape(groups, ctx, rows // groups // ctx, R), 1, 0) for p in parts], 1
    )
    other = swap_cores(lax.dynamic_index_in_dim(part, 1 - place, 0, False).astype(bf16))
    total = lax.dynamic_index_in_dim(part, place, 0, False) + other.astype(f32)
    step = 1
    while step < tp:
        got = flip(total.astype(bf16), step)
        total = total + after(got, *fillers(step, total)).astype(f32)
        step *= 2
    both = in_order(total, swap_cores(total))
    return [jnp.stack([b[i] for b in both], axis=1).reshape(rows, R) for i in range(len(parts))]


def on_device(
    x_in,
    teacher,
    segments,
    valid,
    norm_gain,
    w_in,
    conv_w,
    conv_b,
    x_proj,
    dt_w,
    dt_bias,
    a_log,
    d_skip,
    w_out,
):
    groups, blocklen, width = x_in.shape
    nf, ctx, tp = (lax.axis_size(name) for name in ("fsdp", "context", "tensor"))
    place = lax.axis_index("context")
    rows_here, _, chans_tensor = w_in.shape
    piece = conv_w.shape[1] // ctx
    chans = nf * piece
    taps, rank_dim, nstate = conv_w.shape[0], dt_w.shape[0], a_log.shape[0]
    proj_dim = x_proj.shape[0]
    share = width // tp
    cols_here = w_out.shape[1]
    full = blocklen * ctx
    tokens = groups * full
    part = full // CHUNKS
    sub = part // ctx
    rows = groups * part
    order = range(CHUNKS)
    first_col = lax.axis_index("tensor") * share

    def by_chunks(value):
        if paired():
            return in_order(value, swap_cores(value))
        value = jnp.moveaxis(lax.all_gather(value, "context"), 0, 1)
        value = value.reshape((groups, CHUNKS, part) + value.shape[3:])
        return [value[:, c] for c in order]

    def mine(value):
        value = value.reshape((groups, ctx, sub) + value.shape[2:])
        return lax.dynamic_index_in_dim(value, place, 1, False)

    def to_work(value):
        if not paired():
            return [mine(v) for v in by_chunks(value)]
        value = value.reshape((groups, CHUNKS, sub) + value.shape[2:])
        got = swap_cores(lax.dynamic_index_in_dim(value, 1 - place, 1, False))
        return in_order(lax.dynamic_index_in_dim(value, place, 1, False), got)

    def from_work(values):
        if not paired():
            stacked = jnp.moveaxis(lax.all_gather(jnp.stack(values), "context"), 2, 0)
            stacked = jnp.swapaxes(stacked, 1, 2).reshape((groups, full) + values[0].shape[2:])
            return lax.dynamic_slice_in_dim(stacked, place * blocklen, blocklen, 1)
        keep, sent = in_order(values[0], values[1])
        return jnp.concatenate(in_order(keep, swap_cores(sent)), axis=1)

    if paired():
        x_own, x_other = (v.reshape(rows, width) for v in (x_in, swap_cores(x_in)))
        columns = in_order(*(lax.dynamic_slice_in_dim(v, first_col, share, 1) for v in (x_own, x_other)))
    else:
        x_chunks = [v.reshape(rows, width) for v in by_chunks(x_in)]
        columns = [lax.dynamic_slice_in_dim(v, first_col, share, 1) for v in x_chunks]
    x_shares = [mine(v.reshape(groups, part, share)) for v in columns]
    if not paired():
        *x_shares, x_chunks[0] = lax.optimization_barrier((*x_shares, x_chunks[0]))
    marks_in = jnp.stack([segments, valid], axis=-1)
    marks_in = jnp.concatenate(by_chunks(marks_in), axis=1)
    seg = marks_in[..., 0]
    valid_all = marks_in[..., 1].astype(f32)
    count = sum_over(jnp.sum(valid_all).reshape(1, 1), "fsdp")
    masks = []
    for back in range(taps):
        same = seg[:, back:] == seg[:, : full - back]
        masks.append(jnp.pad(same, ((0, 0), (back, 0)), constant_values=False))
    masks = jnp.stack(masks, axis=-1).astype(f32)
    masks = [masks[:, c * part : (c + 1) * part].reshape(rows, taps) for c in order]
    keeps = [m[:, 1:2] for m in masks]

    wx_own, wz_own = pick(place, w_in, nf, ctx)
    small = jnp.concatenate(
        [x_proj, dt_w, a_log, conv_w, conv_b[None], dt_bias[None], d_skip[None]], axis=0
    )
    nsmall = small.shape[0]
    small = lax.dynamic_slice_in_dim(small, place * piece, piece, 1)
    gain_rows = norm_gain.reshape(-1, piece)
    spare = -(nsmall + gain_rows.shape[0]) % 32
    small = jnp.concatenate([small, gain_rows, jnp.zeros((spare, piece), bf16)], axis=0)
    small = lax.all_gather(after(small, wx_own), "fsdp")
    gain_all = small[:, nsmall : nsmall + gain_rows.shape[0]].reshape(width).astype(f32)
    small = jnp.swapaxes(small[:, :nsmall], 0, 1).reshape(nsmall, chans)
    ends = [0]
    for size in (proj_dim, rank_dim, nstate, taps, 1, 1, 1):
        ends.append(ends[-1] + size)
    xp, dtw, alog, cw, cb, dtb, skip = (small[a:b] for a, b in zip(ends[:-1], ends[1:]))
    cw, cb, skip, dtb = (v.astype(f32) for v in (cw, cb, skip, dtb))
    rates = -jnp.exp(alog.astype(f32))
    a2 = rates * LOG2E
    me, wx_pieces = gather_fsdp(wx_own)
    wz = lax.all_gather(after(wz_own, *wx_pieces), "fsdp", axis=0, tiled=True)
    wout_own = lax.dynamic_index_in_dim(
        w_out.reshape(nf, ctx, piece, cols_here), place, 1, False
    ).reshape(chans, cols_here)
    wout = lax.all_gather(after(wout_own, *wx_pieces), "fsdp")
    wout_t = jnp.swapaxes(wout, 1, 2).reshape(width, chans)
    if nf != tp:
        wout = jnp.swapaxes(wout_t.T.reshape(chans, tp, share), 0, 1)
    win_t = jnp.concatenate([stacked(me, wx_pieces).reshape(width, chans), wz], axis=1)
    win_t = jnp.swapaxes(win_t.reshape(tp, share, 2 * chans), 1, 2)

    bxs, xcs, us, zs, parts, normeds, scales = [], [], [], [], [], [], []
    tail = jnp.zeros((groups * SUB, chans), f32)
    for c in order:
        if paired():
            source = (place == c).astype(jnp.int32), x_own, x_other
        else:
            source = jnp.ones((), jnp.int32), x_chunks[c], x_chunks[c]
        normed, scale, bx, xc, u, proj_part, tail = conv_in(
            groups, me, *source, gain_all[None], wx_pieces, masks[c], cw, cb, xp, tail
        )
        normeds.append(normed)
        scales.append(scale.reshape(groups, part, 1))
        bxs.append(bx)
        xcs.append(xc)
        us.append(u)
        parts.append(proj_part)

    def fillers(step, total):
        c = step // 2
        if c < CHUNKS and len(zs) == c:
            zs.append(jnp.dot(after(normeds[c], total), wz, preferred_element_type=f32))
            return (zs[c],)
        return ()

    projs = sum_parts(parts, groups, fillers)
    for c in range(len(zs), CHUNKS):
        zs.append(jnp.dot(normeds[c], wz, preferred_element_type=f32))

    slot_own = place.reshape(1).astype(jnp.int32)
    slot_other = 1 - slot_own

    def to_shares(value, w):
        value = jnp.moveaxis(value.reshape(groups, ctx, sub, -1), 1, 0).reshape(ctx, groups * sub, -1)
        if paired():
            first = spread(slot_other, value, w)
            total = spread(slot_own, value, w, swap_cores(first))
        else:
            first = total = spread(jnp.zeros((1,), jnp.int32), value.reshape(1, ctx * groups * sub, -1), w)
            total = jnp.moveaxis(total.reshape(tp, ctx, groups * sub, share), 1, 0)
            total = lax.psum_scatter(total, "context", scatter_dimension=0)
        summed = lax.psum_scatter(total, "tensor", scatter_dimension=0)
        return first, total, summed.reshape(groups, sub, share)

    gateds, ys, deltas, states, ranks, bcs = [], [], [], [], [], []
    outs, grad_outs, losses = [], [], []
    targets = to_work(lax.dynamic_slice_in_dim(teacher, first_col, share, 2))
    state = jnp.zeros((groups * nstate, chans), f32)
    for c in order:
        proj = projs[c]
        ranks.append(proj[:, :rank_dim].astype(bf16))
        bcs.append(proj[:, rank_dim:])
        u = us[c] if c == 0 else after(us[c], sent)
        gated, y, delta, h, state = scan_fwd(
            groups, bcs[c], ranks[c], u, zs[c], keeps[c], dtw, dtb, a2, skip, state
        )
        deltas.append(delta)
        gateds.append(gated)
        ys.append(y)
        states.append(h)
        _, sent, branch = to_shares(gated, wout)
        outs.append(x_shares[c].astype(f32) + branch.astype(f32))
        errors = outs[c] - targets[c].astype(f32)
        live = mine(valid_all[:, c * part : (c + 1) * part])[..., None]
        losses.append(jnp.sum(live * errors * errors))
        grad_outs.append((tokens * nf / count[0, 0]) * live * errors)
    loss_value = sum_over(sum(losses).reshape(1, 1), "context", "tensor", "fsdp")[0, 0]
    loss_value = loss_value / width / count[0, 0]
    out_share = from_work(outs)

    late = jnp.zeros((groups * nstate, chans), f32)
    late_conv = jnp.zeros((groups * (taps - 1) * SUB, chans), f32)
    grad_inputs, alongs = [None] * CHUNKS, [None] * CHUNKS
    turn = (((0,), (0,)), ((), ()))
    gwout = gwz = gwx = 0.0
    grads = 0.0
    lows = [None] * CHUNKS
    for c in reversed(order):
        low = grad_outs[c].astype(bf16).reshape(groups * sub, share)
        if c < CHUNKS - 1:
            low = after(low, lows[c + 1])
        lows[c] = lax.all_gather(low, "tensor")

    def grad_gated(c, low):
        gated = jnp.moveaxis(gateds[c].reshape(groups, ctx, sub, chans), 1, 0)
        gated = gated.reshape(ctx, groups * sub, chans)
        if paired():
            other = swap_cores(low)
            gg = collect(slot_own, low, other, wout_t)
            pairs = [
                (lax.dynamic_index_in_dim(gated, place, 0, False), low),
                (lax.dynamic_index_in_dim(gated, 1 - place, 0, False), other),
            ]
        else:
            low = jnp.moveaxis(lax.all_gather(low, "context"), 0, 1).reshape(tp, rows, share)
            gg = jnp.einsum(
                "ztj,zcj->tc", low, wout, preferred_element_type=f32
            ).reshape(ctx, groups * sub, chans)
            pairs = [(gated.reshape(rows, chans), low)]
        gg = jnp.moveaxis(gg.reshape(ctx, groups, sub, chans), 0, 1).reshape(rows, chans)
        return gg, pairs

    gg, pairs = grad_gated(CHUNKS - 1, after(lows[-1], out_share, loss_value, wout_t, win_t))
    for c in reversed(order):
        gz, gpl, gu, grank, gb, gc, late, ga, gdtw, gvec = scan_bwd(
            groups, bcs[c], ranks[c], us[c], zs[c], keeps[c], ys[c], deltas[c], gg, states[c],
            dtw, a2, skip, state, late,
        )
        state = states[c].reshape(groups, part * nstate, chans)[:, :nstate].reshape(-1, chans)
        gproj = jnp.concatenate(
            [grank, gb[0].reshape(rows, nstate), gc[0].reshape(rows, nstate)], axis=1
        )
        gproj = start_sum(gproj, groups)
        summed = gproj[0]
        if c < CHUNKS - 1:
            summed, grad_inputs[c + 1] = lax.optimization_barrier((summed, grad_inputs[c + 1]))
        if c:
            gg_next, pairs_next = grad_gated(c - 1, after(lows[c - 1], summed))
            if c == 1:
                pairs = pairs + pairs_next
        for left, right in pairs if c else []:
            left = after(left, summed)
            gwout += jnp.einsum("tc,ztj->zcj", left, right, preferred_element_type=f32)
        gwz += lax.dot_general(normeds[c], after(gz, summed), turn, preferred_element_type=f32)
        if c < CHUNKS - 1:
            gm = after(gm, summed)
            gwx += lax.dot_general(
                normeds[c + 1], gm[:, :chans], turn, preferred_element_type=f32
            )
        if c:
            gg, pairs = gg_next, pairs_next
            fillers = [gwz, gg]
        else:
            fillers = [gwz, gwx]
        gproj = end_sum(gproj, rows, bf16, *fillers)
        gm, along, late_conv, gconv, gxp = conv_out(
            groups, gu, gproj, xp, xcs[c], bxs[c], zs[c], gz, us[c], masks[c], cw, late_conv
        )
        first, sent, grad_normed = to_shares(gm, win_t)
        if c:
            gg = after(gg, sent)
        grads += jnp.concatenate(
            [gxp, gdtw, ga * LN2, gconv, gvec], axis=0
        )
        alongs[c] = along[0]
        grad_inputs[c] = grad_normed
    gwx += lax.dot_general(
        normeds[0], after(gm, first)[:, :chans], turn, preferred_element_type=f32
    )

    grads = after(grads, sent)
    gwout = jnp.swapaxes(gwout, 0, 1).reshape(chans, nf, cols_here)
    gwout = jnp.swapaxes(gwout, 0, 1).astype(bf16)
    gwz = gwz.astype(bf16).reshape(nf, rows_here, chans)
    gwout, gwz = (lax.psum_scatter(v, "fsdp", scatter_dimension=0) for v in (gwout, gwz))
    gwout, gwz = (v.astype(f32) for v in lax.optimization_barrier((gwout, gwz, sent))[:2])
    gwz_other, gwout_other = (swap_cores(v) if paired() else None for v in (gwz, gwout))
    gwx = scatter_fsdp(gwx.astype(bf16).reshape(nf, rows_here, chans), sent)
    gain_part = jnp.sum(gwx * wx_own.astype(f32) + gwz * wz_own.astype(f32), axis=1)
    sums = sum_over(jnp.concatenate([gain_part] + alongs)[None], "context", "tensor")[0]
    grad_gain = sums[:rows_here] / norm_gain.astype(f32)
    gain_share = lax.dynamic_slice_in_dim(gain_all, first_col, share, 0)
    fixed, factors = [], []
    for c in order:
        along = sums[rows_here + c * rows : rows_here + (c + 1) * rows].reshape(groups, part)
        scale = mine(scales[c])
        fixed.append(
            grad_outs[c]
            - x_shares[c].astype(f32) * (scale * scale * (mine(along)[..., None] / width))
        )
        factors.append(scale * gain_share)
    nrows = grads.shape[0]
    grads = jnp.swapaxes(grads.reshape(nrows, nf, piece), 0, 1)
    grads = scatter_fsdp(grads)
    grads = jnp.swapaxes(gather_context(grads), 0, 1).reshape(nrows, ctx * piece)
    xp_g, dtw_g, alog_g = (grads[a:b] for a, b in zip(ends[:3], ends[1:4]))
    cw_g = grads[ends[3] : ends[4]]
    cb_g = grads[ends[4]]
    dtb_g, skip_g = grads[ends[3] + SUB], grads[ends[3] + SUB + 1]
    if paired() and piece % 128 == 0:
        win_g = put(place, gwx, swap_cores(gwx), gwz, gwz_other, nf)
    else:
        win_g = jnp.stack(
            [
                jnp.moveaxis(gather_context(g).reshape(ctx, rows_here, nf, piece), 0, 2).reshape(
                    rows_here, chans_tensor
                )
                for g in (gwx, gwz)
            ],
            axis=1,
        )
    wout_g = jnp.stack(in_order(gwout, gwout_other)) if paired() else gather_context(gwout)
    wout_g = jnp.swapaxes(wout_g.reshape(ctx, nf, piece, cols_here), 0, 1).reshape(
        chans_tensor, cols_here
    )
    done = (grad_gain, win_g, grads, wout_g)
    got = [grad_inputs[c] if c else after(grad_inputs[c], *done) for c in order]
    grad_share = from_work([f + k * g.astype(f32) for f, k, g in zip(fixed, factors, got)])
    return (
        out_share,
        loss_value,
        grad_share,
        grad_gain,
        win_g,
        cw_g,
        cb_g,
        xp_g,
        dtw_g,
        dtb_g,
        alog_g,
        skip_g,
        wout_g,
    )


def solution(mesh):
    return jax.shard_map(
        on_device,
        mesh=mesh,
        in_specs=(
            P("fsdp", "context", None),
            P("fsdp", "context", None),
            P("fsdp", "context"),
            P("fsdp", "context"),
            P("fsdp"),
            P("fsdp", None, "tensor"),
            P(None, ("tensor", "fsdp")),
            P(("tensor", "fsdp")),
            P(None, ("tensor", "fsdp")),
            P(None, ("tensor", "fsdp")),
            P(("tensor", "fsdp")),
            P(None, ("tensor", "fsdp")),
            P(("tensor", "fsdp")),
            P("tensor", "fsdp"),
        ),
        out_specs=(
            P("fsdp", "context", "tensor"),
            P(),
            P("fsdp", "context", "tensor"),
            P("fsdp"),
            P("fsdp", None, "tensor"),
            P(None, ("tensor", "fsdp")),
            P(("tensor", "fsdp")),
            P(None, ("tensor", "fsdp")),
            P(None, ("tensor", "fsdp")),
            P(("tensor", "fsdp")),
            P(None, ("tensor", "fsdp")),
            P(("tensor", "fsdp")),
            P("tensor", "fsdp"),
        ),
        check_vma=False,
    )
```

```python
import functools

import jax
import jax.numpy as jnp
from jax import lax
from jax.experimental import pallas as pl
from jax.experimental.pallas import tpu as pltpu
from jax.sharding import PartitionSpec as P

f32 = jnp.float32
bf16 = jnp.bfloat16
eps = 1e-05
LOG2E = 1.4426950408889634
LN2 = 0.6931471805599453
FAR = 1e30
SUB = 8
CHUNKS = 2
SCAN_BLOCK = 128
CONV_BLOCK = 256


def pick_block(total, most):
    size = min(total, most)
    while total % size:
        size //= 2
    return size


def whole(shape):
    return pl.BlockSpec(shape, lambda *_: (0,) * len(shape))


def params(*semantics):
    return pltpu.CompilerParams(dimension_semantics=semantics or None)


def cost(flops, arrays, exps=0):
    moved = sum(a.size * a.dtype.itemsize for a in arrays)
    return pl.CostEstimate(flops=int(flops), bytes_accessed=int(moved), transcendentals=int(exps))


def softplus(v):
    tail = jnp.exp(-jnp.abs(v))
    small = tail * (1.0 - tail * (0.5 - tail * (1.0 / 3.0)))
    return jnp.maximum(v, 0.0) + jnp.where(tail < 0.0078125, small, jnp.log(1.0 + tail))


def sigmoid(v):
    return 0.5 * jnp.tanh(0.5 * v) + 0.5


def fold_rows(parts, row):
    half = 1
    while len(parts) > 1:
        low = (row & half) == 0
        parts = [
            jnp.where(low, a, b) + pltpu.roll(jnp.where(low, b, a), half, 0)
            for a, b in zip(parts[0::2], parts[1::2])
        ]
        half *= 2
    return parts[0]


def tiles_of(ref, base, w):
    return [ref[pl.ds(base, SUB), g * w : (g + 1) * w] for g in range(ref.shape[1] // w)]


def row_of(tile, r):
    return jnp.broadcast_to(tile[r : r + 1, :], tile.shape)


UNROLL = 8


def put_columns(ref, values, wide_s, rows_s):
    TB, count = values.shape
    w = ref.shape[1]
    high = values.astype(bf16).astype(f32)
    wide_s[:, 0:count] = high
    wide_s[:, count : 2 * count] = values - high
    wide_s[:, 2 * count :] = jnp.zeros((TB, 128 - 2 * count), f32)
    row = lax.broadcasted_iota(jnp.int32, (SUB, 128), 0)
    lane = lax.broadcasted_iota(jnp.int32, (SUB, 128), 1)
    tiles = count // SUB
    picks = [(lane == row + SUB * i) | (lane == row + SUB * i + count) for i in range(tiles)]
    for t in range(0, TB, 2):
        pair = [jnp.broadcast_to(wide_s[t + d : t + d + 1, :], (SUB, 128)) for d in range(2)]
        for i in range(tiles):
            both = jnp.concatenate([jnp.where(picks[i], v, 0.0) for v in pair], axis=0)
            rows_s[(i * TB + t) * SUB : (i * TB + t + 2) * SUB, :] = both.astype(bf16)
    ones = jnp.ones((128, w), bf16)
    for i in range(tiles):
        block = slice(i * TB * SUB, (i + 1) * TB * SUB)
        ref[block, :] = jnp.dot(rows_s[block, :], ones, preferred_element_type=f32)


def merge_pair(even, odd, low):
    half = SUB // 2
    return jnp.where(low, even, odd) + pltpu.roll(jnp.where(low, odd, even), half, 0)


def row_sums(ref, TB, NG):
    half = SUB // 2
    columns = []
    for g in range(NG):
        parts = [ref[pl.ds(g * TB * half + s, TB, stride=half), :] for s in range(half)]
        while len(parts) > 1:
            parts = [a + b for a, b in zip(parts[0::2], parts[1::2])]
        columns.append(parts[0])
    return jnp.concatenate(columns, axis=1) if NG > 1 else columns[0]


def at_row(t, scale, offset=0):
    return pl.ds(pl.multiple_of(t * scale + offset, SUB), SUB)


def scan_fwd_kernel(
    proj_ref, u_ref, z_ref, keep_ref, dtw_ref, dtb_ref, a2_ref, skip_ref, start_ref, *refs
):
    gated_ref, y_ref, delta_ref, h_ref, last_ref, dec_s, du_s, p_s, bc_s, wide_s, rows_s = refs[-11:]
    TB, C = u_ref.shape
    N = a2_ref.shape[0]
    w = min(128, C)
    NG, NI = C // w, N // SUB

    @pl.when(pl.program_id(1) == 0)
    def _():
        last_ref[...] = start_ref[...]

    rank = proj_ref[:, 0 : dtw_ref.shape[0]].astype(bf16)
    put_columns(bc_s, proj_ref[:, dtw_ref.shape[0] :], wide_s, rows_s)
    delta = softplus(
        jnp.dot(rank, dtw_ref[...], preferred_element_type=f32) + dtb_ref[...]
    )
    delta_ref[...] = delta
    du_s[...] = delta * u_ref[...].astype(f32)
    dec_s[...] = jnp.where(keep_ref[...] > 0.5, delta, FAR)
    part = lambda ref: [
        [ref[SUB * i : SUB * (i + 1), g * w : (g + 1) * w] for g in range(NG)] for i in range(NI)
    ]
    a2 = part(a2_ref)

    low = lax.broadcasted_iota(jnp.int32, (SUB, w), 0) < SUB // 2

    def body(j, h):
        h = [list(r) for r in h]
        before = [None] * NG
        base = pl.multiple_of(j * UNROLL, SUB)
        dls, dus = tiles_of(dec_s, base, w), tiles_of(du_s, base, w)
        for r in range(UNROLL):
            t = base + r
            bv = [bc_s[at_row(t, SUB, i * TB * SUB), :] for i in range(NI)]
            cv = [bc_s[at_row(t, SUB, (NI + i) * TB * SUB), :] for i in range(NI)]
            for g in range(NG):
                dl, du = row_of(dls[g], r), row_of(dus[g], r)
                p = None
                for i in range(NI):
                    h_ref[at_row(t, N, SUB * i), g * w : (g + 1) * w] = h[i][g]
                    h[i][g] = jnp.exp2(dl * a2[i][g]) * h[i][g] + bv[i] * du
                    q = cv[i] * h[i][g]
                    p = q if p is None else p + q
                if r % 2 == 0:
                    before[g] = p
                else:
                    rows = at_row(base, SUB // 2, (r // 2) * SUB + g * TB * SUB // 2)
                    p_s[rows, :] = merge_pair(before[g], p, low)
        return tuple(tuple(r) for r in h)

    h = lax.fori_loop(0, TB // UNROLL, body, tuple(tuple(r) for r in part(last_ref)))
    for i in range(NI):
        for g in range(NG):
            last_ref[SUB * i : SUB * (i + 1), g * w : (g + 1) * w] = h[i][g]
    y = row_sums(p_s, TB, NG) + skip_ref[...] * u_ref[...].astype(f32)
    y_ref[...] = y
    z = z_ref[...]
    gated_ref[...] = (y * z * sigmoid(z)).astype(bf16)


def scan_fwd(groups, proj, u, z, keep, dtw, dtb, a2, skip, start, *first):
    rows, C = u.shape
    N, R = a2.shape[0], dtw.shape[0]
    w = min(128, C)
    TB = pick_block(rows // groups, SCAN_BLOCK)
    nb = rows // groups // TB
    blk = lambda s, n=TB: pl.BlockSpec((n, s), lambda g, b: (g * nb + b, 0))
    own = pl.BlockSpec((N, C), lambda g, b: (g, 0))
    sd = jax.ShapeDtypeStruct
    outs = [
        sd((rows, C), bf16), sd((rows, C), f32), sd((rows, C), f32), sd((rows * N, C), f32),
        sd((groups * N, C), f32),
    ]
    return pl.pallas_call(
        scan_fwd_kernel,
        name="scan_fwd",
        grid=(groups, nb),
        in_specs=[
            blk(R + 2 * N), blk(C), blk(C), blk(1),
            whole(dtw.shape), whole(dtb.shape), whole(a2.shape), whole(skip.shape),
            own,
        ]
        + [pl.BlockSpec(memory_space=pl.ANY)] * len(first),
        out_specs=[blk(C), blk(C), blk(C), blk(C, TB * N), own],
        out_shape=outs,
        scratch_shapes=[pltpu.VMEM((TB, C), f32)] * 2
        + [pltpu.VMEM((TB * (C // w) * SUB // 2, w), f32), pltpu.VMEM((TB * 2 * N, w), f32)]
        + [pltpu.VMEM((TB, 128), f32), pltpu.VMEM((TB * 2 * N, 128), bf16)],
        compiler_params=params("arbitrary", "arbitrary"),
        cost_estimate=cost(rows * C * N * 8, outs, rows * C * N),
    )(proj, u, z, keep, dtw, dtb, a2, skip, start, *first)


def scan_bwd_kernel(
    proj_ref, u_ref, z_ref, keep_ref, y_ref, delta_ref, gg_ref, h_ref,
    dtw_ref, a2_ref, skip_ref, end_ref, late_ref,
    gz_ref, gpl_ref, gu_ref, grank_ref, gb_ref, gc_ref, first_ref, ga_ref, gdtw_ref, gvec_ref,
    dec_s, du_s, gy_s, r_s, s2_s, bc_s, mb_s, mc_s, next_s, wide_s, rows_s,
):
    TB, C = u_ref.shape
    N = a2_ref.shape[0]
    w = min(128, C)
    NG, NI = C // w, N // SUB
    b = pl.program_id(1)

    @pl.when((b == 0) & (pl.program_id(0) == 0))
    def _():
        ga_ref[...] = jnp.zeros_like(ga_ref)
        gdtw_ref[...] = jnp.zeros_like(gdtw_ref)
        gvec_ref[...] = jnp.zeros_like(gvec_ref)

    @pl.when(b == 0)
    def _():
        first_ref[...] = late_ref[...]
        next_s[...] = end_ref[...]

    rank = proj_ref[:, 0 : dtw_ref.shape[0]].astype(bf16)
    put_columns(bc_s, proj_ref[:, dtw_ref.shape[0] :], wide_s, rows_s)
    delta = delta_ref[...]
    u = u_ref[...].astype(f32)
    du_s[...] = delta * u
    dec_s[...] = jnp.where(keep_ref[...] > 0.5, delta, FAR)
    z = z_ref[...]
    sg = sigmoid(z)
    gg = gg_ref[...]
    gy = gg * z * sg
    gy_s[...] = gy
    gz_ref[...] = (gg * y_ref[...] * sg * (1.0 + z * (1.0 - sg))).astype(bf16)
    gvec_ref[1:2, :] += jnp.sum(gy * u, axis=0, keepdims=True)
    part = lambda ref: [
        [ref[SUB * i : SUB * (i + 1), g * w : (g + 1) * w] for g in range(NG)] for i in range(NI)
    ]
    a2 = part(a2_ref)

    low = lax.broadcasted_iota(jnp.int32, (SUB, w), 0) < SUB // 2

    def body(j, carry):
        later = [None] * NG
        dlam, ga, h_now = ([list(r) for r in rows] for rows in carry)
        base = pl.multiple_of(TB - UNROLL - j * UNROLL, SUB)
        dls, dus, gys = tiles_of(dec_s, base, w), tiles_of(du_s, base, w), tiles_of(gy_s, base, w)
        for r in reversed(range(UNROLL)):
            t = base + r
            bv = [bc_s[at_row(t, SUB, i * TB * SUB), :] for i in range(NI)]
            cv = [bc_s[at_row(t, SUB, (NI + i) * TB * SUB), :] for i in range(NI)]
            mb, mc = [None] * NI, [None] * NI
            for g in range(NG):
                dl, du, gyr = row_of(dls[g], r), row_of(dus[g], r), row_of(gys[g], r)
                p, s2 = None, None
                for i in range(NI):
                    h_prev = h_ref[at_row(t, N, SUB * i), g * w : (g + 1) * w]
                    lam = cv[i] * gyr + dlam[i][g]
                    e = dl * a2[i][g]
                    dlam[i][g] = jnp.exp2(e) * lam
                    q = e * (dlam[i][g] * h_prev)
                    p = q if p is None else p + q
                    ga[i][g] = ga[i][g] + q
                    x = lam * bv[i]
                    s2 = x if s2 is None else s2 + x
                    x = lam * du
                    mb[i] = x if mb[i] is None else mb[i] + x
                    x = gyr * h_now[i][g]
                    mc[i] = x if mc[i] is None else mc[i] + x
                    h_now[i][g] = h_prev
                if r % 2:
                    later[g] = (p, s2)
                else:
                    rows = at_row(base, SUB // 2, (r // 2) * SUB + g * TB * SUB // 2)
                    r_s[rows, :] = merge_pair(p, later[g][0], low)
                    s2_s[rows, :] = merge_pair(s2, later[g][1], low)
            for i in range(NI):
                mb_s[at_row(t, N, SUB * i), :] = mb[i]
                mc_s[at_row(t, N, SUB * i), :] = mc[i]
        return tuple(tuple(tuple(r) for r in rows) for rows in (dlam, ga, h_now))

    carry = tuple(tuple(tuple(r) for r in part(ref)) for ref in (first_ref, ga_ref, next_s))
    for ref, rows in zip(
        (first_ref, ga_ref, next_s), lax.fori_loop(0, TB // UNROLL, body, carry)
    ):
        for i in range(NI):
            for g in range(NG):
                ref[SUB * i : SUB * (i + 1), g * w : (g + 1) * w] = rows[i][g]
    ones = jnp.ones((SUB, w), bf16)
    for s, ref in ((mb_s, gb_ref), (mc_s, gc_ref)):
        ref[...] = lax.dot_general(
            ones, s[...].astype(bf16), (((1,), (1,)), ((), ())), preferred_element_type=f32
        )
    s2 = row_sums(s2_s, TB, NG)
    ratio = jnp.where(
        delta < 0.0625,
        1.0 - delta * (0.5 - delta * (1.0 / 6.0 - delta * (1.0 / 24.0 - delta * (1.0 / 120.0)))),
        (1.0 - jnp.exp(-delta)) / jnp.maximum(delta, 0.0625),
    )
    gpre = ratio * (row_sums(r_s, TB, NG) * LN2 + du_s[...] * s2)
    low = gpre.astype(bf16)
    gpl_ref[...] = low
    gu_ref[...] = gy_s[...] * skip_ref[...] + delta * s2
    grank_ref[...] = lax.dot_general(
        low, dtw_ref[...], (((1,), (1,)), ((), ())), preferred_element_type=f32
    )
    gdtw_ref[...] += lax.dot_general(
        rank, low, (((0,), (0,)), ((), ())), preferred_element_type=f32
    )
    gvec_ref[0:1, :] += jnp.sum(gpre, axis=0, keepdims=True)


def scan_bwd(groups, proj, u, z, keep, y, delta, gg, h, dtw, a2, skip, end, late):
    rows, C = u.shape
    N, R = a2.shape[0], dtw.shape[0]
    w = min(128, C)
    TB = pick_block(rows // groups, SCAN_BLOCK)
    nb = rows // groups // TB
    where = lambda g, b: g * nb + nb - 1 - b
    blk = lambda s, n=TB: pl.BlockSpec((n, s), lambda g, b: (where(g, b), 0))
    own = pl.BlockSpec((N, C), lambda g, b: (g, 0))
    across = pl.BlockSpec((SUB, TB * N), lambda g, b: (0, where(g, b)))
    sd = jax.ShapeDtypeStruct
    outs = [
        sd((rows, C), bf16), sd((rows, C), bf16), sd((rows, C), f32), sd((rows, R), f32),
        sd((SUB, rows * N), f32), sd((SUB, rows * N), f32), sd((groups * N, C), f32),
        sd((N, C), f32), sd((R, C), f32), sd((8, C), f32),
    ]
    fold = pltpu.VMEM((TB * (C // w) * SUB // 2, w), f32)
    return pl.pallas_call(
        scan_bwd_kernel,
        name="scan_bwd",
        grid=(groups, nb),
        in_specs=[
            blk(R + 2 * N), blk(C), blk(C), blk(1), blk(C), blk(C), blk(C), blk(C, TB * N),
            whole(dtw.shape), whole(a2.shape), whole(skip.shape), own, own,
        ],
        out_specs=[
            blk(C), blk(C), blk(C), blk(R), across, across, own,
            whole((N, C)), whole((R, C)), whole((8, C)),
        ],
        out_shape=outs,
        scratch_shapes=[pltpu.VMEM((TB, C), f32)] * 3
        + [fold] * 2
        + [pltpu.VMEM((TB * 2 * N, w), f32)]
        + [pltpu.VMEM((TB * N, w), f32)] * 2
        + [pltpu.VMEM((N, C), f32)]
        + [pltpu.VMEM((TB, 128), f32), pltpu.VMEM((TB * 2 * N, 128), bf16)],
        compiler_params=params("arbitrary", "arbitrary"),
        cost_estimate=cost(rows * C * N * 20, outs + [h], rows * C * N),
    )(proj, u, z, keep, y, delta, gg, h, dtw, a2, skip, end, late)


def pick_kernel(slot_ref, w_ref, x_ref, z_ref):
    x_ref[...] = w_ref[:, 0, :]
    z_ref[...] = w_ref[:, 1, :]


def pick(place, w_in, pieces, ctx):
    rows, _, total = w_in.shape
    piece = total // pieces // ctx
    if piece % 128:
        own = lax.dynamic_index_in_dim(
            w_in.reshape(rows, 2, pieces, ctx, piece), place, 3, False
        ).reshape(rows, 2, pieces * piece)
        return own[:, 0], own[:, 1]
    out = jax.ShapeDtypeStruct((rows, pieces * piece), w_in.dtype)
    spec = pl.BlockSpec((rows, piece), lambda f, s: (0, f))
    return pl.pallas_call(
        pick_kernel,
        name="pick",
        grid_spec=pltpu.PrefetchScalarGridSpec(
            num_scalar_prefetch=1,
            grid=(pieces,),
            in_specs=[pl.BlockSpec((rows, 2, piece), lambda f, s: (0, 0, f * ctx + s[0]))],
            out_specs=[spec, spec],
        ),
        out_shape=[out, out],
        compiler_params=params("arbitrary"),
        cost_estimate=cost(0, [out, out, out, out]),
    )(place.reshape(1).astype(jnp.int32), w_in)


def put_kernel(slot_ref, xa_ref, xb_ref, za_ref, zb_ref, o_ref):
    first = slot_ref[0] == 0
    piece = o_ref.shape[2] // 2
    for branch, (own, other) in enumerate(((xa_ref, xb_ref), (za_ref, zb_ref))):
        a, b = own[...], other[...]
        o_ref[:, branch, 0:piece] = jnp.where(first, a, b)
        o_ref[:, branch, piece:] = jnp.where(first, b, a)


def put(place, x_own, x_other, z_own, z_other, pieces):
    rows, C = x_own.shape
    piece = C // pieces
    TB = pick_block(rows, 256)
    spec = pl.BlockSpec((TB, piece), lambda b, f, s: (b, f))
    out = jax.ShapeDtypeStruct((rows, 2, 2 * C), x_own.dtype)
    return pl.pallas_call(
        put_kernel,
        name="put",
        grid_spec=pltpu.PrefetchScalarGridSpec(
            num_scalar_prefetch=1,
            grid=(rows // TB, pieces),
            in_specs=[spec] * 4,
            out_specs=pl.BlockSpec((TB, 2, 2 * piece), lambda b, f, s: (b, 0, f)),
        ),
        out_shape=out,
        compiler_params=params("arbitrary", "arbitrary"),
        cost_estimate=cost(0, [out, out]),
    )(place.reshape(1).astype(jnp.int32), x_own, x_other, z_own, z_other)


def conv_in_kernel(
    place_ref, own_ref, other_ref, gain_ref, mask_ref, cw_ref, cb_ref, xp_ref, halo_ref, *refs
):
    pieces, outs = refs[:-8], refs[-8:]
    norm_ref, scale_ref, bx_ref, xc_ref, u_ref, proj_ref, tail_ref, ext_s = outs
    TB, C = u_ref.shape
    taps = cw_ref.shape[0]

    @pl.when(pl.program_id(1) == 0)
    def _():
        ext_s[0:SUB, :] = halo_ref[...]

    x = jnp.where(place_ref[1] == 1, own_ref[...], other_ref[...]).astype(f32)
    scale = lax.rsqrt(jnp.mean(x * x, axis=1, keepdims=True) + eps)
    scale_ref[...] = scale
    norm_ref[...] = (x * scale * gain_ref[...]).astype(bf16)
    bx = 0.0
    for turn, w_ref in enumerate(pieces):
        deep = w_ref.shape[0]
        first = pl.multiple_of((place_ref[0] ^ turn) * deep, deep)
        bx += jnp.dot(norm_ref[:, pl.ds(first, deep)], w_ref[...], preferred_element_type=f32)
    bx_ref[...] = bx
    ext_s[SUB:, :] = bx
    total = cb_ref[...] + cw_ref[taps - 1 : taps, :] * bx
    for tap in range(taps - 1):
        back = taps - 1 - tap
        total += cw_ref[tap : tap + 1, :] * (
            ext_s[SUB - back : SUB - back + TB, :] * mask_ref[:, back : back + 1]
        )
    xc_ref[...] = total
    u = (total * sigmoid(total)).astype(bf16)
    u_ref[...] = u
    proj_ref[...] = lax.dot_general(
        u, xp_ref[...], (((1,), (1,)), ((), ())), preferred_element_type=f32
    )
    ext_s[0:SUB, :] = bx[TB - SUB :, :]
    tail_ref[...] = bx[TB - SUB :, :]


def conv_in(groups, me, use_own, own, other, gain, pieces, masks, cw, cb, xp, halo):
    rows, D = own.shape
    C = pieces[0].shape[1]
    TB = pick_block(rows // groups, CONV_BLOCK)
    nb = rows // groups // TB
    blk = lambda s: pl.BlockSpec((TB, s), lambda g, b, _: (g * nb + b, 0))
    mine = pl.BlockSpec((SUB, C), lambda g, b, _: (g, 0))
    sd = jax.ShapeDtypeStruct
    R = xp.shape[0]
    outs = [
        sd((rows, D), bf16), sd((rows, 1), f32), sd((rows, C), f32), sd((rows, C), f32),
        sd((rows, C), bf16), sd((rows, R), f32), sd((groups * SUB, C), f32),
    ]
    return pl.pallas_call(
        conv_in_kernel,
        name="conv_in",
        grid_spec=pltpu.PrefetchScalarGridSpec(
            num_scalar_prefetch=1,
            grid=(groups, nb),
            in_specs=[
                pl.BlockSpec((TB, D), lambda g, b, p: ((g * nb + b) * p[1], 0)),
                pl.BlockSpec((TB, D), lambda g, b, p: ((g * nb + b) * (1 - p[1]), 0)),
                whole(gain.shape), blk(masks.shape[1]), whole(cw.shape), whole(cb.shape),
                whole(xp.shape), mine,
            ]
            + [whole(p.shape) for p in pieces],
            out_specs=[blk(D), blk(1), blk(C), blk(C), blk(C), blk(R), mine],
            scratch_shapes=[pltpu.VMEM((TB + SUB, C), f32)],
        ),
        out_shape=outs,
        compiler_params=params("arbitrary", "arbitrary"),
        cost_estimate=cost(2 * rows * D * C, outs + [own], rows * C),
    )(jnp.stack([me, use_own]).astype(jnp.int32), own, other, gain, masks, cw, cb, xp, halo, *pieces)


def conv_out_kernel(
    gu_ref, gp_ref, xp_ref, xc_ref, bx_ref, z_ref, gz_ref, u_ref, mask_ref, cw_ref, late_ref,
    gm_ref, along_ref, early_ref, gconv_ref, gxp_ref,
    *ext_s,
):
    TB, C = u_ref.shape
    taps = cw_ref.shape[0]

    @pl.when((pl.program_id(1) == 0) & (pl.program_id(0) == 0))
    def _():
        gconv_ref[...] = jnp.zeros_like(gconv_ref)
        gxp_ref[...] = jnp.zeros_like(gxp_ref)

    @pl.when(pl.program_id(1) == 0)
    def _():
        for back in range(1, taps):
            ext_s[back - 1][TB:, :] = late_ref[(back - 1) * SUB : back * SUB, :]

    gp = gp_ref[...]
    xc = xc_ref[...]
    sg = sigmoid(xc)
    inner = gu_ref[...] + jnp.dot(gp, xp_ref[...], preferred_element_type=f32)
    gxc = inner * (sg * (1.0 + xc * (1.0 - sg)))
    bx = bx_ref[...]
    gx = cw_ref[taps - 1 : taps, :] * gxc
    gconv_ref[taps - 1 : taps, :] += jnp.sum(gxc * bx, axis=0, keepdims=True)
    gconv_ref[taps : taps + 1, :] += jnp.sum(gxc, axis=0, keepdims=True)
    for back in range(1, taps):
        tap = taps - 1 - back
        ext = ext_s[back - 1]
        reached = gxc * mask_ref[:, back : back + 1]
        ext[0:TB, :] = reached
        moved = ext[back : back + TB, :]
        gx += cw_ref[tap : tap + 1, :] * moved
        gconv_ref[tap : tap + 1, :] += jnp.sum(moved * bx, axis=0, keepdims=True)
        ext[TB:, :] = reached[0:SUB, :]
        early_ref[(back - 1) * SUB : back * SUB, :] = reached[0:SUB, :]
    gz = gz_ref[...]
    gx = gx.astype(bf16)
    gm_ref[:, 0:C] = gx
    gm_ref[:, C:] = gz
    terms = (gx.astype(f32) * bx + gz.astype(f32) * z_ref[...]).astype(bf16)
    along_ref[...] = lax.dot_general(
        jnp.ones((SUB, C), bf16), terms, (((1,), (1,)), ((), ())), preferred_element_type=f32
    )
    gxp_ref[...] += lax.dot_general(
        gp, u_ref[...], (((0,), (0,)), ((), ())), preferred_element_type=f32
    )


def conv_out(groups, gu, gp, xp, xc, bx, z, gz, u, masks, cw, late):
    rows, C = u.shape
    taps = cw.shape[0]
    R = xp.shape[0]
    TB = pick_block(rows // groups, CONV_BLOCK)
    nb = rows // groups // TB
    blk = lambda s: pl.BlockSpec((TB, s), lambda g, b: (g * nb + nb - 1 - b, 0))
    own = pl.BlockSpec(((taps - 1) * SUB, C), lambda g, b: (g, 0))
    sd = jax.ShapeDtypeStruct
    outs = [
        sd((rows, 2 * C), bf16), sd((SUB, rows), f32), sd((groups * (taps - 1) * SUB, C), f32),
        sd((8, C), f32), sd((R, C), f32),
    ]
    return pl.pallas_call(
        conv_out_kernel,
        name="conv_out",
        grid=(groups, nb),
        in_specs=[
            blk(C), blk(R), whole(xp.shape), blk(C), blk(C), blk(C), blk(C), blk(C),
            blk(masks.shape[1]), whole(cw.shape), own,
        ],
        out_specs=[
            blk(2 * C),
            pl.BlockSpec((SUB, TB), lambda g, b: (0, g * nb + nb - 1 - b)),
            own,
            whole((8, C)),
            whole((R, C)),
        ],
        out_shape=outs,
        scratch_shapes=[pltpu.VMEM((TB + SUB, C), f32)] * (taps - 1),
        compiler_params=params("arbitrary", "arbitrary"),
        cost_estimate=cost(4 * rows * R * C, outs + [gu, xc, bx, z], rows * C),
    )(gu, gp, xp, xc, bx, z, gz, u, masks, cw, late)


def spread_kernel(slot_ref, x_ref, w_ref, *refs, adding):
    o_ref = refs[-1]
    for z in range(o_ref.shape[0]):
        total = jnp.dot(x_ref[0], w_ref[z], preferred_element_type=f32)
        if adding:
            total = total + refs[0][z].astype(f32)
        o_ref[z] = total.astype(bf16)


def spread(slot, x, w, added=(), first=()):
    _, rows, K = x.shape
    shares, _, share = w.shape
    per = 2 if shares % 2 == 0 and rows * share <= 512 * 512 else 1
    out = jax.ShapeDtypeStruct((shares, rows, share), bf16)
    block = pl.BlockSpec((per, rows, share), lambda z, s: (z, 0, 0))
    return pl.pallas_call(
        functools.partial(spread_kernel, adding=len(added)),
        name="spread",
        grid_spec=pltpu.PrefetchScalarGridSpec(
            num_scalar_prefetch=1,
            grid=(shares // per,),
            in_specs=[
                pl.BlockSpec((1, rows, K), lambda z, s: (s[0], 0, 0)),
                pl.BlockSpec((per, K, share), lambda z, s: (z, 0, 0)),
            ]
            + [block] * len(added)
            + [pl.BlockSpec(memory_space=pl.ANY)] * len(first),
            out_specs=block,
        ),
        out_shape=out,
        compiler_params=params("arbitrary"),
        cost_estimate=cost(2 * rows * K * shares * share, [out, x, w]),
    )(slot, x, w, *added, *first)


def collect_kernel(slot_ref, own_ref, other_ref, w_ref, o_ref):
    shares, _, share = own_ref.shape

    def product(ref):
        total = jnp.dot(ref[0], w_ref[0:share, :], preferred_element_type=f32)
        for z in range(1, shares):
            total += jnp.dot(
                ref[z], w_ref[z * share : (z + 1) * share, :], preferred_element_type=f32
            )
        o_ref[0] = total

    @pl.when(pl.program_id(0) == 0)
    def _():
        product(own_ref)

    @pl.when(pl.program_id(0) == 1)
    def _():
        product(other_ref)


def collect(slot, own, other, w):
    shares, rows, share = own.shape
    C = w.shape[1]
    out = jax.ShapeDtypeStruct((2, rows, C), f32)
    return pl.pallas_call(
        collect_kernel,
        name="collect",
        grid_spec=pltpu.PrefetchScalarGridSpec(
            num_scalar_prefetch=1,
            grid=(2,),
            in_specs=[
                pl.BlockSpec(own.shape, lambda s, p: (0, 0, 0)),
                pl.BlockSpec(own.shape, lambda s, p: (0, 0, 0)),
                pl.BlockSpec(w.shape, lambda s, p: (0, 0)),
            ],
            out_specs=pl.BlockSpec((1, rows, C), lambda s, p: (s + p[0] - 2 * s * p[0], 0, 0)),
        ),
        out_shape=out,
        compiler_params=params("arbitrary"),
        cost_estimate=cost(4 * rows * C * share * shares, [out, own, other, w]),
    )(slot, own, other, w)


def after(value, *others):
    return lax.optimization_barrier((value,) + others)[0]


def swap_cores(value):
    return lax.ppermute(value, "context", [(0, 1), (1, 0)])


def paired():
    return lax.axis_size("context") == 2


def in_order(own, other):
    first = lax.axis_index("context") == 0
    return jnp.where(first, own, other), jnp.where(first, other, own)


def gather_context(value):
    if not paired():
        return lax.all_gather(value, "context")
    return jnp.stack(in_order(value, swap_cores(value)))


def sum_over(value, *axes):
    for axis in axes:
        size, step = lax.axis_size(axis), 1
        if size & (size - 1):
            value = lax.psum(value, axis)
            continue
        while step < size:
            value = value + lax.ppermute(value, axis, [(i, i ^ step) for i in range(size)])
            step *= 2
    return value


ROW = [(0, 1), (1, 0), (2, 3), (3, 2)]
COLUMN = [(0, 2), (2, 0), (1, 3), (3, 1)]


def gather_fsdp(value, *hold):
    size = lax.axis_size("fsdp")
    if size != 4 or value.shape[0] % 2:
        pieces = lax.all_gather(value, "fsdp")
        return jnp.zeros((), jnp.int32), [pieces[i] for i in range(size)]
    half = value.shape[0] // 2
    row = lax.ppermute(value, "fsdp", ROW)
    column = lax.ppermute(value, "fsdp", COLUMN)
    if hold:
        row, column = lax.optimization_barrier((row, column) + hold)[:2]
    far = jnp.concatenate(
        [lax.ppermute(row[:half], "fsdp", COLUMN), lax.ppermute(column[half:], "fsdp", ROW)]
    )
    return lax.axis_index("fsdp"), [value, row, column, far]


def stacked(me, pieces):
    if len(pieces) != 4:
        return jnp.stack(pieces)
    a, b, c, d = pieces
    odd, high = me % 2 == 1, me // 2 == 1
    pick2 = lambda flag, x, y: jnp.where(flag, y, x)
    return jnp.stack(
        [
            pick2(high, pick2(odd, a, b), pick2(odd, c, d)),
            pick2(high, pick2(odd, b, a), pick2(odd, d, c)),
            pick2(high, pick2(odd, c, d), pick2(odd, a, b)),
            pick2(high, pick2(odd, d, c), pick2(odd, b, a)),
        ]
    )


def scatter_fsdp(parts, *hold):
    size = lax.axis_size("fsdp")
    if size & (size - 1):
        return lax.psum_scatter(parts, "fsdp", scatter_dimension=0).astype(f32)
    me = lax.axis_index("fsdp")
    take = lambda i: lax.dynamic_index_in_dim(parts, i, 0, False)
    got = [
        lax.ppermute(take(me ^ turn), "fsdp", [(i, i ^ turn) for i in range(size)])
        for turn in range(1, size)
    ]
    if hold:
        got = lax.optimization_barrier((*got, *hold))[: size - 1]
    return sum([g.astype(f32) for g in got], take(me).astype(f32))


def flip(value, step):
    size = lax.axis_size("tensor")
    return lax.ppermute(value, "tensor", [(i, i ^ step) for i in range(size)])


def start_sum(part, groups):
    rows, R = part.shape
    tp, ctx = lax.axis_size("tensor"), lax.axis_size("context")
    if not paired() or tp & (tp - 1):
        return lax.psum(part, ("tensor", "context")), []
    place = lax.axis_index("context")
    part = jnp.moveaxis(part.reshape(groups, ctx, rows // groups // ctx, R), 1, 0)
    other = swap_cores(lax.dynamic_index_in_dim(part, 1 - place, 0, False).astype(bf16))
    total = lax.dynamic_index_in_dim(part, place, 0, False) + other.astype(f32)
    sent = total.astype(bf16)
    return total, [flip(sent, step) for step in range(1, tp)]


def end_sum(begun, rows, out_type, *meanwhile):
    total, got = begun
    R = total.shape[-1]
    for piece in got:
        total = total + after(piece, *meanwhile).astype(f32)
    total = total.astype(out_type)
    if got:
        total = jnp.moveaxis(jnp.stack(in_order(total, swap_cores(total))), 0, 1)
    return total.reshape(rows, R)


def sum_parts(parts, groups, fillers):
    rows, R = parts[0].shape
    tp, ctx = lax.axis_size("tensor"), lax.axis_size("context")
    if not paired() or tp & (tp - 1):
        fillers(0, parts[0])
        return [lax.psum(part, ("tensor", "context")) for part in parts]
    place = lax.axis_index("context")
    part = jnp.stack(
        [jnp.moveaxis(p.reshape(groups, ctx, rows // groups // ctx, R), 1, 0) for p in parts], 1
    )
    other = swap_cores(lax.dynamic_index_in_dim(part, 1 - place, 0, False).astype(bf16))
    total = lax.dynamic_index_in_dim(part, place, 0, False) + other.astype(f32)
    step = 1
    while step < tp:
        got = flip(total.astype(bf16), step)
        total = total + after(got, *fillers(step, total)).astype(f32)
        step *= 2
    both = in_order(total, swap_cores(total))
    return [jnp.stack([b[i] for b in both], axis=1).reshape(rows, R) for i in range(len(parts))]


def on_device(
    x_in,
    teacher,
    segments,
    valid,
    norm_gain,
    w_in,
    conv_w,
    conv_b,
    x_proj,
    dt_w,
    dt_bias,
    a_log,
    d_skip,
    w_out,
):
    groups, blocklen, width = x_in.shape
    nf, ctx, tp = (lax.axis_size(name) for name in ("fsdp", "context", "tensor"))
    place = lax.axis_index("context")
    rows_here, _, chans_tensor = w_in.shape
    piece = conv_w.shape[1] // ctx
    chans = nf * piece
    taps, rank_dim, nstate = conv_w.shape[0], dt_w.shape[0], a_log.shape[0]
    proj_dim = x_proj.shape[0]
    share = width // tp
    cols_here = w_out.shape[1]
    full = blocklen * ctx
    tokens = groups * full
    part = full // CHUNKS
    sub = part // ctx
    rows = groups * part
    order = range(CHUNKS)
    first_col = lax.axis_index("tensor") * share

    def by_chunks(value):
        if paired():
            return in_order(value, swap_cores(value))
        value = jnp.moveaxis(lax.all_gather(value, "context"), 0, 1)
        value = value.reshape((groups, CHUNKS, part) + value.shape[3:])
        return [value[:, c] for c in order]

    def mine(value):
        value = value.reshape((groups, ctx, sub) + value.shape[2:])
        return lax.dynamic_index_in_dim(value, place, 1, False)

    def to_work(value):
        if not paired():
            return [mine(v) for v in by_chunks(value)]
        value = value.reshape((groups, CHUNKS, sub) + value.shape[2:])
        got = swap_cores(lax.dynamic_index_in_dim(value, 1 - place, 1, False))
        return in_order(lax.dynamic_index_in_dim(value, place, 1, False), got)

    def from_work(values):
        if not paired():
            stacked = jnp.moveaxis(lax.all_gather(jnp.stack(values), "context"), 2, 0)
            stacked = jnp.swapaxes(stacked, 1, 2).reshape((groups, full) + values[0].shape[2:])
            return lax.dynamic_slice_in_dim(stacked, place * blocklen, blocklen, 1)
        keep, sent = in_order(values[0], values[1])
        return jnp.concatenate(in_order(keep, swap_cores(sent)), axis=1)

    if paired():
        x_own, x_other = (v.reshape(rows, width) for v in (x_in, swap_cores(x_in)))
        columns = in_order(*(lax.dynamic_slice_in_dim(v, first_col, share, 1) for v in (x_own, x_other)))
    else:
        x_chunks = [v.reshape(rows, width) for v in by_chunks(x_in)]
        columns = [lax.dynamic_slice_in_dim(v, first_col, share, 1) for v in x_chunks]
    x_shares = [mine(v.reshape(groups, part, share)) for v in columns]
    if not paired():
        *x_shares, x_chunks[0] = lax.optimization_barrier((*x_shares, x_chunks[0]))
    marks_in = jnp.stack([segments, valid], axis=-1)
    marks_in = jnp.concatenate(by_chunks(marks_in), axis=1)
    seg = marks_in[..., 0]
    valid_all = marks_in[..., 1].astype(f32)
    count = sum_over(jnp.sum(valid_all).reshape(1, 1), "fsdp")
    masks = []
    for back in range(taps):
        same = seg[:, back:] == seg[:, : full - back]
        masks.append(jnp.pad(same, ((0, 0), (back, 0)), constant_values=False))
    masks = jnp.stack(masks, axis=-1).astype(f32)
    masks = [masks[:, c * part : (c + 1) * part].reshape(rows, taps) for c in order]
    keeps = [m[:, 1:2] for m in masks]

    wx_own, wz_own = pick(place, w_in, nf, ctx)
    small = jnp.concatenate(
        [x_proj, dt_w, a_log, conv_w, conv_b[None], dt_bias[None], d_skip[None]], axis=0
    )
    nsmall = small.shape[0]
    small = lax.dynamic_slice_in_dim(small, place * piece, piece, 1)
    gain_rows = norm_gain.reshape(-1, piece)
    spare = -(nsmall + gain_rows.shape[0]) % 32
    small = jnp.concatenate([small, gain_rows, jnp.zeros((spare, piece), bf16)], axis=0)
    small = lax.all_gather(after(small, wx_own), "fsdp")
    gain_all = small[:, nsmall : nsmall + gain_rows.shape[0]].reshape(width).astype(f32)
    small = jnp.swapaxes(small[:, :nsmall], 0, 1).reshape(nsmall, chans)
    ends = [0]
    for size in (proj_dim, rank_dim, nstate, taps, 1, 1, 1):
        ends.append(ends[-1] + size)
    xp, dtw, alog, cw, cb, dtb, skip = (small[a:b] for a, b in zip(ends[:-1], ends[1:]))
    cw, cb, skip, dtb = (v.astype(f32) for v in (cw, cb, skip, dtb))
    rates = -jnp.exp(alog.astype(f32))
    a2 = rates * LOG2E
    me, wx_pieces = gather_fsdp(wx_own)
    wz = lax.all_gather(after(wz_own, *wx_pieces), "fsdp", axis=0, tiled=True)
    wout_own = lax.dynamic_index_in_dim(
        w_out.reshape(nf, ctx, piece, cols_here), place, 1, False
    ).reshape(chans, cols_here)
    wout = lax.all_gather(after(wout_own, *wx_pieces), "fsdp")
    wout_t = jnp.swapaxes(wout, 1, 2).reshape(width, chans)
    if nf != tp:
        wout = jnp.swapaxes(wout_t.T.reshape(chans, tp, share), 0, 1)
    win_t = jnp.concatenate([stacked(me, wx_pieces).reshape(width, chans), wz], axis=1)
    win_t = jnp.swapaxes(win_t.reshape(tp, share, 2 * chans), 1, 2)

    bxs, xcs, us, zs, parts, normeds, scales = [], [], [], [], [], [], []
    tail = jnp.zeros((groups * SUB, chans), f32)
    for c in order:
        if paired():
            source = (place == c).astype(jnp.int32), x_own, x_other
        else:
            source = jnp.ones((), jnp.int32), x_chunks[c], x_chunks[c]
        normed, scale, bx, xc, u, proj_part, tail = conv_in(
            groups, me, *source, gain_all[None], wx_pieces, masks[c], cw, cb, xp, tail
        )
        normeds.append(normed)
        scales.append(scale.reshape(groups, part, 1))
        bxs.append(bx)
        xcs.append(xc)
        us.append(u)
        parts.append(proj_part)

    def fillers(step, total):
        c = step // 2
        if c < CHUNKS and len(zs) == c:
            zs.append(jnp.dot(after(normeds[c], total), wz, preferred_element_type=f32))
            return (zs[c],)
        return ()

    projs = sum_parts(parts, groups, fillers)
    for c in range(len(zs), CHUNKS):
        zs.append(jnp.dot(normeds[c], wz, preferred_element_type=f32))

    slot_own = place.reshape(1).astype(jnp.int32)
    slot_other = 1 - slot_own

    def to_shares(value, w, between=None):
        value = jnp.moveaxis(value.reshape(groups, ctx, sub, -1), 1, 0).reshape(ctx, groups * sub, -1)
        if paired():
            send = spread(slot_other, value, w)
            first = [between(send)] if between else []
            total = spread(slot_own, value, w, [swap_cores(send)], first)
        else:
            first = [between(value)] if between else []
            total = spread(jnp.zeros((1,), jnp.int32), value.reshape(1, ctx * groups * sub, -1), w)
            total = jnp.moveaxis(total.reshape(tp, ctx, groups * sub, share), 1, 0)
            total = lax.psum_scatter(total, "context", scatter_dimension=0)
        summed = lax.psum_scatter(total, "tensor", scatter_dimension=0)
        return first, total, summed.reshape(groups, sub, share)

    gateds, ys, deltas, states = [], [], [], []
    outs, grad_outs, losses = [], [], []
    targets = to_work(lax.dynamic_slice_in_dim(teacher, first_col, share, 2))
    state = jnp.zeros((groups * nstate, chans), f32)
    for c in order:
        u = us[c] if c == 0 else after(us[c], sent)
        gated, y, delta, h, state = scan_fwd(
            groups, projs[c], u, zs[c], keeps[c], dtw, dtb, a2, skip, state
        )
        deltas.append(delta)
        gateds.append(gated)
        ys.append(y)
        states.append(h)
        _, sent, branch = to_shares(gated, wout)
        outs.append(x_shares[c].astype(f32) + branch.astype(f32))
        errors = outs[c] - targets[c].astype(f32)
        live = mine(valid_all[:, c * part : (c + 1) * part])[..., None]
        losses.append(jnp.sum(live * errors * errors))
        grad_outs.append((tokens * nf / count[0, 0]) * live * errors)
    loss_value = sum_over(sum(losses).reshape(1, 1), "context", "tensor", "fsdp")[0, 0]
    loss_value = loss_value / width / count[0, 0]
    out_share = from_work(outs)

    late = jnp.zeros((groups * nstate, chans), f32)
    late_conv = jnp.zeros((groups * (taps - 1) * SUB, chans), f32)
    grad_inputs, alongs = [None] * CHUNKS, [None] * CHUNKS
    turn = (((0,), (0,)), ((), ()))
    gwout = gwz = gwx = 0.0
    grads = 0.0
    lows = [None] * CHUNKS
    for c in reversed(order):
        low = grad_outs[c].astype(bf16).reshape(groups * sub, share)
        if c < CHUNKS - 1:
            low = after(low, lows[c + 1])
        lows[c] = lax.all_gather(low, "tensor")

    gated_parts = []
    for gated in gateds if paired() else []:
        gated = jnp.moveaxis(gated.reshape(groups, ctx, sub, chans), 1, 0)
        gated = gated.reshape(ctx, groups * sub, chans)
        gated_parts.append(
            [lax.dynamic_index_in_dim(gated, i, 0, False) for i in (place, 1 - place)]
        )

    def grad_gated(c, low):
        if paired():
            other = swap_cores(low)
            gg = collect(slot_own, low, other, wout_t)
            pairs = list(zip(gated_parts[c], (low, other)))
        else:
            low = jnp.moveaxis(lax.all_gather(low, "context"), 0, 1).reshape(tp, rows, share)
            gg = jnp.einsum(
                "ztj,zcj->tc", low, wout, preferred_element_type=f32
            ).reshape(ctx, groups * sub, chans)
            gated = jnp.moveaxis(gateds[c].reshape(groups, ctx, sub, chans), 1, 0)
            pairs = [(gated.reshape(rows, chans), low)]
        gg = jnp.moveaxis(gg.reshape(ctx, groups, sub, chans), 0, 1).reshape(rows, chans)
        return gg, pairs

    last, *gated_parts = lax.optimization_barrier(
        (lows[-1], *gated_parts, out_share, loss_value, wout_t, win_t)
    )[: 1 + len(gated_parts)]
    gg, pairs = grad_gated(CHUNKS - 1, last)
    for c in reversed(order):
        gz, gpl, gu, grank, gb, gc, late, ga, gdtw, gvec = scan_bwd(
            groups, projs[c], us[c], zs[c], keeps[c], ys[c], deltas[c], gg, states[c],
            dtw, a2, skip, state, late,
        )
        state = states[c].reshape(groups, part * nstate, chans)[:, :nstate].reshape(-1, chans)
        gproj = jnp.concatenate(
            [grank, gb[0].reshape(rows, nstate), gc[0].reshape(rows, nstate)], axis=1
        )
        gproj = start_sum(gproj, groups)
        summed = gproj[0]
        if c < CHUNKS - 1:
            summed, grad_inputs[c + 1] = lax.optimization_barrier((summed, grad_inputs[c + 1]))
        if c:
            gg_next, pairs_next = grad_gated(c - 1, after(lows[c - 1], summed))
            if c == 1:
                pairs = pairs + pairs_next
        for left, right in pairs if c else []:
            left = after(left, summed)
            gwout += jnp.einsum("tc,ztj->zcj", left, right, preferred_element_type=f32)
        gwz += lax.dot_general(normeds[c], after(gz, summed), turn, preferred_element_type=f32)
        if c < CHUNKS - 1:
            gm = after(gm, summed)
            gwx += lax.dot_general(
                normeds[c + 1], gm[:, :chans], turn, preferred_element_type=f32
            )
        if c:
            gg, pairs = gg_next, pairs_next
            fillers = [gwz, gg, gwout]
        else:
            if paired():
                gwout = after(gwout, summed)
            wout_g = gather_context(gwout.astype(f32))
            wout_g = jnp.swapaxes(wout_g.reshape(ctx, nf, piece, cols_here), 0, 1).reshape(
                chans_tensor, cols_here
            )
            fillers = [gwz, gwx, wout_g] if paired() else []
        gproj = end_sum(gproj, rows, bf16, *fillers)
        gm, along, late_conv, gconv, gxp = conv_out(
            groups, gu, gproj, xp, xcs[c], bxs[c], zs[c], gz, us[c], masks[c], cw, late_conv
        )
        def grad_wx(token):
            return gwx + lax.dot_general(
                normeds[0], after(gm, token)[:, :chans], turn, preferred_element_type=f32
            )

        first, sent, grad_normed = to_shares(gm, win_t, None if c else grad_wx)
        if not c:
            gwx = first[0]
            gconv, gxp, along = lax.optimization_barrier((gconv, gxp, along, sent))[:3]
        if c == 1:
            gwout = jnp.swapaxes(gwout, 0, 1).reshape(chans, nf, cols_here)
            gwout = jnp.swapaxes(gwout, 0, 1).astype(bf16)
            gwout = lax.psum_scatter(gwout, "fsdp", scatter_dimension=0)
        if c:
            gg = after(gg, sent, gwout) if paired() else gg
        grads += jnp.concatenate(
            [gxp, gdtw, ga * LN2, gconv, gvec], axis=0
        )
        alongs[c] = along[0]
        grad_inputs[c] = grad_normed
    grads = after(grads, sent)
    gwz = lax.psum_scatter(
        gwz.astype(bf16).reshape(nf, rows_here, chans), "fsdp", scatter_dimension=0
    )
    gwz = after(gwz, sent).astype(f32)
    gwz_other = swap_cores(gwz) if paired() else None
    sums = sum_over(jnp.concatenate(alongs)[None], "context", "tensor")[0]
    gwx = scatter_fsdp(gwx.astype(bf16).reshape(nf, rows_here, chans), sent, sums)
    gain_part = jnp.sum(gwx * wx_own.astype(f32) + gwz * wz_own.astype(f32), axis=1)
    gain_share = lax.dynamic_slice_in_dim(gain_all, first_col, share, 0)
    fixed, factors = [], []
    for c in order:
        along = sums[c * rows : (c + 1) * rows].reshape(groups, part)
        scale = mine(scales[c])
        fixed.append(
            grad_outs[c]
            - x_shares[c].astype(f32) * (scale * scale * (mine(along)[..., None] / width))
        )
        factors.append(scale * gain_share)
    nrows = grads.shape[0]
    grads = jnp.swapaxes(grads.reshape(nrows, nf, piece), 0, 1)
    grads = scatter_fsdp(grads)
    grads = jnp.swapaxes(gather_context(grads), 0, 1).reshape(nrows, ctx * piece)
    xp_g, dtw_g, alog_g = (grads[a:b] for a, b in zip(ends[:3], ends[1:4]))
    cw_g = grads[ends[3] : ends[4]]
    cb_g = grads[ends[4]]
    dtb_g, skip_g = grads[ends[3] + SUB], grads[ends[3] + SUB + 1]
    if paired() and piece % 128 == 0:
        win_g = put(place, gwx, swap_cores(gwx), gwz, gwz_other, nf)
    else:
        win_g = jnp.stack(
            [
                jnp.moveaxis(gather_context(g).reshape(ctx, rows_here, nf, piece), 0, 2).reshape(
                    rows_here, chans_tensor
                )
                for g in (gwx, gwz)
            ],
            axis=1,
        )
    if paired():
        gain_part = after(gain_part, win_g)
    grad_gain = sum_over(gain_part[None], "context", "tensor")[0] / norm_gain.astype(f32)
    done = (grads, win_g, *fixed)
    got = [grad_inputs[c] if c else after(grad_inputs[c], *done) for c in order]
    grad_share = from_work([f + k * g.astype(f32) for f, k, g in zip(fixed, factors, got)])
    return (
        out_share,
        loss_value,
        grad_share,
        grad_gain,
        win_g,
        cw_g,
        cb_g,
        xp_g,
        dtw_g,
        dtb_g,
        alog_g,
        skip_g,
        wout_g,
    )


def solution(mesh):
    return jax.shard_map(
        on_device,
        mesh=mesh,
        in_specs=(
            P("fsdp", "context", None),
            P("fsdp", "context", None),
            P("fsdp", "context"),
            P("fsdp", "context"),
            P("fsdp"),
            P("fsdp", None, "tensor"),
            P(None, ("tensor", "fsdp")),
            P(("tensor", "fsdp")),
            P(None, ("tensor", "fsdp")),
            P(None, ("tensor", "fsdp")),
            P(("tensor", "fsdp")),
            P(None, ("tensor", "fsdp")),
            P(("tensor", "fsdp")),
            P("tensor", "fsdp"),
        ),
        out_specs=(
            P("fsdp", "context", "tensor"),
            P(),
            P("fsdp", "context", "tensor"),
            P("fsdp"),
            P("fsdp", None, "tensor"),
            P(None, ("tensor", "fsdp")),
            P(("tensor", "fsdp")),
            P(None, ("tensor", "fsdp")),
            P(None, ("tensor", "fsdp")),
            P(("tensor", "fsdp")),
            P(None, ("tensor", "fsdp")),
            P(("tensor", "fsdp")),
            P("tensor", "fsdp"),
        ),
        check_vma=False,
    )
```

```python
import functools

import jax
import jax.numpy as jnp
from jax import lax
from jax.experimental import pallas as pl
from jax.experimental.pallas import tpu as pltpu
from jax.sharding import PartitionSpec as P

f32 = jnp.float32
bf16 = jnp.bfloat16
eps = 1e-05
LOG2E = 1.4426950408889634
LN2 = 0.6931471805599453
FAR = 1e30
SUB = 8
CHUNKS = 2
SCAN_BLOCK = 128
CONV_BLOCK = 256


def pick_block(total, most):
    size = min(total, most)
    while total % size:
        size //= 2
    return size


def whole(shape):
    return pl.BlockSpec(shape, lambda *_: (0,) * len(shape))


def params(*semantics):
    return pltpu.CompilerParams(dimension_semantics=semantics or None)


def cost(flops, arrays, exps=0):
    moved = sum(a.size * a.dtype.itemsize for a in arrays)
    return pl.CostEstimate(flops=int(flops), bytes_accessed=int(moved), transcendentals=int(exps))


def softplus(v):
    tail = jnp.exp(-jnp.abs(v))
    small = tail * (1.0 - tail * (0.5 - tail * (1.0 / 3.0)))
    return jnp.maximum(v, 0.0) + jnp.where(tail < 0.0078125, small, jnp.log(1.0 + tail))


def sigmoid(v):
    return 0.5 * jnp.tanh(0.5 * v) + 0.5


def fold_rows(parts, row):
    half = 1
    while len(parts) > 1:
        low = (row & half) == 0
        parts = [
            jnp.where(low, a, b) + pltpu.roll(jnp.where(low, b, a), half, 0)
            for a, b in zip(parts[0::2], parts[1::2])
        ]
        half *= 2
    return parts[0]


def tiles_of(ref, base, w):
    return [ref[pl.ds(base, SUB), g * w : (g + 1) * w] for g in range(ref.shape[1] // w)]


def row_of(tile, r):
    return jnp.broadcast_to(tile[r : r + 1, :], tile.shape)


UNROLL = 8


def put_columns(ref, values, wide_s, rows_s):
    TB, count = values.shape
    w = ref.shape[1]
    high = values.astype(bf16).astype(f32)
    wide_s[:, 0:count] = high
    wide_s[:, count : 2 * count] = values - high
    wide_s[:, 2 * count :] = jnp.zeros((TB, 128 - 2 * count), f32)
    row = lax.broadcasted_iota(jnp.int32, (SUB, 128), 0)
    lane = lax.broadcasted_iota(jnp.int32, (SUB, 128), 1)
    tiles = count // SUB
    picks = [(lane == row + SUB * i) | (lane == row + SUB * i + count) for i in range(tiles)]
    for t in range(0, TB, 2):
        pair = [jnp.broadcast_to(wide_s[t + d : t + d + 1, :], (SUB, 128)) for d in range(2)]
        for i in range(tiles):
            both = jnp.concatenate([jnp.where(picks[i], v, 0.0) for v in pair], axis=0)
            rows_s[(i * TB + t) * SUB : (i * TB + t + 2) * SUB, :] = both.astype(bf16)
    ones = jnp.ones((128, w), bf16)
    for i in range(tiles):
        block = slice(i * TB * SUB, (i + 1) * TB * SUB)
        ref[block, :] = jnp.dot(rows_s[block, :], ones, preferred_element_type=f32)


def merge_pair(even, odd, low):
    half = SUB // 2
    return jnp.where(low, even, odd) + pltpu.roll(jnp.where(low, odd, even), half, 0)


def row_sums(ref, TB, NG):
    half = SUB // 2
    columns = []
    for g in range(NG):
        parts = [ref[pl.ds(g * TB * half + s, TB, stride=half), :] for s in range(half)]
        while len(parts) > 1:
            parts = [a + b for a, b in zip(parts[0::2], parts[1::2])]
        columns.append(parts[0])
    return jnp.concatenate(columns, axis=1) if NG > 1 else columns[0]


def at_row(t, scale, offset=0):
    return pl.ds(pl.multiple_of(t * scale + offset, SUB), SUB)


def scan_fwd_kernel(
    proj_ref, u_ref, z_ref, mask_ref, dtw_ref, dtb_ref, a2_ref, skip_ref, start_ref, *refs
):
    gated_ref, y_ref, delta_ref, h_ref, last_ref, dec_s, du_s, p_s, bc_s, wide_s, rows_s = refs[-11:]
    TB, C = u_ref.shape
    N = a2_ref.shape[0]
    w = min(128, C)
    NG, NI = C // w, N // SUB

    @pl.when(pl.program_id(1) == 0)
    def _():
        last_ref[...] = start_ref[...]

    rank = proj_ref[0 : dtw_ref.shape[0], :].astype(bf16)
    put_columns(bc_s, proj_ref[dtw_ref.shape[0] :, :].T, wide_s, rows_s)
    delta = softplus(
        lax.dot_general(
            rank, dtw_ref[...], (((0,), (0,)), ((), ())), preferred_element_type=f32
        ) + dtb_ref[...]
    )
    delta_ref[...] = delta
    du_s[...] = delta * u_ref[...].astype(f32)
    dec_s[...] = jnp.where(mask_ref[:, 1:2] > 0.5, delta, FAR)
    part = lambda ref: [
        [ref[SUB * i : SUB * (i + 1), g * w : (g + 1) * w] for g in range(NG)] for i in range(NI)
    ]
    a2 = part(a2_ref)

    low = lax.broadcasted_iota(jnp.int32, (SUB, w), 0) < SUB // 2

    def body(j, h):
        h = [list(r) for r in h]
        before = [None] * NG
        base = pl.multiple_of(j * UNROLL, SUB)
        dls, dus = tiles_of(dec_s, base, w), tiles_of(du_s, base, w)
        for r in range(UNROLL):
            t = base + r
            bv = [bc_s[at_row(t, SUB, i * TB * SUB), :] for i in range(NI)]
            cv = [bc_s[at_row(t, SUB, (NI + i) * TB * SUB), :] for i in range(NI)]
            for g in range(NG):
                dl, du = row_of(dls[g], r), row_of(dus[g], r)
                p = None
                for i in range(NI):
                    h_ref[at_row(t, N, SUB * i), g * w : (g + 1) * w] = h[i][g]
                    h[i][g] = jnp.exp2(dl * a2[i][g]) * h[i][g] + bv[i] * du
                    q = cv[i] * h[i][g]
                    p = q if p is None else p + q
                if r % 2 == 0:
                    before[g] = p
                else:
                    rows = at_row(base, SUB // 2, (r // 2) * SUB + g * TB * SUB // 2)
                    p_s[rows, :] = merge_pair(before[g], p, low)
        return tuple(tuple(r) for r in h)

    h = lax.fori_loop(0, TB // UNROLL, body, tuple(tuple(r) for r in part(last_ref)))
    for i in range(NI):
        for g in range(NG):
            last_ref[SUB * i : SUB * (i + 1), g * w : (g + 1) * w] = h[i][g]
    y = row_sums(p_s, TB, NG) + skip_ref[...] * u_ref[...].astype(f32)
    y_ref[...] = y
    z = z_ref[...]
    gated_ref[...] = (y * z * sigmoid(z)).astype(bf16)


def scan_fwd(groups, proj, u, z, masks, dtw, dtb, a2, skip, start, *first):
    rows, C = u.shape
    N, R = a2.shape[0], dtw.shape[0]
    w = min(128, C)
    TB = pick_block(rows // groups, SCAN_BLOCK)
    nb = rows // groups // TB
    blk = lambda s, n=TB: pl.BlockSpec((n, s), lambda g, b: (g * nb + b, 0))
    own = pl.BlockSpec((N, C), lambda g, b: (g, 0))
    sd = jax.ShapeDtypeStruct
    outs = [
        sd((rows, C), bf16), sd((rows, C), f32), sd((rows, C), f32), sd((rows * N, C), f32),
        sd((groups * N, C), f32),
    ]
    return pl.pallas_call(
        scan_fwd_kernel,
        name="scan_fwd",
        grid=(groups, nb),
        in_specs=[
            pl.BlockSpec((R + 2 * N, TB), lambda g, b: (0, g * nb + b)), blk(C), blk(C), blk(masks.shape[1]),
            whole(dtw.shape), whole(dtb.shape), whole(a2.shape), whole(skip.shape),
            own,
        ]
        + [pl.BlockSpec(memory_space=pl.ANY)] * len(first),
        out_specs=[blk(C), blk(C), blk(C), blk(C, TB * N), own],
        out_shape=outs,
        scratch_shapes=[pltpu.VMEM((TB, C), f32)] * 2
        + [pltpu.VMEM((TB * (C // w) * SUB // 2, w), f32), pltpu.VMEM((TB * 2 * N, w), f32)]
        + [pltpu.VMEM((TB, 128), f32), pltpu.VMEM((TB * 2 * N, 128), bf16)],
        compiler_params=params("arbitrary", "arbitrary"),
        cost_estimate=cost(rows * C * N * 8, outs, rows * C * N),
    )(proj, u, z, masks, dtw, dtb, a2, skip, start, *first)


def scan_bwd_kernel(
    proj_ref, u_ref, z_ref, mask_ref, y_ref, delta_ref, gg_ref, h_ref,
    dtw_ref, a2_ref, skip_ref, places_ref, end_ref, late_ref,
    gz_ref, gu_ref, gproj_ref, first_ref, ga_ref, gdtw_ref, gvec_ref,
    dec_s, du_s, gy_s, r_s, s2_s, bc_s, mb_s, mc_s, next_s, wide_s, rows_s,
):
    TB, C = u_ref.shape
    N = a2_ref.shape[0]
    w = min(128, C)
    NG, NI = C // w, N // SUB
    b = pl.program_id(1)

    @pl.when((b == 0) & (pl.program_id(0) == 0))
    def _():
        ga_ref[...] = jnp.zeros_like(ga_ref)
        gdtw_ref[...] = jnp.zeros_like(gdtw_ref)
        gvec_ref[...] = jnp.zeros_like(gvec_ref)

    @pl.when(b == 0)
    def _():
        first_ref[...] = late_ref[...]
        next_s[...] = end_ref[...]

    rank = proj_ref[0 : dtw_ref.shape[0], :].astype(bf16)
    put_columns(bc_s, proj_ref[dtw_ref.shape[0] :, :].T, wide_s, rows_s)
    delta = delta_ref[...]
    u = u_ref[...].astype(f32)
    du_s[...] = delta * u
    dec_s[...] = jnp.where(mask_ref[:, 1:2] > 0.5, delta, FAR)
    z = z_ref[...]
    sg = sigmoid(z)
    gg = gg_ref[...]
    gy = gg * z * sg
    gy_s[...] = gy
    gz_ref[...] = (gg * y_ref[...] * sg * (1.0 + z * (1.0 - sg))).astype(bf16)
    gvec_ref[1:2, :] += jnp.sum(gy * u, axis=0, keepdims=True)
    part = lambda ref: [
        [ref[SUB * i : SUB * (i + 1), g * w : (g + 1) * w] for g in range(NG)] for i in range(NI)
    ]
    a2 = part(a2_ref)

    low = lax.broadcasted_iota(jnp.int32, (SUB, w), 0) < SUB // 2

    def body(j, carry):
        later = [None] * NG
        dlam, ga, h_now = ([list(r) for r in rows] for rows in carry)
        base = pl.multiple_of(TB - UNROLL - j * UNROLL, SUB)
        dls, dus, gys = tiles_of(dec_s, base, w), tiles_of(du_s, base, w), tiles_of(gy_s, base, w)
        for r in reversed(range(UNROLL)):
            t = base + r
            bv = [bc_s[at_row(t, SUB, i * TB * SUB), :] for i in range(NI)]
            cv = [bc_s[at_row(t, SUB, (NI + i) * TB * SUB), :] for i in range(NI)]
            mb, mc = [None] * NI, [None] * NI
            for g in range(NG):
                dl, du, gyr = row_of(dls[g], r), row_of(dus[g], r), row_of(gys[g], r)
                p, s2 = None, None
                for i in range(NI):
                    h_prev = h_ref[at_row(t, N, SUB * i), g * w : (g + 1) * w]
                    lam = cv[i] * gyr + dlam[i][g]
                    e = dl * a2[i][g]
                    dlam[i][g] = jnp.exp2(e) * lam
                    q = e * (dlam[i][g] * h_prev)
                    p = q if p is None else p + q
                    ga[i][g] = ga[i][g] + q
                    x = lam * bv[i]
                    s2 = x if s2 is None else s2 + x
                    x = lam * du
                    mb[i] = x if mb[i] is None else mb[i] + x
                    x = gyr * h_now[i][g]
                    mc[i] = x if mc[i] is None else mc[i] + x
                    h_now[i][g] = h_prev
                if r % 2:
                    later[g] = (p, s2)
                else:
                    rows = at_row(base, SUB // 2, (r // 2) * SUB + g * TB * SUB // 2)
                    r_s[rows, :] = merge_pair(p, later[g][0], low)
                    s2_s[rows, :] = merge_pair(s2, later[g][1], low)
            for i in range(NI):
                mb_s[at_row(t, N, SUB * i), :] = mb[i]
                mc_s[at_row(t, N, SUB * i), :] = mc[i]
        return tuple(tuple(tuple(r) for r in rows) for rows in (dlam, ga, h_now))

    carry = tuple(tuple(tuple(r) for r in part(ref)) for ref in (first_ref, ga_ref, next_s))
    for ref, rows in zip(
        (first_ref, ga_ref, next_s), lax.fori_loop(0, TB // UNROLL, body, carry)
    ):
        for i in range(NI):
            for g in range(NG):
                ref[SUB * i : SUB * (i + 1), g * w : (g + 1) * w] = rows[i][g]
    ones = jnp.ones((SUB, w), bf16)
    pick = (lax.broadcasted_iota(jnp.int32, (N, TB * N), 1) % N) == lax.broadcasted_iota(
        jnp.int32, (N, TB * N), 0
    )
    picked = []
    for scratch in (mb_s, mc_s):
        flat = lax.dot_general(
            ones, scratch[...].astype(bf16), (((1,), (1,)), ((), ())), preferred_element_type=f32
        )
        picked.append(jnp.where(pick, jnp.concatenate([flat] * NI, axis=0), 0.0))
    gproj_ref[dtw_ref.shape[0] :, :] = jnp.dot(
        jnp.concatenate(picked, axis=0).astype(bf16), places_ref[...], preferred_element_type=f32
    )
    s2 = row_sums(s2_s, TB, NG)
    ratio = jnp.where(
        delta < 0.0625,
        1.0 - delta * (0.5 - delta * (1.0 / 6.0 - delta * (1.0 / 24.0 - delta * (1.0 / 120.0)))),
        (1.0 - jnp.exp(-delta)) / jnp.maximum(delta, 0.0625),
    )
    gpre = ratio * (row_sums(r_s, TB, NG) * LN2 + du_s[...] * s2)
    low = gpre.astype(bf16)
    gu_ref[...] = gy_s[...] * skip_ref[...] + delta * s2
    gproj_ref[0 : dtw_ref.shape[0], :] = lax.dot_general(
        dtw_ref[...], low, (((1,), (1,)), ((), ())), preferred_element_type=f32
    )
    gdtw_ref[...] += jnp.dot(rank, low, preferred_element_type=f32)
    gvec_ref[0:1, :] += jnp.sum(gpre, axis=0, keepdims=True)


def scan_bwd(groups, proj, u, z, masks, y, delta, gg, h, dtw, a2, skip, places, end, late):
    rows, C = u.shape
    N, R = a2.shape[0], dtw.shape[0]
    w = min(128, C)
    TB = pick_block(rows // groups, SCAN_BLOCK)
    nb = rows // groups // TB
    where = lambda g, b: g * nb + nb - 1 - b
    blk = lambda s, n=TB: pl.BlockSpec((n, s), lambda g, b: (where(g, b), 0))
    own = pl.BlockSpec((N, C), lambda g, b: (g, 0))
    rowed = lambda n: pl.BlockSpec((n, TB), lambda g, b: (0, where(g, b)))
    sd = jax.ShapeDtypeStruct
    outs = [
        sd((rows, C), bf16), sd((rows, C), f32), sd((R + 2 * N, rows), f32), sd((groups * N, C), f32),
        sd((N, C), f32), sd((R, C), f32), sd((8, C), f32),
    ]
    fold = pltpu.VMEM((TB * (C // w) * SUB // 2, w), f32)
    return pl.pallas_call(
        scan_bwd_kernel,
        name="scan_bwd",
        grid=(groups, nb),
        in_specs=[
            rowed(R + 2 * N), blk(C), blk(C), blk(masks.shape[1]), blk(C), blk(C), blk(C), blk(C, TB * N),
            whole(dtw.shape), whole(a2.shape), whole(skip.shape), whole(places.shape), own, own,
        ],
        out_specs=[
            blk(C), blk(C), rowed(R + 2 * N), own,
            whole((N, C)), whole((R, C)), whole((8, C)),
        ],
        out_shape=outs,
        scratch_shapes=[pltpu.VMEM((TB, C), f32)] * 3
        + [fold] * 2
        + [pltpu.VMEM((TB * 2 * N, w), f32)]
        + [pltpu.VMEM((TB * N, w), f32)] * 2
        + [pltpu.VMEM((N, C), f32)]
        + [pltpu.VMEM((TB, 128), f32), pltpu.VMEM((TB * 2 * N, 128), bf16)],
        compiler_params=params("arbitrary", "arbitrary"),
        cost_estimate=cost(rows * C * N * 20, outs + [h], rows * C * N),
    )(proj, u, z, masks, y, delta, gg, h, dtw, a2, skip, places, end, late)


def pick_kernel(slot_ref, w_ref, x_ref, z_ref):
    x_ref[...] = w_ref[:, 0, :]
    z_ref[...] = w_ref[:, 1, :]


def pick(place, w_in, pieces, ctx):
    rows, _, total = w_in.shape
    piece = total // pieces // ctx
    if piece % 128:
        own = lax.dynamic_index_in_dim(
            w_in.reshape(rows, 2, pieces, ctx, piece), place, 3, False
        ).reshape(rows, 2, pieces * piece)
        return own[:, 0], own[:, 1]
    out = jax.ShapeDtypeStruct((rows, pieces * piece), w_in.dtype)
    spec = pl.BlockSpec((rows, piece), lambda f, s: (0, f))
    return pl.pallas_call(
        pick_kernel,
        name="pick",
        grid_spec=pltpu.PrefetchScalarGridSpec(
            num_scalar_prefetch=1,
            grid=(pieces,),
            in_specs=[pl.BlockSpec((rows, 2, piece), lambda f, s: (0, 0, f * ctx + s[0]))],
            out_specs=[spec, spec],
        ),
        out_shape=[out, out],
        compiler_params=params("arbitrary"),
        cost_estimate=cost(0, [out, out, out, out]),
    )(place.reshape(1).astype(jnp.int32), w_in)


def put_kernel(slot_ref, xa_ref, xb_ref, za_ref, zb_ref, o_ref):
    first = slot_ref[0] == 0
    piece = o_ref.shape[2] // 2
    for branch, (own, other) in enumerate(((xa_ref, xb_ref), (za_ref, zb_ref))):
        a, b = own[...], other[...]
        o_ref[:, branch, 0:piece] = jnp.where(first, a, b)
        o_ref[:, branch, piece:] = jnp.where(first, b, a)


def put(place, x_own, x_other, z_own, z_other, pieces):
    rows, C = x_own.shape
    piece = C // pieces
    TB = pick_block(rows, 256)
    spec = pl.BlockSpec((TB, piece), lambda b, f, s: (b, f))
    out = jax.ShapeDtypeStruct((rows, 2, 2 * C), x_own.dtype)
    return pl.pallas_call(
        put_kernel,
        name="put",
        grid_spec=pltpu.PrefetchScalarGridSpec(
            num_scalar_prefetch=1,
            grid=(rows // TB, pieces),
            in_specs=[spec] * 4,
            out_specs=pl.BlockSpec((TB, 2, 2 * piece), lambda b, f, s: (b, 0, f)),
        ),
        out_shape=out,
        compiler_params=params("arbitrary", "arbitrary"),
        cost_estimate=cost(0, [out, out]),
    )(place.reshape(1).astype(jnp.int32), x_own, x_other, z_own, z_other)


def conv_in_kernel(
    place_ref, own_ref, other_ref, gain_ref, mask_ref, cw_ref, cb_ref, xp_ref, halo_ref, *refs
):
    pieces, outs = refs[:-8], refs[-8:]
    norm_ref, scale_ref, bx_ref, xc_ref, u_ref, proj_ref, tail_ref, ext_s = outs
    TB, C = u_ref.shape
    taps = cw_ref.shape[0]

    @pl.when(pl.program_id(1) == 0)
    def _():
        ext_s[0:SUB, :] = halo_ref[...]

    x = jnp.where(place_ref[1] == 1, own_ref[...], other_ref[...]).astype(f32)
    scale = lax.rsqrt(jnp.mean(x * x, axis=1, keepdims=True) + eps)
    scale_ref[...] = scale
    norm_ref[...] = (x * scale * gain_ref[...]).astype(bf16)
    bx = 0.0
    for turn, w_ref in enumerate(pieces):
        deep = w_ref.shape[0]
        first = pl.multiple_of((place_ref[0] ^ turn) * deep, deep)
        bx += jnp.dot(norm_ref[:, pl.ds(first, deep)], w_ref[...], preferred_element_type=f32)
    bx_ref[...] = bx
    ext_s[SUB:, :] = bx
    total = cb_ref[...] + cw_ref[taps - 1 : taps, :] * bx
    for tap in range(taps - 1):
        back = taps - 1 - tap
        total += cw_ref[tap : tap + 1, :] * (
            ext_s[SUB - back : SUB - back + TB, :] * mask_ref[:, back : back + 1]
        )
    xc_ref[...] = total
    u = (total * sigmoid(total)).astype(bf16)
    u_ref[...] = u
    proj_ref[...] = lax.dot_general(
        xp_ref[...], u, (((1,), (1,)), ((), ())), preferred_element_type=f32
    )
    ext_s[0:SUB, :] = bx[TB - SUB :, :]
    tail_ref[...] = bx[TB - SUB :, :]


def conv_in(groups, me, use_own, own, other, gain, pieces, masks, cw, cb, xp, halo):
    rows, D = own.shape
    C = pieces[0].shape[1]
    TB = pick_block(rows // groups, CONV_BLOCK)
    nb = rows // groups // TB
    blk = lambda s: pl.BlockSpec((TB, s), lambda g, b, _: (g * nb + b, 0))
    mine = pl.BlockSpec((SUB, C), lambda g, b, _: (g, 0))
    sd = jax.ShapeDtypeStruct
    R = xp.shape[0]
    outs = [
        sd((rows, D), bf16), sd((rows, 1), f32), sd((rows, C), f32), sd((rows, C), f32),
        sd((rows, C), bf16), sd((R, rows), f32), sd((groups * SUB, C), f32),
    ]
    return pl.pallas_call(
        conv_in_kernel,
        name="conv_in",
        grid_spec=pltpu.PrefetchScalarGridSpec(
            num_scalar_prefetch=1,
            grid=(groups, nb),
            in_specs=[
                pl.BlockSpec((TB, D), lambda g, b, p: ((g * nb + b) * p[1], 0)),
                pl.BlockSpec((TB, D), lambda g, b, p: ((g * nb + b) * (1 - p[1]), 0)),
                whole(gain.shape), blk(masks.shape[1]), whole(cw.shape), whole(cb.shape),
                whole(xp.shape), mine,
            ]
            + [whole(p.shape) for p in pieces],
            out_specs=[
                blk(D), blk(1), blk(C), blk(C), blk(C),
                pl.BlockSpec((R, TB), lambda g, b, _: (0, g * nb + b)), mine,
            ],
            scratch_shapes=[pltpu.VMEM((TB + SUB, C), f32)],
        ),
        out_shape=outs,
        compiler_params=params("arbitrary", "arbitrary"),
        cost_estimate=cost(2 * rows * D * C, outs + [own], rows * C),
    )(jnp.stack([me, use_own]).astype(jnp.int32), own, other, gain, masks, cw, cb, xp, halo, *pieces)


def conv_out_kernel(
    gu_ref, gp_ref, xp_ref, xc_ref, bx_ref, z_ref, gz_ref, u_ref, mask_ref, cw_ref, late_ref,
    gm_ref, along_ref, early_ref, gconv_ref, gxp_ref,
    *ext_s,
):
    TB, C = u_ref.shape
    taps = cw_ref.shape[0]

    @pl.when((pl.program_id(1) == 0) & (pl.program_id(0) == 0))
    def _():
        gconv_ref[...] = jnp.zeros_like(gconv_ref)
        gxp_ref[...] = jnp.zeros_like(gxp_ref)

    @pl.when(pl.program_id(1) == 0)
    def _():
        for back in range(1, taps):
            ext_s[back - 1][TB:, :] = late_ref[(back - 1) * SUB : back * SUB, :]

    gp = gp_ref[...]
    xc = xc_ref[...]
    sg = sigmoid(xc)
    inner = gu_ref[...] + lax.dot_general(
        gp, xp_ref[...], (((0,), (0,)), ((), ())), preferred_element_type=f32
    )
    gxc = inner * (sg * (1.0 + xc * (1.0 - sg)))
    bx = bx_ref[...]
    gx = cw_ref[taps - 1 : taps, :] * gxc
    gconv_ref[taps - 1 : taps, :] += jnp.sum(gxc * bx, axis=0, keepdims=True)
    gconv_ref[taps : taps + 1, :] += jnp.sum(gxc, axis=0, keepdims=True)
    for back in range(1, taps):
        tap = taps - 1 - back
        ext = ext_s[back - 1]
        reached = gxc * mask_ref[:, back : back + 1]
        ext[0:TB, :] = reached
        moved = ext[back : back + TB, :]
        gx += cw_ref[tap : tap + 1, :] * moved
        gconv_ref[tap : tap + 1, :] += jnp.sum(moved * bx, axis=0, keepdims=True)
        ext[TB:, :] = reached[0:SUB, :]
        early_ref[(back - 1) * SUB : back * SUB, :] = reached[0:SUB, :]
    gz = gz_ref[...]
    gx = gx.astype(bf16)
    gm_ref[:, 0:C] = gx
    gm_ref[:, C:] = gz
    terms = (gx.astype(f32) * bx + gz.astype(f32) * z_ref[...]).astype(bf16)
    along_ref[...] = lax.dot_general(
        jnp.ones((SUB, C), bf16), terms, (((1,), (1,)), ((), ())), preferred_element_type=f32
    )
    gxp_ref[...] += jnp.dot(gp, u_ref[...], preferred_element_type=f32)


def conv_out(groups, gu, gp, xp, xc, bx, z, gz, u, masks, cw, late):
    rows, C = u.shape
    taps = cw.shape[0]
    R = xp.shape[0]
    TB = pick_block(rows // groups, CONV_BLOCK)
    nb = rows // groups // TB
    blk = lambda s: pl.BlockSpec((TB, s), lambda g, b: (g * nb + nb - 1 - b, 0))
    own = pl.BlockSpec(((taps - 1) * SUB, C), lambda g, b: (g, 0))
    sd = jax.ShapeDtypeStruct
    outs = [
        sd((rows, 2 * C), bf16), sd((SUB, rows), f32), sd((groups * (taps - 1) * SUB, C), f32),
        sd((8, C), f32), sd((R, C), f32),
    ]
    return pl.pallas_call(
        conv_out_kernel,
        name="conv_out",
        grid=(groups, nb),
        in_specs=[
            blk(C), pl.BlockSpec((R, TB), lambda g, b: (0, g * nb + nb - 1 - b)),
            whole(xp.shape), blk(C), blk(C), blk(C), blk(C), blk(C),
            blk(masks.shape[1]), whole(cw.shape), own,
        ],
        out_specs=[
            blk(2 * C),
            pl.BlockSpec((SUB, TB), lambda g, b: (0, g * nb + nb - 1 - b)),
            own,
            whole((8, C)),
            whole((R, C)),
        ],
        out_shape=outs,
        scratch_shapes=[pltpu.VMEM((TB + SUB, C), f32)] * (taps - 1),
        compiler_params=params("arbitrary", "arbitrary"),
        cost_estimate=cost(4 * rows * R * C, outs + [gu, xc, bx, z], rows * C),
    )(gu, gp, xp, xc, bx, z, gz, u, masks, cw, late)


def spread_kernel(slot_ref, x_ref, w_ref, *refs, adding):
    o_ref = refs[-1]
    for z in range(o_ref.shape[0]):
        total = jnp.dot(x_ref[0], w_ref[z], preferred_element_type=f32)
        if adding:
            total = total + refs[0][z].astype(f32)
        o_ref[z] = total.astype(bf16)


def spread(slot, x, w, added=(), first=()):
    _, rows, K = x.shape
    shares, _, share = w.shape
    per = 2 if shares % 2 == 0 and rows * share <= 512 * 512 else 1
    out = jax.ShapeDtypeStruct((shares, rows, share), bf16)
    block = pl.BlockSpec((per, rows, share), lambda z, s: (z, 0, 0))
    return pl.pallas_call(
        functools.partial(spread_kernel, adding=len(added)),
        name="spread",
        grid_spec=pltpu.PrefetchScalarGridSpec(
            num_scalar_prefetch=1,
            grid=(shares // per,),
            in_specs=[
                pl.BlockSpec((1, rows, K), lambda z, s: (s[0], 0, 0)),
                pl.BlockSpec((per, K, share), lambda z, s: (z, 0, 0)),
            ]
            + [block] * len(added)
            + [pl.BlockSpec(memory_space=pl.ANY)] * len(first),
            out_specs=block,
        ),
        out_shape=out,
        compiler_params=params("arbitrary"),
        cost_estimate=cost(2 * rows * K * shares * share, [out, x, w]),
    )(slot, x, w, *added, *first)


def collect_kernel(slot_ref, own_ref, other_ref, w_ref, o_ref):
    shares, _, share = own_ref.shape

    def product(ref):
        total = jnp.dot(ref[0], w_ref[0:share, :], preferred_element_type=f32)
        for z in range(1, shares):
            total += jnp.dot(
                ref[z], w_ref[z * share : (z + 1) * share, :], preferred_element_type=f32
            )
        o_ref[0] = total

    @pl.when(pl.program_id(0) == 0)
    def _():
        product(own_ref)

    @pl.when(pl.program_id(0) == 1)
    def _():
        product(other_ref)


def collect(slot, own, other, w):
    shares, rows, share = own.shape
    C = w.shape[1]
    out = jax.ShapeDtypeStruct((2, rows, C), f32)
    return pl.pallas_call(
        collect_kernel,
        name="collect",
        grid_spec=pltpu.PrefetchScalarGridSpec(
            num_scalar_prefetch=1,
            grid=(2,),
            in_specs=[
                pl.BlockSpec(own.shape, lambda s, p: (0, 0, 0)),
                pl.BlockSpec(own.shape, lambda s, p: (0, 0, 0)),
                pl.BlockSpec(w.shape, lambda s, p: (0, 0)),
            ],
            out_specs=pl.BlockSpec((1, rows, C), lambda s, p: (s + p[0] - 2 * s * p[0], 0, 0)),
        ),
        out_shape=out,
        compiler_params=params("arbitrary"),
        cost_estimate=cost(4 * rows * C * share * shares, [out, own, other, w]),
    )(slot, own, other, w)


def after(value, *others):
    return lax.optimization_barrier((value,) + others)[0]


def swap_cores(value):
    return lax.ppermute(value, "context", [(0, 1), (1, 0)])


def paired():
    return lax.axis_size("context") == 2


def in_order(own, other):
    first = lax.axis_index("context") == 0
    return jnp.where(first, own, other), jnp.where(first, other, own)


def gather_context(value):
    if not paired():
        return lax.all_gather(value, "context")
    return jnp.stack(in_order(value, swap_cores(value)))


def sum_over(value, *axes):
    for axis in axes:
        size, step = lax.axis_size(axis), 1
        if size & (size - 1):
            value = lax.psum(value, axis)
            continue
        while step < size:
            value = value + lax.ppermute(value, axis, [(i, i ^ step) for i in range(size)])
            step *= 2
    return value


ROW = [(0, 1), (1, 0), (2, 3), (3, 2)]
COLUMN = [(0, 2), (2, 0), (1, 3), (3, 1)]


def gather_fsdp(value, *hold):
    size = lax.axis_size("fsdp")
    if size != 4 or value.shape[0] % 2:
        pieces = lax.all_gather(value, "fsdp")
        return jnp.zeros((), jnp.int32), [pieces[i] for i in range(size)]
    half = value.shape[0] // 2
    row = lax.ppermute(value, "fsdp", ROW)
    column = lax.ppermute(value, "fsdp", COLUMN)
    if hold:
        row, column = lax.optimization_barrier((row, column) + hold)[:2]
    far = jnp.concatenate(
        [lax.ppermute(row[:half], "fsdp", COLUMN), lax.ppermute(column[half:], "fsdp", ROW)]
    )
    return lax.axis_index("fsdp"), [value, row, column, far]


def stacked(me, pieces):
    if len(pieces) != 4:
        return jnp.stack(pieces)
    a, b, c, d = pieces
    odd, high = me % 2 == 1, me // 2 == 1
    pick2 = lambda flag, x, y: jnp.where(flag, y, x)
    return jnp.stack(
        [
            pick2(high, pick2(odd, a, b), pick2(odd, c, d)),
            pick2(high, pick2(odd, b, a), pick2(odd, d, c)),
            pick2(high, pick2(odd, c, d), pick2(odd, a, b)),
            pick2(high, pick2(odd, d, c), pick2(odd, b, a)),
        ]
    )


def scatter_fsdp(parts, *hold):
    size = lax.axis_size("fsdp")
    if size & (size - 1):
        return lax.psum_scatter(parts, "fsdp", scatter_dimension=0).astype(f32)
    me = lax.axis_index("fsdp")
    take = lambda i: lax.dynamic_index_in_dim(parts, i, 0, False)
    got = [
        lax.ppermute(take(me ^ turn), "fsdp", [(i, i ^ turn) for i in range(size)])
        for turn in range(1, size)
    ]
    if hold:
        got = lax.optimization_barrier((*got, *hold))[: size - 1]
    return sum([g.astype(f32) for g in got], take(me).astype(f32))


def flip(value, step):
    size = lax.axis_size("tensor")
    return lax.ppermute(value, "tensor", [(i, i ^ step) for i in range(size)])


def token_share(part, groups, i):
    each = part.shape[1] // groups
    size = each // lax.axis_size("context")
    return jnp.concatenate(
        [lax.dynamic_slice_in_dim(part, g * each + i * size, size, 1) for g in range(groups)], axis=1
    )


def token_join(values, groups):
    size = values[0].shape[-1] // groups
    return jnp.concatenate(
        [v[..., g * size : (g + 1) * size] for g in range(groups) for v in values], axis=-1
    )


def start_sum(part, groups):
    tp = lax.axis_size("tensor")
    if not paired() or tp & (tp - 1):
        return lax.psum(part, ("tensor", "context")), []
    place = lax.axis_index("context")
    other = swap_cores(token_share(part, groups, 1 - place).astype(bf16))
    total = token_share(part, groups, place) + other.astype(f32)
    sent = total.astype(bf16)
    return total, [flip(sent, step) for step in range(1, tp)]


def end_sum(begun, groups, out_type, *meanwhile):
    total, got = begun
    for piece in got:
        total = total + after(piece, *meanwhile).astype(f32)
    total = total.astype(out_type)
    return token_join(in_order(total, swap_cores(total)), groups) if got else total


def sum_parts(parts, groups, fillers):
    tp = lax.axis_size("tensor")
    if not paired() or tp & (tp - 1):
        fillers(1, parts[0])
        return [lax.psum(part, ("tensor", "context")) for part in parts]
    place = lax.axis_index("context")
    share = lambda i: jnp.concatenate([token_share(p, groups, i) for p in parts], axis=0)
    total = share(place) + swap_cores(share(1 - place).astype(bf16)).astype(f32)
    step = 1
    while step < tp:
        got = flip(total.astype(bf16), step)
        total = total + after(got, *fillers(step, total)).astype(f32)
        step *= 2
    R = parts[0].shape[0]
    total = token_join(in_order(total, swap_cores(total)), groups)
    return [total[i * R : (i + 1) * R] for i in range(len(parts))]


def on_device(
    x_in,
    teacher,
    segments,
    valid,
    norm_gain,
    w_in,
    conv_w,
    conv_b,
    x_proj,
    dt_w,
    dt_bias,
    a_log,
    d_skip,
    w_out,
):
    groups, blocklen, width = x_in.shape
    nf, ctx, tp = (lax.axis_size(name) for name in ("fsdp", "context", "tensor"))
    place = lax.axis_index("context")
    rows_here, _, chans_tensor = w_in.shape
    piece = conv_w.shape[1] // ctx
    chans = nf * piece
    taps, rank_dim, nstate = conv_w.shape[0], dt_w.shape[0], a_log.shape[0]
    proj_dim = x_proj.shape[0]
    share = width // tp
    cols_here = w_out.shape[1]
    full = blocklen * ctx
    tokens = groups * full
    part = full // CHUNKS
    sub = part // ctx
    rows = groups * part
    order = range(CHUNKS)
    first_col = lax.axis_index("tensor") * share

    def by_chunks(value):
        if paired():
            return in_order(value, swap_cores(value))
        value = jnp.moveaxis(lax.all_gather(value, "context"), 0, 1)
        value = value.reshape((groups, CHUNKS, part) + value.shape[3:])
        return [value[:, c] for c in order]

    def mine(value):
        value = value.reshape((groups, ctx, sub) + value.shape[2:])
        return lax.dynamic_index_in_dim(value, place, 1, False)

    def to_work(value):
        if not paired():
            return [mine(v) for v in by_chunks(value)]
        value = value.reshape((groups, CHUNKS, sub) + value.shape[2:])
        got = swap_cores(lax.dynamic_index_in_dim(value, 1 - place, 1, False))
        return in_order(lax.dynamic_index_in_dim(value, place, 1, False), got)

    def from_work(values):
        if not paired():
            stacked = jnp.moveaxis(lax.all_gather(jnp.stack(values), "context"), 2, 0)
            stacked = jnp.swapaxes(stacked, 1, 2).reshape((groups, full) + values[0].shape[2:])
            return lax.dynamic_slice_in_dim(stacked, place * blocklen, blocklen, 1)
        keep, sent = in_order(values[0], values[1])
        return jnp.concatenate(in_order(keep, swap_cores(sent)), axis=1)

    if paired():
        x_own, x_other = (v.reshape(rows, width) for v in (x_in, swap_cores(x_in)))
        columns = in_order(*(lax.dynamic_slice_in_dim(v, first_col, share, 1) for v in (x_own, x_other)))
    else:
        x_chunks = [v.reshape(rows, width) for v in by_chunks(x_in)]
        columns = [lax.dynamic_slice_in_dim(v, first_col, share, 1) for v in x_chunks]
    x_shares = [mine(v.reshape(groups, part, share)) for v in columns]
    if not paired():
        *x_shares, x_chunks[0] = lax.optimization_barrier((*x_shares, x_chunks[0]))
    marks_in = jnp.stack([segments, valid], axis=-1)
    marks_in = jnp.concatenate(by_chunks(marks_in), axis=1)
    seg = marks_in[..., 0]
    valid_all = marks_in[..., 1].astype(f32)
    count = sum_over(jnp.sum(valid_all).reshape(1, 1), "fsdp")
    masks = []
    for back in range(taps):
        same = seg[:, back:] == seg[:, : full - back]
        masks.append(jnp.pad(same, ((0, 0), (back, 0)), constant_values=False))
    masks = jnp.stack(masks, axis=-1).astype(f32)
    masks = [masks[:, c * part : (c + 1) * part].reshape(rows, taps) for c in order]

    wx_own, wz_own = pick(place, w_in, nf, ctx)
    small = jnp.concatenate(
        [x_proj, dt_w, a_log, conv_w, conv_b[None], dt_bias[None], d_skip[None]], axis=0
    )
    nsmall = small.shape[0]
    small = lax.dynamic_slice_in_dim(small, place * piece, piece, 1)
    gain_rows = norm_gain.reshape(-1, piece)
    spare = -(nsmall + gain_rows.shape[0]) % 32
    small = jnp.concatenate([small, gain_rows, jnp.zeros((spare, piece), bf16)], axis=0)
    small = lax.all_gather(after(small, wx_own), "fsdp")
    gain_all = small[:, nsmall : nsmall + gain_rows.shape[0]].reshape(width).astype(f32)
    small = jnp.swapaxes(small[:, :nsmall], 0, 1).reshape(nsmall, chans)
    ends = [0]
    for size in (proj_dim, rank_dim, nstate, taps, 1, 1, 1):
        ends.append(ends[-1] + size)
    xp, dtw, alog, cw, cb, dtb, skip = (small[a:b] for a, b in zip(ends[:-1], ends[1:]))
    cw, cb, skip, dtb = (v.astype(f32) for v in (cw, cb, skip, dtb))
    rates = -jnp.exp(alog.astype(f32))
    a2 = rates * LOG2E
    me, wx_pieces = gather_fsdp(wx_own)
    wz = lax.all_gather(after(wz_own, *wx_pieces), "fsdp", axis=0, tiled=True)
    wout_own = lax.dynamic_index_in_dim(
        w_out.reshape(nf, ctx, piece, cols_here), place, 1, False
    ).reshape(chans, cols_here)
    wout = lax.all_gather(after(wout_own, *wx_pieces), "fsdp")
    wout_t = jnp.swapaxes(wout, 1, 2).reshape(width, chans)
    if nf != tp:
        wout = jnp.swapaxes(wout_t.T.reshape(chans, tp, share), 0, 1)
    win_t = jnp.concatenate([stacked(me, wx_pieces).reshape(width, chans), wz], axis=1)
    win_t = jnp.swapaxes(win_t.reshape(tp, share, 2 * chans), 1, 2)

    bxs, xcs, us, zs, parts, normeds, scales = [], [], [], [], [], [], []
    tail = jnp.zeros((groups * SUB, chans), f32)
    for c in order:
        if paired():
            source = (place == c).astype(jnp.int32), x_own, x_other
        else:
            source = jnp.ones((), jnp.int32), x_chunks[c], x_chunks[c]
        normed, scale, bx, xc, u, proj_part, tail = conv_in(
            groups, me, *source, gain_all[None], wx_pieces, masks[c], cw, cb, xp, tail
        )
        normeds.append(normed)
        scales.append(scale.reshape(groups, part, 1))
        bxs.append(bx)
        xcs.append(xc)
        us.append(u)
        parts.append(proj_part)

    def fillers(step, total):
        c = step // 2
        if c < CHUNKS and len(zs) == c:
            zs.append(jnp.dot(after(normeds[c], total), wz, preferred_element_type=f32))
            return (zs[c],)
        return ()

    projs = sum_parts(parts, groups, fillers)
    for c in range(len(zs), CHUNKS):
        zs.append(jnp.dot(normeds[c], wz, preferred_element_type=f32))

    slot_own = place.reshape(1).astype(jnp.int32)
    slot_other = 1 - slot_own

    def to_shares(value, w, between=None):
        value = jnp.moveaxis(value.reshape(groups, ctx, sub, -1), 1, 0).reshape(ctx, groups * sub, -1)
        if paired():
            send = spread(slot_other, value, w)
            first = [between(send)] if between else []
            total = spread(slot_own, value, w, [swap_cores(send)], first)
        else:
            first = [between(value)] if between else []
            total = spread(jnp.zeros((1,), jnp.int32), value.reshape(1, ctx * groups * sub, -1), w)
            total = jnp.moveaxis(total.reshape(tp, ctx, groups * sub, share), 1, 0)
            total = lax.psum_scatter(total, "context", scatter_dimension=0)
        summed = lax.psum_scatter(total, "tensor", scatter_dimension=0)
        return first, total, summed.reshape(groups, sub, share)

    gateds, ys, deltas, states = [], [], [], []
    outs, grad_outs, losses = [], [], []
    targets = to_work(lax.dynamic_slice_in_dim(teacher, first_col, share, 2))
    state = jnp.zeros((groups * nstate, chans), f32)
    for c in order:
        u = us[c] if c == 0 else after(us[c], sent)
        gated, y, delta, h, state = scan_fwd(
            groups, projs[c], u, zs[c], masks[c], dtw, dtb, a2, skip, state
        )
        deltas.append(delta)
        gateds.append(gated)
        ys.append(y)
        states.append(h)
        _, sent, branch = to_shares(gated, wout)
        outs.append(x_shares[c].astype(f32) + branch.astype(f32))
        errors = outs[c] - targets[c].astype(f32)
        live = mine(valid_all[:, c * part : (c + 1) * part])[..., None]
        losses.append(jnp.sum(live * errors * errors))
        grad_outs.append((tokens * nf / count[0, 0]) * live * errors)
    loss_value = sum_over(sum(losses).reshape(1, 1), "context", "tensor", "fsdp")[0, 0]
    loss_value = loss_value / width / count[0, 0]
    out_share = from_work(outs)

    late = jnp.zeros((groups * nstate, chans), f32)
    late_conv = jnp.zeros((groups * (taps - 1) * SUB, chans), f32)
    grad_inputs, alongs = [None] * CHUNKS, [None] * CHUNKS
    turn = (((0,), (0,)), ((), ()))
    size = pick_block(part, SCAN_BLOCK)
    places = (
        lax.broadcasted_iota(jnp.int32, (size * nstate, size), 0) // nstate
        == lax.broadcasted_iota(jnp.int32, (size * nstate, size), 1)
    ).astype(bf16)
    gwout = gwz = gwx = 0.0
    grads = 0.0
    lows = [None] * CHUNKS
    for c in reversed(order):
        low = grad_outs[c].astype(bf16).reshape(groups * sub, share)
        if c < CHUNKS - 1:
            low = after(low, lows[c + 1])
        lows[c] = lax.all_gather(low, "tensor")

    gated_parts = []
    for gated in gateds if paired() else []:
        gated = jnp.moveaxis(gated.reshape(groups, ctx, sub, chans), 1, 0)
        gated = gated.reshape(ctx, groups * sub, chans)
        gated_parts.append(
            [lax.dynamic_index_in_dim(gated, i, 0, False) for i in (place, 1 - place)]
        )

    def grad_gated(c, low):
        if paired():
            other = swap_cores(low)
            gg = collect(slot_own, low, other, wout_t)
            pairs = list(zip(gated_parts[c], (low, other)))
        else:
            low = jnp.moveaxis(lax.all_gather(low, "context"), 0, 1).reshape(tp, rows, share)
            gg = jnp.einsum(
                "ztj,zcj->tc", low, wout, preferred_element_type=f32
            ).reshape(ctx, groups * sub, chans)
            gated = jnp.moveaxis(gateds[c].reshape(groups, ctx, sub, chans), 1, 0)
            pairs = [(gated.reshape(rows, chans), low)]
        gg = jnp.moveaxis(gg.reshape(ctx, groups, sub, chans), 0, 1).reshape(rows, chans)
        return gg, pairs

    last, places, *gated_parts = lax.optimization_barrier(
        (lows[-1], places, *gated_parts, out_share, loss_value, wout_t, win_t)
    )[: 2 + len(gated_parts)]
    gg, pairs = grad_gated(CHUNKS - 1, last)
    for c in reversed(order):
        gz, gu, gproj, late, ga, gdtw, gvec = scan_bwd(
            groups, projs[c], us[c], zs[c], masks[c], ys[c], deltas[c], gg, states[c],
            dtw, a2, skip, places, state, late,
        )
        state = states[c].reshape(groups, part * nstate, chans)[:, :nstate].reshape(-1, chans)
        gproj = start_sum(gproj, groups)
        summed = gproj[0]
        if c < CHUNKS - 1:
            summed, grad_inputs[c + 1] = lax.optimization_barrier((summed, grad_inputs[c + 1]))
        if c:
            gg_next, pairs_next = grad_gated(c - 1, after(lows[c - 1], summed))
            if c == 1:
                pairs = pairs + pairs_next
        for left, right in pairs if c else []:
            left = after(left, summed)
            gwout += jnp.einsum("tc,ztj->zcj", left, right, preferred_element_type=f32)
        gwz += lax.dot_general(normeds[c], after(gz, summed), turn, preferred_element_type=f32)
        if c < CHUNKS - 1:
            gm = after(gm, summed)
            gwx += lax.dot_general(
                normeds[c + 1], gm[:, :chans], turn, preferred_element_type=f32
            )
        if c:
            gg, pairs = gg_next, pairs_next
            fillers = [gwz, gg, gwout]
        else:
            fillers = [gwz, gwx] if paired() else []
        gproj = end_sum(gproj, groups, bf16, *fillers)
        gm, along, late_conv, gconv, gxp = conv_out(
            groups, gu, gproj, xp, xcs[c], bxs[c], zs[c], gz, us[c], masks[c], cw, late_conv
        )
        def grad_wx(token):
            return gwx + lax.dot_general(
                normeds[0], after(gm, token)[:, :chans], turn, preferred_element_type=f32
            )

        first, sent, grad_normed = to_shares(gm, win_t, None if c else grad_wx)
        if not c:
            gwx = first[0]
            gconv, gxp, along = lax.optimization_barrier((gconv, gxp, along, sent))[:3]
        if c == 1:
            gwout = jnp.swapaxes(gwout, 0, 1).reshape(chans, nf, cols_here)
            gwout = jnp.swapaxes(gwout, 0, 1).astype(bf16)
            gwout = lax.psum_scatter(gwout, "fsdp", scatter_dimension=0)
        if c:
            gg = after(gg, sent, gwout) if paired() else gg
        grads += jnp.concatenate(
            [gxp, gdtw, ga * LN2, gconv, gvec], axis=0
        )
        alongs[c] = along[0]
        grad_inputs[c] = grad_normed
    grads = after(grads, sent)
    gwz = lax.psum_scatter(
        gwz.astype(bf16).reshape(nf, rows_here, chans), "fsdp", scatter_dimension=0
    )
    gwz = after(gwz, sent).astype(f32)
    gwz_other = swap_cores(gwz) if paired() else None
    sums = sum_over(jnp.concatenate(alongs)[None], "context", "tensor")[0]
    wout_g = gather_context((after(gwout, sent) if paired() else gwout).astype(f32))
    wout_g = jnp.swapaxes(wout_g.reshape(ctx, nf, piece, cols_here), 0, 1).reshape(
        chans_tensor, cols_here
    )
    gwx = scatter_fsdp(
        gwx.astype(bf16).reshape(nf, rows_here, chans), sent, sums, *([wout_g] if paired() else [])
    )
    gain_part = jnp.sum(gwx * wx_own.astype(f32) + gwz * wz_own.astype(f32), axis=1)
    gain_share = lax.dynamic_slice_in_dim(gain_all, first_col, share, 0)
    fixed, factors = [], []
    for c in order:
        along = sums[c * rows : (c + 1) * rows].reshape(groups, part)
        scale = mine(scales[c])
        fixed.append(
            grad_outs[c]
            - x_shares[c].astype(f32) * (scale * scale * (mine(along)[..., None] / width))
        )
        factors.append(scale * gain_share)
    nrows = grads.shape[0]
    grads = jnp.swapaxes(grads.reshape(nrows, nf, piece), 0, 1)
    grads = scatter_fsdp(grads)
    grads = jnp.swapaxes(gather_context(grads), 0, 1).reshape(nrows, ctx * piece)
    xp_g, dtw_g, alog_g = (grads[a:b] for a, b in zip(ends[:3], ends[1:4]))
    cw_g = grads[ends[3] : ends[4]]
    cb_g = grads[ends[4]]
    dtb_g, skip_g = grads[ends[3] + SUB], grads[ends[3] + SUB + 1]
    if paired() and piece % 128 == 0:
        win_g = put(place, gwx, swap_cores(gwx), gwz, gwz_other, nf)
    else:
        win_g = jnp.stack(
            [
                jnp.moveaxis(gather_context(g).reshape(ctx, rows_here, nf, piece), 0, 2).reshape(
                    rows_here, chans_tensor
                )
                for g in (gwx, gwz)
            ],
            axis=1,
        )
    if paired():
        gain_part = after(gain_part, win_g)
    grad_gain = sum_over(gain_part[None], "context", "tensor")[0] / norm_gain.astype(f32)
    done = (grads, win_g, *fixed)
    got = [grad_inputs[c] if c else after(grad_inputs[c], *done) for c in order]
    grad_share = from_work([f + k * g.astype(f32) for f, k, g in zip(fixed, factors, got)])
    return (
        out_share,
        loss_value,
        grad_share,
        grad_gain,
        win_g,
        cw_g,
        cb_g,
        xp_g,
        dtw_g,
        dtb_g,
        alog_g,
        skip_g,
        wout_g,
    )


def solution(mesh):
    return jax.shard_map(
        on_device,
        mesh=mesh,
        in_specs=(
            P("fsdp", "context", None),
            P("fsdp", "context", None),
            P("fsdp", "context"),
            P("fsdp", "context"),
            P("fsdp"),
            P("fsdp", None, "tensor"),
            P(None, ("tensor", "fsdp")),
            P(("tensor", "fsdp")),
            P(None, ("tensor", "fsdp")),
            P(None, ("tensor", "fsdp")),
            P(("tensor", "fsdp")),
            P(None, ("tensor", "fsdp")),
            P(("tensor", "fsdp")),
            P("tensor", "fsdp"),
        ),
        out_specs=(
            P("fsdp", "context", "tensor"),
            P(),
            P("fsdp", "context", "tensor"),
            P("fsdp"),
            P("fsdp", None, "tensor"),
            P(None, ("tensor", "fsdp")),
            P(("tensor", "fsdp")),
            P(None, ("tensor", "fsdp")),
            P(None, ("tensor", "fsdp")),
            P(("tensor", "fsdp")),
            P(None, ("tensor", "fsdp")),
            P(("tensor", "fsdp")),
            P("tensor", "fsdp"),
        ),
        check_vma=False,
    )
```

```python
import functools

import jax
import jax.numpy as jnp
from jax import lax
from jax.experimental import pallas as pl
from jax.experimental.pallas import tpu as pltpu
from jax.sharding import PartitionSpec as P

f32 = jnp.float32
bf16 = jnp.bfloat16
eps = 1e-05
LOG2E = 1.4426950408889634
LN2 = 0.6931471805599453
FAR = 1e30
SUB = 8
CHUNKS = 2
SCAN_BLOCK = 128
CONV_BLOCK = 256


def pick_block(total, most):
    size = min(total, most)
    while total % size:
        size //= 2
    return size


def whole(shape):
    return pl.BlockSpec(shape, lambda *_: (0,) * len(shape))


def params(*semantics):
    return pltpu.CompilerParams(dimension_semantics=semantics or None)


def cost(flops, arrays, exps=0):
    moved = sum(a.size * a.dtype.itemsize for a in arrays)
    return pl.CostEstimate(flops=int(flops), bytes_accessed=int(moved), transcendentals=int(exps))


def softplus(v):
    tail = jnp.exp(-jnp.abs(v))
    small = tail * (1.0 - tail * (0.5 - tail * (1.0 / 3.0)))
    return jnp.maximum(v, 0.0) + jnp.where(tail < 0.0078125, small, jnp.log(1.0 + tail))


def sigmoid(v):
    return 0.5 * jnp.tanh(0.5 * v) + 0.5


def fold_rows(parts, row):
    half = 1
    while len(parts) > 1:
        low = (row & half) == 0
        parts = [
            jnp.where(low, a, b) + pltpu.roll(jnp.where(low, b, a), half, 0)
            for a, b in zip(parts[0::2], parts[1::2])
        ]
        half *= 2
    return parts[0]


def tiles_of(ref, base, w):
    return [ref[pl.ds(base, SUB), g * w : (g + 1) * w] for g in range(ref.shape[1] // w)]


def row_of(tile, r):
    return jnp.broadcast_to(tile[r : r + 1, :], tile.shape)


UNROLL = 8


def put_columns(ref, values, wide_s, rows_s):
    TB, count = values.shape
    w = ref.shape[1]
    high = values.astype(bf16).astype(f32)
    wide_s[:, 0:count] = high
    wide_s[:, count : 2 * count] = values - high
    wide_s[:, 2 * count :] = jnp.zeros((TB, 128 - 2 * count), f32)
    row = lax.broadcasted_iota(jnp.int32, (SUB, 128), 0)
    lane = lax.broadcasted_iota(jnp.int32, (SUB, 128), 1)
    tiles = count // SUB
    picks = [(lane == row + SUB * i) | (lane == row + SUB * i + count) for i in range(tiles)]
    for t in range(0, TB, 2):
        pair = [jnp.broadcast_to(wide_s[t + d : t + d + 1, :], (SUB, 128)) for d in range(2)]
        for i in range(tiles):
            both = jnp.concatenate([jnp.where(picks[i], v, 0.0) for v in pair], axis=0)
            rows_s[(i * TB + t) * SUB : (i * TB + t + 2) * SUB, :] = both.astype(bf16)
    ones = jnp.ones((128, w), bf16)
    for i in range(tiles):
        block = slice(i * TB * SUB, (i + 1) * TB * SUB)
        ref[block, :] = jnp.dot(rows_s[block, :], ones, preferred_element_type=f32)


def merge_pair(even, odd, low):
    half = SUB // 2
    return jnp.where(low, even, odd) + pltpu.roll(jnp.where(low, odd, even), half, 0)


def row_sums(ref, TB, NG):
    half = SUB // 2
    columns = []
    for g in range(NG):
        parts = [ref[pl.ds(g * TB * half + s, TB, stride=half), :] for s in range(half)]
        while len(parts) > 1:
            parts = [a + b for a, b in zip(parts[0::2], parts[1::2])]
        columns.append(parts[0])
    return jnp.concatenate(columns, axis=1) if NG > 1 else columns[0]


def at_row(t, scale, offset=0):
    return pl.ds(pl.multiple_of(t * scale + offset, SUB), SUB)


def scan_fwd_kernel(
    proj_ref, u_ref, z_ref, mask_ref, dtw_ref, dtb_ref, a2_ref, skip_ref, start_ref, *refs
):
    gated_ref, y_ref, delta_ref, h_ref, last_ref, dec_s, du_s, p_s, bc_s, wide_s, rows_s = refs[-11:]
    TB, C = u_ref.shape
    N = a2_ref.shape[0]
    w = min(128, C)
    NG, NI = C // w, N // SUB

    @pl.when(pl.program_id(1) == 0)
    def _():
        last_ref[...] = start_ref[...]

    rank = proj_ref[0 : dtw_ref.shape[0], :].astype(bf16)
    put_columns(bc_s, proj_ref[dtw_ref.shape[0] :, :].T, wide_s, rows_s)
    delta = softplus(
        lax.dot_general(
            rank, dtw_ref[...], (((0,), (0,)), ((), ())), preferred_element_type=f32
        ) + dtb_ref[...]
    )
    delta_ref[...] = delta
    du_s[...] = delta * u_ref[...].astype(f32)
    dec_s[...] = jnp.where(mask_ref[:, 1:2] > 0.5, delta, FAR)
    part = lambda ref: [
        [ref[SUB * i : SUB * (i + 1), g * w : (g + 1) * w] for g in range(NG)] for i in range(NI)
    ]
    a2 = part(a2_ref)

    low = lax.broadcasted_iota(jnp.int32, (SUB, w), 0) < SUB // 2

    def body(j, h):
        h = [list(r) for r in h]
        before = [None] * NG
        base = pl.multiple_of(j * UNROLL, SUB)
        dls, dus = tiles_of(dec_s, base, w), tiles_of(du_s, base, w)
        for r in range(UNROLL):
            t = base + r
            bv = [bc_s[at_row(t, SUB, i * TB * SUB), :] for i in range(NI)]
            cv = [bc_s[at_row(t, SUB, (NI + i) * TB * SUB), :] for i in range(NI)]
            for g in range(NG):
                dl, du = row_of(dls[g], r), row_of(dus[g], r)
                p = None
                for i in range(NI):
                    h_ref[at_row(t, N, SUB * i), g * w : (g + 1) * w] = h[i][g]
                    h[i][g] = jnp.exp2(dl * a2[i][g]) * h[i][g] + bv[i] * du
                    q = cv[i] * h[i][g]
                    p = q if p is None else p + q
                if r % 2 == 0:
                    before[g] = p
                else:
                    rows = at_row(base, SUB // 2, (r // 2) * SUB + g * TB * SUB // 2)
                    p_s[rows, :] = merge_pair(before[g], p, low)
        return tuple(tuple(r) for r in h)

    h = lax.fori_loop(0, TB // UNROLL, body, tuple(tuple(r) for r in part(last_ref)))
    for i in range(NI):
        for g in range(NG):
            last_ref[SUB * i : SUB * (i + 1), g * w : (g + 1) * w] = h[i][g]
    y = row_sums(p_s, TB, NG) + skip_ref[...] * u_ref[...].astype(f32)
    y_ref[...] = y
    z = z_ref[...]
    gated_ref[...] = (y * z * sigmoid(z)).astype(bf16)


def scan_fwd(groups, proj, u, z, masks, dtw, dtb, a2, skip, start, *first):
    rows, C = u.shape
    N, R = a2.shape[0], dtw.shape[0]
    w = min(128, C)
    TB = pick_block(rows // groups, SCAN_BLOCK)
    nb = rows // groups // TB
    blk = lambda s, n=TB: pl.BlockSpec((n, s), lambda g, b: (g * nb + b, 0))
    own = pl.BlockSpec((N, C), lambda g, b: (g, 0))
    sd = jax.ShapeDtypeStruct
    outs = [
        sd((rows, C), bf16), sd((rows, C), f32), sd((rows, C), f32), sd((rows * N, C), f32),
        sd((groups * N, C), f32),
    ]
    return pl.pallas_call(
        scan_fwd_kernel,
        name="scan_fwd",
        grid=(groups, nb),
        in_specs=[
            pl.BlockSpec((R + 2 * N, TB), lambda g, b: (0, g * nb + b)), blk(C), blk(C), blk(masks.shape[1]),
            whole(dtw.shape), whole(dtb.shape), whole(a2.shape), whole(skip.shape),
            own,
        ]
        + [pl.BlockSpec(memory_space=pl.ANY)] * len(first),
        out_specs=[blk(C), blk(C), blk(C), blk(C, TB * N), own],
        out_shape=outs,
        scratch_shapes=[pltpu.VMEM((TB, C), f32)] * 2
        + [pltpu.VMEM((TB * (C // w) * SUB // 2, w), f32), pltpu.VMEM((TB * 2 * N, w), f32)]
        + [pltpu.VMEM((TB, 128), f32), pltpu.VMEM((TB * 2 * N, 128), bf16)],
        compiler_params=params("arbitrary", "arbitrary"),
        cost_estimate=cost(rows * C * N * 8, outs, rows * C * N),
    )(proj, u, z, masks, dtw, dtb, a2, skip, start, *first)


def scan_bwd_kernel(
    proj_ref, u_ref, z_ref, mask_ref, y_ref, delta_ref, gg_ref, h_ref,
    dtw_ref, a2_ref, skip_ref, places_ref, end_ref, late_ref,
    gz_ref, gu_ref, gproj_ref, first_ref, ga_ref, gdtw_ref, gvec_ref,
    dec_s, du_s, gy_s, r_s, s2_s, bc_s, mb_s, mc_s, next_s, wide_s, rows_s,
):
    TB, C = u_ref.shape
    N = a2_ref.shape[0]
    w = min(128, C)
    NG, NI = C // w, N // SUB
    b = pl.program_id(1)

    @pl.when((b == 0) & (pl.program_id(0) == 0))
    def _():
        ga_ref[...] = jnp.zeros_like(ga_ref)
        gdtw_ref[...] = jnp.zeros_like(gdtw_ref)
        gvec_ref[...] = jnp.zeros_like(gvec_ref)

    @pl.when(b == 0)
    def _():
        first_ref[...] = late_ref[...]
        next_s[...] = end_ref[...]

    rank = proj_ref[0 : dtw_ref.shape[0], :].astype(bf16)
    put_columns(bc_s, proj_ref[dtw_ref.shape[0] :, :].T, wide_s, rows_s)
    delta = delta_ref[...]
    u = u_ref[...].astype(f32)
    du_s[...] = delta * u
    dec_s[...] = jnp.where(mask_ref[:, 1:2] > 0.5, delta, FAR)
    z = z_ref[...]
    sg = sigmoid(z)
    gg = gg_ref[...]
    gy = gg * z * sg
    gy_s[...] = gy
    gz_ref[...] = (gg * y_ref[...] * sg * (1.0 + z * (1.0 - sg))).astype(bf16)
    gvec_ref[1:2, :] += jnp.sum(gy * u, axis=0, keepdims=True)
    part = lambda ref: [
        [ref[SUB * i : SUB * (i + 1), g * w : (g + 1) * w] for g in range(NG)] for i in range(NI)
    ]
    a2 = part(a2_ref)

    low = lax.broadcasted_iota(jnp.int32, (SUB, w), 0) < SUB // 2

    def body(j, carry):
        later = [None] * NG
        dlam, ga, h_now = ([list(r) for r in rows] for rows in carry)
        base = pl.multiple_of(TB - UNROLL - j * UNROLL, SUB)
        dls, dus, gys = tiles_of(dec_s, base, w), tiles_of(du_s, base, w), tiles_of(gy_s, base, w)
        for r in reversed(range(UNROLL)):
            t = base + r
            bv = [bc_s[at_row(t, SUB, i * TB * SUB), :] for i in range(NI)]
            cv = [bc_s[at_row(t, SUB, (NI + i) * TB * SUB), :] for i in range(NI)]
            mb, mc = [None] * NI, [None] * NI
            for g in range(NG):
                dl, du, gyr = row_of(dls[g], r), row_of(dus[g], r), row_of(gys[g], r)
                p, s2 = None, None
                for i in range(NI):
                    h_prev = h_ref[at_row(t, N, SUB * i), g * w : (g + 1) * w]
                    lam = cv[i] * gyr + dlam[i][g]
                    e = dl * a2[i][g]
                    dlam[i][g] = jnp.exp2(e) * lam
                    q = e * (dlam[i][g] * h_prev)
                    p = q if p is None else p + q
                    ga[i][g] = ga[i][g] + q
                    x = lam * bv[i]
                    s2 = x if s2 is None else s2 + x
                    x = lam * du
                    mb[i] = x if mb[i] is None else mb[i] + x
                    x = gyr * h_now[i][g]
                    mc[i] = x if mc[i] is None else mc[i] + x
                    h_now[i][g] = h_prev
                if r % 2:
                    later[g] = (p, s2)
                else:
                    rows = at_row(base, SUB // 2, (r // 2) * SUB + g * TB * SUB // 2)
                    r_s[rows, :] = merge_pair(p, later[g][0], low)
                    s2_s[rows, :] = merge_pair(s2, later[g][1], low)
            for i in range(NI):
                mb_s[at_row(t, N, SUB * i), :] = mb[i]
                mc_s[at_row(t, N, SUB * i), :] = mc[i]
        return tuple(tuple(tuple(r) for r in rows) for rows in (dlam, ga, h_now))

    carry = tuple(tuple(tuple(r) for r in part(ref)) for ref in (first_ref, ga_ref, next_s))
    for ref, rows in zip(
        (first_ref, ga_ref, next_s), lax.fori_loop(0, TB // UNROLL, body, carry)
    ):
        for i in range(NI):
            for g in range(NG):
                ref[SUB * i : SUB * (i + 1), g * w : (g + 1) * w] = rows[i][g]
    ones = jnp.ones((SUB, w), bf16)
    pick = (lax.broadcasted_iota(jnp.int32, (N, TB * N), 1) % N) == lax.broadcasted_iota(
        jnp.int32, (N, TB * N), 0
    )
    picked = []
    for scratch in (mb_s, mc_s):
        flat = lax.dot_general(
            ones, scratch[...].astype(bf16), (((1,), (1,)), ((), ())), preferred_element_type=f32
        )
        picked.append(jnp.where(pick, jnp.concatenate([flat] * NI, axis=0), 0.0))
    gproj_ref[dtw_ref.shape[0] :, :] = jnp.dot(
        jnp.concatenate(picked, axis=0).astype(bf16), places_ref[...], preferred_element_type=f32
    )
    s2 = row_sums(s2_s, TB, NG)
    ratio = jnp.where(
        delta < 0.0625,
        1.0 - delta * (0.5 - delta * (1.0 / 6.0 - delta * (1.0 / 24.0 - delta * (1.0 / 120.0)))),
        (1.0 - jnp.exp(-delta)) / jnp.maximum(delta, 0.0625),
    )
    gpre = ratio * (row_sums(r_s, TB, NG) * LN2 + du_s[...] * s2)
    low = gpre.astype(bf16)
    gu_ref[...] = gy_s[...] * skip_ref[...] + delta * s2
    gproj_ref[0 : dtw_ref.shape[0], :] = lax.dot_general(
        dtw_ref[...], low, (((1,), (1,)), ((), ())), preferred_element_type=f32
    )
    gdtw_ref[...] += jnp.dot(rank, low, preferred_element_type=f32)
    gvec_ref[0:1, :] += jnp.sum(gpre, axis=0, keepdims=True)


def scan_bwd(groups, proj, u, z, masks, y, delta, gg, h, dtw, a2, skip, places, end, late):
    rows, C = u.shape
    N, R = a2.shape[0], dtw.shape[0]
    w = min(128, C)
    TB = pick_block(rows // groups, SCAN_BLOCK)
    nb = rows // groups // TB
    where = lambda g, b: g * nb + nb - 1 - b
    blk = lambda s, n=TB: pl.BlockSpec((n, s), lambda g, b: (where(g, b), 0))
    own = pl.BlockSpec((N, C), lambda g, b: (g, 0))
    rowed = lambda n: pl.BlockSpec((n, TB), lambda g, b: (0, where(g, b)))
    sd = jax.ShapeDtypeStruct
    outs = [
        sd((rows, C), bf16), sd((rows, C), f32), sd((R + 2 * N, rows), f32), sd((groups * N, C), f32),
        sd((N, C), f32), sd((R, C), f32), sd((8, C), f32),
    ]
    fold = pltpu.VMEM((TB * (C // w) * SUB // 2, w), f32)
    return pl.pallas_call(
        scan_bwd_kernel,
        name="scan_bwd",
        grid=(groups, nb),
        in_specs=[
            rowed(R + 2 * N), blk(C), blk(C), blk(masks.shape[1]), blk(C), blk(C), blk(C), blk(C, TB * N),
            whole(dtw.shape), whole(a2.shape), whole(skip.shape), whole(places.shape), own, own,
        ],
        out_specs=[
            blk(C), blk(C), rowed(R + 2 * N), own,
            whole((N, C)), whole((R, C)), whole((8, C)),
        ],
        out_shape=outs,
        scratch_shapes=[pltpu.VMEM((TB, C), f32)] * 3
        + [fold] * 2
        + [pltpu.VMEM((TB * 2 * N, w), f32)]
        + [pltpu.VMEM((TB * N, w), f32)] * 2
        + [pltpu.VMEM((N, C), f32)]
        + [pltpu.VMEM((TB, 128), f32), pltpu.VMEM((TB * 2 * N, 128), bf16)],
        compiler_params=params("arbitrary", "arbitrary"),
        cost_estimate=cost(rows * C * N * 20, outs + [h], rows * C * N),
    )(proj, u, z, masks, y, delta, gg, h, dtw, a2, skip, places, end, late)


def pick_kernel(slot_ref, w_ref, x_ref, z_ref):
    x_ref[...] = w_ref[:, 0, :]
    z_ref[...] = w_ref[:, 1, :]


def pick(place, w_in, pieces, ctx):
    rows, _, total = w_in.shape
    piece = total // pieces // ctx
    if piece % 128:
        own = lax.dynamic_index_in_dim(
            w_in.reshape(rows, 2, pieces, ctx, piece), place, 3, False
        ).reshape(rows, 2, pieces * piece)
        return own[:, 0], own[:, 1]
    out = jax.ShapeDtypeStruct((rows, pieces * piece), w_in.dtype)
    spec = pl.BlockSpec((rows, piece), lambda f, s: (0, f))
    return pl.pallas_call(
        pick_kernel,
        name="pick",
        grid_spec=pltpu.PrefetchScalarGridSpec(
            num_scalar_prefetch=1,
            grid=(pieces,),
            in_specs=[pl.BlockSpec((rows, 2, piece), lambda f, s: (0, 0, f * ctx + s[0]))],
            out_specs=[spec, spec],
        ),
        out_shape=[out, out],
        compiler_params=params("arbitrary"),
        cost_estimate=cost(0, [out, out, out, out]),
    )(place.reshape(1).astype(jnp.int32), w_in)


def put_kernel(slot_ref, xa_ref, xb_ref, za_ref, zb_ref, o_ref):
    first = slot_ref[0] == 0
    piece = o_ref.shape[2] // 2
    for branch, (own, other) in enumerate(((xa_ref, xb_ref), (za_ref, zb_ref))):
        a, b = own[...], other[...]
        o_ref[:, branch, 0:piece] = jnp.where(first, a, b)
        o_ref[:, branch, piece:] = jnp.where(first, b, a)


def put(place, x_own, x_other, z_own, z_other, pieces):
    rows, C = x_own.shape
    piece = C // pieces
    TB = pick_block(rows, 256)
    spec = pl.BlockSpec((TB, piece), lambda b, f, s: (b, f))
    out = jax.ShapeDtypeStruct((rows, 2, 2 * C), x_own.dtype)
    return pl.pallas_call(
        put_kernel,
        name="put",
        grid_spec=pltpu.PrefetchScalarGridSpec(
            num_scalar_prefetch=1,
            grid=(rows // TB, pieces),
            in_specs=[spec] * 4,
            out_specs=pl.BlockSpec((TB, 2, 2 * piece), lambda b, f, s: (b, 0, f)),
        ),
        out_shape=out,
        compiler_params=params("arbitrary", "arbitrary"),
        cost_estimate=cost(0, [out, out]),
    )(place.reshape(1).astype(jnp.int32), x_own, x_other, z_own, z_other)


def conv_in_kernel(
    place_ref, own_ref, other_ref, gain_ref, mask_ref, cw_ref, cb_ref, xp_ref, halo_ref, *refs
):
    pieces, outs = refs[:-8], refs[-8:]
    norm_ref, scale_ref, bx_ref, xc_ref, u_ref, proj_ref, tail_ref, ext_s = outs
    TB, C = u_ref.shape
    taps = cw_ref.shape[0]

    @pl.when(pl.program_id(1) == 0)
    def _():
        ext_s[0:SUB, :] = halo_ref[...]

    x = jnp.where(place_ref[1] == 1, own_ref[...], other_ref[...]).astype(f32)
    scale = lax.rsqrt(jnp.mean(x * x, axis=1, keepdims=True) + eps)
    scale_ref[...] = scale
    norm_ref[...] = (x * scale * gain_ref[...]).astype(bf16)
    bx = 0.0
    for turn, w_ref in enumerate(pieces):
        deep = w_ref.shape[0]
        first = pl.multiple_of((place_ref[0] ^ turn) * deep, deep)
        bx += jnp.dot(norm_ref[:, pl.ds(first, deep)], w_ref[...], preferred_element_type=f32)
    bx_ref[...] = bx
    ext_s[SUB:, :] = bx
    total = cb_ref[...] + cw_ref[taps - 1 : taps, :] * bx
    for tap in range(taps - 1):
        back = taps - 1 - tap
        total += cw_ref[tap : tap + 1, :] * (
            ext_s[SUB - back : SUB - back + TB, :] * mask_ref[:, back : back + 1]
        )
    xc_ref[...] = total
    u = (total * sigmoid(total)).astype(bf16)
    u_ref[...] = u
    proj_ref[...] = lax.dot_general(
        xp_ref[...], u, (((1,), (1,)), ((), ())), preferred_element_type=f32
    )
    ext_s[0:SUB, :] = bx[TB - SUB :, :]
    tail_ref[...] = bx[TB - SUB :, :]


def conv_in(groups, me, use_own, own, other, gain, pieces, masks, cw, cb, xp, halo):
    rows, D = own.shape
    C = pieces[0].shape[1]
    TB = pick_block(rows // groups, CONV_BLOCK)
    nb = rows // groups // TB
    blk = lambda s: pl.BlockSpec((TB, s), lambda g, b, _: (g * nb + b, 0))
    mine = pl.BlockSpec((SUB, C), lambda g, b, _: (g, 0))
    sd = jax.ShapeDtypeStruct
    R = xp.shape[0]
    outs = [
        sd((rows, D), bf16), sd((rows, 1), f32), sd((rows, C), f32), sd((rows, C), f32),
        sd((rows, C), bf16), sd((R, rows), f32), sd((groups * SUB, C), f32),
    ]
    return pl.pallas_call(
        conv_in_kernel,
        name="conv_in",
        grid_spec=pltpu.PrefetchScalarGridSpec(
            num_scalar_prefetch=1,
            grid=(groups, nb),
            in_specs=[
                pl.BlockSpec((TB, D), lambda g, b, p: ((g * nb + b) * p[1], 0)),
                pl.BlockSpec((TB, D), lambda g, b, p: ((g * nb + b) * (1 - p[1]), 0)),
                whole(gain.shape), blk(masks.shape[1]), whole(cw.shape), whole(cb.shape),
                whole(xp.shape), mine,
            ]
            + [whole(p.shape) for p in pieces],
            out_specs=[
                blk(D), blk(1), blk(C), blk(C), blk(C),
                pl.BlockSpec((R, TB), lambda g, b, _: (0, g * nb + b)), mine,
            ],
            scratch_shapes=[pltpu.VMEM((TB + SUB, C), f32)],
        ),
        out_shape=outs,
        compiler_params=params("arbitrary", "arbitrary"),
        cost_estimate=cost(2 * rows * D * C, outs + [own], rows * C),
    )(jnp.stack([me, use_own]).astype(jnp.int32), own, other, gain, masks, cw, cb, xp, halo, *pieces)


def conv_out_kernel(
    gu_ref, gp_ref, xp_ref, xc_ref, bx_ref, z_ref, gz_ref, u_ref, mask_ref, cw_ref, late_ref,
    gm_ref, along_ref, early_ref, gconv_ref, gxp_ref,
    *ext_s,
):
    TB, C = u_ref.shape
    taps = cw_ref.shape[0]

    @pl.when((pl.program_id(1) == 0) & (pl.program_id(0) == 0))
    def _():
        gconv_ref[...] = jnp.zeros_like(gconv_ref)
        gxp_ref[...] = jnp.zeros_like(gxp_ref)

    @pl.when(pl.program_id(1) == 0)
    def _():
        for back in range(1, taps):
            ext_s[back - 1][TB:, :] = late_ref[(back - 1) * SUB : back * SUB, :]

    gp = gp_ref[...]
    xc = xc_ref[...]
    sg = sigmoid(xc)
    inner = gu_ref[...] + lax.dot_general(
        gp, xp_ref[...], (((0,), (0,)), ((), ())), preferred_element_type=f32
    )
    gxc = inner * (sg * (1.0 + xc * (1.0 - sg)))
    bx = bx_ref[...]
    gx = cw_ref[taps - 1 : taps, :] * gxc
    gconv_ref[taps - 1 : taps, :] += jnp.sum(gxc * bx, axis=0, keepdims=True)
    gconv_ref[taps : taps + 1, :] += jnp.sum(gxc, axis=0, keepdims=True)
    for back in range(1, taps):
        tap = taps - 1 - back
        ext = ext_s[back - 1]
        reached = gxc * mask_ref[:, back : back + 1]
        ext[0:TB, :] = reached
        moved = ext[back : back + TB, :]
        gx += cw_ref[tap : tap + 1, :] * moved
        gconv_ref[tap : tap + 1, :] += jnp.sum(moved * bx, axis=0, keepdims=True)
        ext[TB:, :] = reached[0:SUB, :]
        early_ref[(back - 1) * SUB : back * SUB, :] = reached[0:SUB, :]
    gz = gz_ref[...]
    gx = gx.astype(bf16)
    gm_ref[:, 0:C] = gx
    gm_ref[:, C:] = gz
    terms = (gx.astype(f32) * bx + gz.astype(f32) * z_ref[...]).astype(bf16)
    along_ref[...] = lax.dot_general(
        jnp.ones((SUB, C), bf16), terms, (((1,), (1,)), ((), ())), preferred_element_type=f32
    )
    gxp_ref[...] += jnp.dot(gp, u_ref[...], preferred_element_type=f32)


def conv_out(groups, gu, gp, xp, xc, bx, z, gz, u, masks, cw, late):
    rows, C = u.shape
    taps = cw.shape[0]
    R = xp.shape[0]
    TB = pick_block(rows // groups, CONV_BLOCK)
    nb = rows // groups // TB
    blk = lambda s: pl.BlockSpec((TB, s), lambda g, b: (g * nb + nb - 1 - b, 0))
    own = pl.BlockSpec(((taps - 1) * SUB, C), lambda g, b: (g, 0))
    sd = jax.ShapeDtypeStruct
    outs = [
        sd((rows, 2 * C), bf16), sd((SUB, rows), f32), sd((groups * (taps - 1) * SUB, C), f32),
        sd((8, C), f32), sd((R, C), f32),
    ]
    return pl.pallas_call(
        conv_out_kernel,
        name="conv_out",
        grid=(groups, nb),
        in_specs=[
            blk(C), pl.BlockSpec((R, TB), lambda g, b: (0, g * nb + nb - 1 - b)),
            whole(xp.shape), blk(C), blk(C), blk(C), blk(C), blk(C),
            blk(masks.shape[1]), whole(cw.shape), own,
        ],
        out_specs=[
            blk(2 * C),
            pl.BlockSpec((SUB, TB), lambda g, b: (0, g * nb + nb - 1 - b)),
            own,
            whole((8, C)),
            whole((R, C)),
        ],
        out_shape=outs,
        scratch_shapes=[pltpu.VMEM((TB + SUB, C), f32)] * (taps - 1),
        compiler_params=params("arbitrary", "arbitrary"),
        cost_estimate=cost(4 * rows * R * C, outs + [gu, xc, bx, z], rows * C),
    )(gu, gp, xp, xc, bx, z, gz, u, masks, cw, late)


def spread_kernel(slot_ref, x_ref, w_ref, *refs, adding):
    o_ref = refs[-1]
    for z in range(o_ref.shape[0]):
        total = jnp.dot(x_ref[0], w_ref[z], preferred_element_type=f32)
        if adding:
            total = total + refs[0][z].astype(f32)
        o_ref[z] = total.astype(bf16)


def spread(slot, x, w, added=(), first=()):
    _, rows, K = x.shape
    shares, _, share = w.shape
    per = 2 if shares % 2 == 0 and rows * share <= 512 * 512 else 1
    out = jax.ShapeDtypeStruct((shares, rows, share), bf16)
    block = pl.BlockSpec((per, rows, share), lambda z, s: (z, 0, 0))
    return pl.pallas_call(
        functools.partial(spread_kernel, adding=len(added)),
        name="spread",
        grid_spec=pltpu.PrefetchScalarGridSpec(
            num_scalar_prefetch=1,
            grid=(shares // per,),
            in_specs=[
                pl.BlockSpec((1, rows, K), lambda z, s: (s[0], 0, 0)),
                pl.BlockSpec((per, K, share), lambda z, s: (z, 0, 0)),
            ]
            + [block] * len(added)
            + [pl.BlockSpec(memory_space=pl.ANY)] * len(first),
            out_specs=block,
        ),
        out_shape=out,
        compiler_params=params("arbitrary"),
        cost_estimate=cost(2 * rows * K * shares * share, [out, x, w]),
    )(slot, x, w, *added, *first)


def collect_kernel(slot_ref, own_ref, other_ref, w_ref, o_ref):
    shares, _, share = own_ref.shape

    def product(ref):
        total = jnp.dot(ref[0], w_ref[0:share, :], preferred_element_type=f32)
        for z in range(1, shares):
            total += jnp.dot(
                ref[z], w_ref[z * share : (z + 1) * share, :], preferred_element_type=f32
            )
        o_ref[0] = total

    @pl.when(pl.program_id(0) == 0)
    def _():
        product(own_ref)

    @pl.when(pl.program_id(0) == 1)
    def _():
        product(other_ref)


def collect(slot, own, other, w):
    shares, rows, share = own.shape
    C = w.shape[1]
    out = jax.ShapeDtypeStruct((2, rows, C), f32)
    return pl.pallas_call(
        collect_kernel,
        name="collect",
        grid_spec=pltpu.PrefetchScalarGridSpec(
            num_scalar_prefetch=1,
            grid=(2,),
            in_specs=[
                pl.BlockSpec(own.shape, lambda s, p: (0, 0, 0)),
                pl.BlockSpec(own.shape, lambda s, p: (0, 0, 0)),
                pl.BlockSpec(w.shape, lambda s, p: (0, 0)),
            ],
            out_specs=pl.BlockSpec((1, rows, C), lambda s, p: (s + p[0] - 2 * s * p[0], 0, 0)),
        ),
        out_shape=out,
        compiler_params=params("arbitrary"),
        cost_estimate=cost(4 * rows * C * share * shares, [out, own, other, w]),
    )(slot, own, other, w)


def after(value, *others):
    return lax.optimization_barrier((value,) + others)[0]


def swap_cores(value):
    return lax.ppermute(value, "context", [(0, 1), (1, 0)])


def paired():
    return lax.axis_size("context") == 2


def in_order(own, other):
    first = lax.axis_index("context") == 0
    return jnp.where(first, own, other), jnp.where(first, other, own)


def gather_context(value):
    if not paired():
        return lax.all_gather(value, "context")
    return jnp.stack(in_order(value, swap_cores(value)))


def sum_over(value, *axes):
    for axis in axes:
        size, step = lax.axis_size(axis), 1
        if size & (size - 1):
            value = lax.psum(value, axis)
            continue
        while step < size:
            value = value + lax.ppermute(value, axis, [(i, i ^ step) for i in range(size)])
            step *= 2
    return value


ROW = [(0, 1), (1, 0), (2, 3), (3, 2)]
COLUMN = [(0, 2), (2, 0), (1, 3), (3, 1)]


def gather_fsdp(value, *hold):
    size = lax.axis_size("fsdp")
    if size != 4 or value.shape[0] % 2:
        pieces = lax.all_gather(value, "fsdp")
        return jnp.zeros((), jnp.int32), [pieces[i] for i in range(size)]
    half = value.shape[0] // 2
    row = lax.ppermute(value, "fsdp", ROW)
    column = lax.ppermute(value, "fsdp", COLUMN)
    if hold:
        row, column = lax.optimization_barrier((row, column) + hold)[:2]
    far = jnp.concatenate(
        [lax.ppermute(row[:half], "fsdp", COLUMN), lax.ppermute(column[half:], "fsdp", ROW)]
    )
    return lax.axis_index("fsdp"), [value, row, column, far]


def stacked(me, pieces):
    if len(pieces) != 4:
        return jnp.stack(pieces)
    a, b, c, d = pieces
    odd, high = me % 2 == 1, me // 2 == 1
    pick2 = lambda flag, x, y: jnp.where(flag, y, x)
    return jnp.stack(
        [
            pick2(high, pick2(odd, a, b), pick2(odd, c, d)),
            pick2(high, pick2(odd, b, a), pick2(odd, d, c)),
            pick2(high, pick2(odd, c, d), pick2(odd, a, b)),
            pick2(high, pick2(odd, d, c), pick2(odd, b, a)),
        ]
    )


def scatter_fsdp(parts, *hold):
    size = lax.axis_size("fsdp")
    if size & (size - 1):
        return lax.psum_scatter(parts, "fsdp", scatter_dimension=0).astype(f32)
    me = lax.axis_index("fsdp")
    take = lambda i: lax.dynamic_index_in_dim(parts, i, 0, False)
    got = [
        lax.ppermute(take(me ^ turn), "fsdp", [(i, i ^ turn) for i in range(size)])
        for turn in range(1, size)
    ]
    if hold:
        got = lax.optimization_barrier((*got, *hold))[: size - 1]
    return sum([g.astype(f32) for g in got], take(me).astype(f32))


def flip(value, step):
    size = lax.axis_size("tensor")
    return lax.ppermute(value, "tensor", [(i, i ^ step) for i in range(size)])


def token_share(part, groups, i):
    each = part.shape[1] // groups
    size = each // lax.axis_size("context")
    return jnp.concatenate(
        [lax.dynamic_slice_in_dim(part, g * each + i * size, size, 1) for g in range(groups)], axis=1
    )


def token_join(values, groups):
    size = values[0].shape[-1] // groups
    return jnp.concatenate(
        [v[..., g * size : (g + 1) * size] for g in range(groups) for v in values], axis=-1
    )


def start_sum(part, groups):
    tp = lax.axis_size("tensor")
    if not paired() or tp & (tp - 1):
        return lax.psum(part, ("tensor", "context")), []
    place = lax.axis_index("context")
    other = swap_cores(token_share(part, groups, 1 - place).astype(bf16))
    total = token_share(part, groups, place) + other.astype(f32)
    sent = total.astype(bf16)
    return total, [flip(sent, step) for step in range(1, tp)]


def end_sum(begun, groups, out_type, *meanwhile):
    total, got = begun
    for piece in got:
        total = total + after(piece, *meanwhile).astype(f32)
    total = total.astype(out_type)
    return token_join(in_order(total, swap_cores(total)), groups) if got else total


def sum_parts(parts, groups, fillers):
    tp = lax.axis_size("tensor")
    if not paired() or tp & (tp - 1):
        fillers(1, parts[0])
        return [lax.psum(part, ("tensor", "context")) for part in parts]
    place = lax.axis_index("context")
    share = lambda i: jnp.concatenate([token_share(p, groups, i) for p in parts], axis=0)
    total = share(place) + swap_cores(share(1 - place).astype(bf16)).astype(f32)
    step = 1
    while step < tp:
        got = flip(total.astype(bf16), step)
        total = total + after(got, *fillers(step, total)).astype(f32)
        step *= 2
    R = parts[0].shape[0]
    total = token_join(in_order(total, swap_cores(total)), groups)
    return [total[i * R : (i + 1) * R] for i in range(len(parts))]


def on_device(
    x_in,
    teacher,
    segments,
    valid,
    norm_gain,
    w_in,
    conv_w,
    conv_b,
    x_proj,
    dt_w,
    dt_bias,
    a_log,
    d_skip,
    w_out,
):
    groups, blocklen, width = x_in.shape
    nf, ctx, tp = (lax.axis_size(name) for name in ("fsdp", "context", "tensor"))
    place = lax.axis_index("context")
    rows_here, _, chans_tensor = w_in.shape
    piece = conv_w.shape[1] // ctx
    chans = nf * piece
    taps, rank_dim, nstate = conv_w.shape[0], dt_w.shape[0], a_log.shape[0]
    proj_dim = x_proj.shape[0]
    share = width // tp
    cols_here = w_out.shape[1]
    full = blocklen * ctx
    tokens = groups * full
    part = full // CHUNKS
    sub = part // ctx
    rows = groups * part
    order = range(CHUNKS)
    first_col = lax.axis_index("tensor") * share

    def by_chunks(value):
        if paired():
            return in_order(value, swap_cores(value))
        value = jnp.moveaxis(lax.all_gather(value, "context"), 0, 1)
        value = value.reshape((groups, CHUNKS, part) + value.shape[3:])
        return [value[:, c] for c in order]

    def mine(value):
        value = value.reshape((groups, ctx, sub) + value.shape[2:])
        return lax.dynamic_index_in_dim(value, place, 1, False)

    def to_work(value):
        if not paired():
            return [mine(v) for v in by_chunks(value)]
        value = value.reshape((groups, CHUNKS, sub) + value.shape[2:])
        got = swap_cores(lax.dynamic_index_in_dim(value, 1 - place, 1, False))
        return in_order(lax.dynamic_index_in_dim(value, place, 1, False), got)

    def from_work(values):
        if not paired():
            stacked = jnp.moveaxis(lax.all_gather(jnp.stack(values), "context"), 2, 0)
            stacked = jnp.swapaxes(stacked, 1, 2).reshape((groups, full) + values[0].shape[2:])
            return lax.dynamic_slice_in_dim(stacked, place * blocklen, blocklen, 1)
        keep, sent = in_order(values[0], values[1])
        return jnp.concatenate(in_order(keep, swap_cores(sent)), axis=1)

    if paired():
        x_own, x_other = (v.reshape(rows, width) for v in (x_in, swap_cores(x_in)))
        columns = in_order(*(lax.dynamic_slice_in_dim(v, first_col, share, 1) for v in (x_own, x_other)))
    else:
        x_chunks = [v.reshape(rows, width) for v in by_chunks(x_in)]
        columns = [lax.dynamic_slice_in_dim(v, first_col, share, 1) for v in x_chunks]
    x_shares = [mine(v.reshape(groups, part, share)) for v in columns]
    if not paired():
        *x_shares, x_chunks[0] = lax.optimization_barrier((*x_shares, x_chunks[0]))
    marks_in = jnp.stack([segments, valid], axis=-1)
    marks_in = jnp.concatenate(by_chunks(marks_in), axis=1)
    seg = marks_in[..., 0]
    valid_all = marks_in[..., 1].astype(f32)
    count = sum_over(jnp.sum(valid_all).reshape(1, 1), "fsdp")
    masks = []
    for back in range(taps):
        same = seg[:, back:] == seg[:, : full - back]
        masks.append(jnp.pad(same, ((0, 0), (back, 0)), constant_values=False))
    masks = jnp.stack(masks, axis=-1).astype(f32)
    masks = [masks[:, c * part : (c + 1) * part].reshape(rows, taps) for c in order]

    wx_own, wz_own = pick(place, w_in, nf, ctx)
    small = jnp.concatenate(
        [x_proj, dt_w, a_log, conv_w, conv_b[None], dt_bias[None], d_skip[None]], axis=0
    )
    nsmall = small.shape[0]
    small = lax.dynamic_slice_in_dim(small, place * piece, piece, 1)
    gain_rows = norm_gain.reshape(-1, piece)
    spare = -(nsmall + gain_rows.shape[0]) % 32
    small = jnp.concatenate([small, gain_rows, jnp.zeros((spare, piece), bf16)], axis=0)
    small = lax.all_gather(after(small, wx_own), "fsdp")
    gain_all = small[:, nsmall : nsmall + gain_rows.shape[0]].reshape(width).astype(f32)
    small = jnp.swapaxes(small[:, :nsmall], 0, 1).reshape(nsmall, chans)
    ends = [0]
    for size in (proj_dim, rank_dim, nstate, taps, 1, 1, 1):
        ends.append(ends[-1] + size)
    xp, dtw, alog, cw, cb, dtb, skip = (small[a:b] for a, b in zip(ends[:-1], ends[1:]))
    cw, cb, skip, dtb = (v.astype(f32) for v in (cw, cb, skip, dtb))
    rates = -jnp.exp(alog.astype(f32))
    a2 = rates * LOG2E
    me, wx_pieces = gather_fsdp(wx_own)
    wz = lax.all_gather(after(wz_own, *wx_pieces), "fsdp", axis=0, tiled=True)
    wout_own = lax.dynamic_index_in_dim(
        w_out.reshape(nf, ctx, piece, cols_here), place, 1, False
    ).reshape(chans, cols_here)
    wout = lax.all_gather(after(wout_own, *wx_pieces), "fsdp")
    wout_t = jnp.swapaxes(wout, 1, 2).reshape(width, chans)
    if nf != tp:
        wout = jnp.swapaxes(wout_t.T.reshape(chans, tp, share), 0, 1)
    win_t = jnp.concatenate([stacked(me, wx_pieces).reshape(width, chans), wz], axis=1)
    win_t = jnp.swapaxes(win_t.reshape(tp, share, 2 * chans), 1, 2)

    bxs, xcs, us, zs, parts, normeds, scales = [], [], [], [], [], [], []
    tail = jnp.zeros((groups * SUB, chans), f32)
    for c in order:
        if paired():
            source = (place == c).astype(jnp.int32), x_own, x_other
        else:
            source = jnp.ones((), jnp.int32), x_chunks[c], x_chunks[c]
        normed, scale, bx, xc, u, proj_part, tail = conv_in(
            groups, me, *source, gain_all[None], wx_pieces, masks[c], cw, cb, xp, tail
        )
        normeds.append(normed)
        scales.append(scale.reshape(groups, part, 1))
        bxs.append(bx)
        xcs.append(xc)
        us.append(u)
        parts.append(proj_part)

    def fillers(step, total):
        c = step // 2
        if c < CHUNKS and len(zs) == c:
            zs.append(jnp.dot(after(normeds[c], total), wz, preferred_element_type=f32))
            return (zs[c],)
        return ()

    projs = sum_parts(parts, groups, fillers)
    for c in range(len(zs), CHUNKS):
        zs.append(jnp.dot(normeds[c], wz, preferred_element_type=f32))

    slot_own = place.reshape(1).astype(jnp.int32)
    slot_other = 1 - slot_own

    def to_shares(value, w, between=None):
        value = jnp.moveaxis(value.reshape(groups, ctx, sub, -1), 1, 0).reshape(ctx, groups * sub, -1)
        if paired():
            send = spread(slot_other, value, w)
            first = [between(send)] if between else []
            total = spread(slot_own, value, w, [swap_cores(send)], first)
        else:
            first = [between(value)] if between else []
            total = spread(jnp.zeros((1,), jnp.int32), value.reshape(1, ctx * groups * sub, -1), w)
            total = jnp.moveaxis(total.reshape(tp, ctx, groups * sub, share), 1, 0)
            total = lax.psum_scatter(total, "context", scatter_dimension=0)
        summed = lax.psum_scatter(total, "tensor", scatter_dimension=0)
        return first, total, summed.reshape(groups, sub, share)

    gateds, ys, deltas, states = [], [], [], []
    outs, grad_outs, losses = [], [], []
    targets = to_work(lax.dynamic_slice_in_dim(teacher, first_col, share, 2))
    state = jnp.zeros((groups * nstate, chans), f32)
    for c in order:
        u = us[c] if c == 0 else after(us[c], sent)
        gated, y, delta, h, state = scan_fwd(
            groups, projs[c], u, zs[c], masks[c], dtw, dtb, a2, skip, state
        )
        deltas.append(delta)
        gateds.append(gated)
        ys.append(y)
        states.append(h)
        _, sent, branch = to_shares(gated, wout)
        outs.append(x_shares[c].astype(f32) + branch.astype(f32))
        errors = outs[c] - targets[c].astype(f32)
        live = mine(valid_all[:, c * part : (c + 1) * part])[..., None]
        losses.append(jnp.sum(live * errors * errors))
        grad_outs.append((tokens * nf / count[0, 0]) * live * errors)
    loss_value = sum_over(sum(losses).reshape(1, 1), "context", "tensor", "fsdp")[0, 0]
    loss_value = loss_value / width / count[0, 0]
    out_share = from_work(outs)

    late = jnp.zeros((groups * nstate, chans), f32)
    late_conv = jnp.zeros((groups * (taps - 1) * SUB, chans), f32)
    grad_inputs, alongs = [None] * CHUNKS, [None] * CHUNKS
    turn = (((0,), (0,)), ((), ()))
    size = pick_block(part, SCAN_BLOCK)
    places = (
        lax.broadcasted_iota(jnp.int32, (size * nstate, size), 0) // nstate
        == lax.broadcasted_iota(jnp.int32, (size * nstate, size), 1)
    ).astype(bf16)
    gwout = gwz = gwx = 0.0
    grads = 0.0
    lows = [None] * CHUNKS
    for c in reversed(order):
        low = grad_outs[c].astype(bf16).reshape(groups * sub, share)
        if c < CHUNKS - 1:
            low = after(low, lows[c + 1])
        lows[c] = lax.all_gather(low, "tensor")

    gated_parts = []
    for gated in gateds if paired() else []:
        gated = jnp.moveaxis(gated.reshape(groups, ctx, sub, chans), 1, 0)
        gated = gated.reshape(ctx, groups * sub, chans)
        gated_parts.append(
            [lax.dynamic_index_in_dim(gated, i, 0, False) for i in (place, 1 - place)]
        )

    def grad_gated(c, low):
        if paired():
            other = swap_cores(low)
            gg = collect(slot_own, low, other, wout_t)
            pairs = list(zip(gated_parts[c], (low, other)))
        else:
            low = jnp.moveaxis(lax.all_gather(low, "context"), 0, 1).reshape(tp, rows, share)
            gg = jnp.einsum(
                "ztj,zcj->tc", low, wout, preferred_element_type=f32
            ).reshape(ctx, groups * sub, chans)
            gated = jnp.moveaxis(gateds[c].reshape(groups, ctx, sub, chans), 1, 0)
            pairs = [(gated.reshape(rows, chans), low)]
        gg = jnp.moveaxis(gg.reshape(ctx, groups, sub, chans), 0, 1).reshape(rows, chans)
        return gg, pairs

    last, places, *gated_parts = lax.optimization_barrier(
        (lows[-1], places, *gated_parts, out_share, loss_value, wout_t, win_t)
    )[: 2 + len(gated_parts)]
    gg, pairs = grad_gated(CHUNKS - 1, last)
    for c in reversed(order):
        gz, gu, gproj, late, ga, gdtw, gvec = scan_bwd(
            groups, projs[c], us[c], zs[c], masks[c], ys[c], deltas[c], gg, states[c],
            dtw, a2, skip, places, state, late,
        )
        state = states[c].reshape(groups, part * nstate, chans)[:, :nstate].reshape(-1, chans)
        gproj = start_sum(gproj, groups)
        summed = gproj[0]
        if c < CHUNKS - 1:
            summed, grad_inputs[c + 1] = lax.optimization_barrier((summed, grad_inputs[c + 1]))
        if c:
            gg_next, pairs_next = grad_gated(c - 1, after(lows[c - 1], summed))
            if c == 1:
                pairs = pairs + pairs_next
        for left, right in pairs if c else []:
            left = after(left, summed)
            gwout += jnp.einsum("tc,ztj->zcj", left, right, preferred_element_type=f32)
        gwz += lax.dot_general(normeds[c], after(gz, summed), turn, preferred_element_type=f32)
        if c < CHUNKS - 1:
            gm = after(gm, summed)
            gwx += lax.dot_general(
                normeds[c + 1], gm[:, :chans], turn, preferred_element_type=f32
            )
        if c:
            gg, pairs = gg_next, pairs_next
            fillers = [gwz, gg, gwout]
        else:
            fillers = [gwz, gwx] if paired() else []
        gproj = end_sum(gproj, groups, bf16, *fillers)
        gm, along, late_conv, gconv, gxp = conv_out(
            groups, gu, gproj, xp, xcs[c], bxs[c], zs[c], gz, us[c], masks[c], cw, late_conv
        )
        def grad_wx(token):
            return gwx + lax.dot_general(
                normeds[0], after(gm, token)[:, :chans], turn, preferred_element_type=f32
            )

        first, sent, grad_normed = to_shares(gm, win_t, None if c else grad_wx)
        if not c:
            gwx = first[0]
            gconv, gxp, along = lax.optimization_barrier((gconv, gxp, along, sent))[:3]
        if c == 1:
            gwout = jnp.swapaxes(gwout, 0, 1).reshape(chans, nf, cols_here)
            gwout = jnp.swapaxes(gwout, 0, 1).astype(bf16)
            gwout = lax.psum_scatter(gwout, "fsdp", scatter_dimension=0)
        if c:
            gg = after(gg, sent, gwout) if paired() else gg
        grads += jnp.concatenate(
            [gxp, gdtw, ga * LN2, gconv, gvec], axis=0
        )
        alongs[c] = along[0]
        grad_inputs[c] = grad_normed
    grads = after(grads, sent)
    gwz = lax.psum_scatter(
        gwz.astype(bf16).reshape(nf, rows_here, chans), "fsdp", scatter_dimension=0
    )
    gwz = after(gwz, sent).astype(f32)
    gwz_other = swap_cores(gwz) if paired() else None
    sums = sum_over(jnp.concatenate(alongs)[None], "context", "tensor")[0]
    wout_g = gather_context((after(gwout, sent) if paired() else gwout).astype(f32))
    wout_g = jnp.swapaxes(wout_g.reshape(ctx, nf, piece, cols_here), 0, 1).reshape(
        chans_tensor, cols_here
    )
    gwx = scatter_fsdp(
        gwx.astype(bf16).reshape(nf, rows_here, chans), sent, sums, *([wout_g] if paired() else [])
    )
    gain_part = jnp.sum(gwx * wx_own.astype(f32) + gwz * wz_own.astype(f32), axis=1)
    gain_share = lax.dynamic_slice_in_dim(gain_all, first_col, share, 0)
    fixed, factors = [], []
    for c in order:
        along = sums[c * rows : (c + 1) * rows].reshape(groups, part)
        scale = mine(scales[c])
        fixed.append(
            grad_outs[c]
            - x_shares[c].astype(f32) * (scale * scale * (mine(along)[..., None] / width))
        )
        factors.append(scale * gain_share)
    nrows = grads.shape[0]
    grads = jnp.swapaxes(grads.reshape(nrows, nf, piece), 0, 1)
    grads = scatter_fsdp(grads)
    grads = jnp.swapaxes(gather_context(grads), 0, 1).reshape(nrows, ctx * piece)
    xp_g, dtw_g, alog_g = (grads[a:b] for a, b in zip(ends[:3], ends[1:4]))
    cw_g = grads[ends[3] : ends[4]]
    cb_g = grads[ends[4]]
    dtb_g, skip_g = grads[ends[3] + SUB], grads[ends[3] + SUB + 1]
    if paired() and piece % 128 == 0:
        win_g = put(place, gwx, swap_cores(gwx), gwz, gwz_other, nf)
    else:
        win_g = jnp.stack(
            [
                jnp.moveaxis(gather_context(g).reshape(ctx, rows_here, nf, piece), 0, 2).reshape(
                    rows_here, chans_tensor
                )
                for g in (gwx, gwz)
            ],
            axis=1,
        )
    grad_gain = sum_over(gain_part[None], "context", "tensor")[0] / norm_gain.astype(f32)
    done = (grads, win_g, *fixed)
    got = [grad_inputs[c] if c else after(grad_inputs[c], *done) for c in order]
    grad_share = from_work([f + k * g.astype(f32) for f, k, g in zip(fixed, factors, got)])
    return (
        out_share,
        loss_value,
        grad_share,
        grad_gain,
        win_g,
        cw_g,
        cb_g,
        xp_g,
        dtw_g,
        dtb_g,
        alog_g,
        skip_g,
        wout_g,
    )


def solution(mesh):
    return jax.shard_map(
        on_device,
        mesh=mesh,
        in_specs=(
            P("fsdp", "context", None),
            P("fsdp", "context", None),
            P("fsdp", "context"),
            P("fsdp", "context"),
            P("fsdp"),
            P("fsdp", None, "tensor"),
            P(None, ("tensor", "fsdp")),
            P(("tensor", "fsdp")),
            P(None, ("tensor", "fsdp")),
            P(None, ("tensor", "fsdp")),
            P(("tensor", "fsdp")),
            P(None, ("tensor", "fsdp")),
            P(("tensor", "fsdp")),
            P("tensor", "fsdp"),
        ),
        out_specs=(
            P("fsdp", "context", "tensor"),
            P(),
            P("fsdp", "context", "tensor"),
            P("fsdp"),
            P("fsdp", None, "tensor"),
            P(None, ("tensor", "fsdp")),
            P(("tensor", "fsdp")),
            P(None, ("tensor", "fsdp")),
            P(None, ("tensor", "fsdp")),
            P(("tensor", "fsdp")),
            P(None, ("tensor", "fsdp")),
            P(("tensor", "fsdp")),
            P("tensor", "fsdp"),
        ),
        check_vma=False,
    )
```
